32 devices in a mesh: bx: 8 (over y, x, core), by: 4 (over z).
Axes of the slice: x: 2, y: 2, z: 4, core: 2. Of those that a mesh axis runs over, the one named last changes fastest.
Arguments:
- basis: float32 [4, 16, 8, 16, 512], P(None, 'bx', 'by'), may hold values from -6 to 6
- coef: float32 [16, 8, 16], P('bx', 'by'), may hold values from 0.5 to 4
- modes: float32 [3, 8, 8], replicated, may hold values from -1 to 1, as said below
- eigen: float32 [3, 8], replicated, may hold values from 0.2 to 20
- mask: int32 [16, 8, 16], P('bx', 'by'), may hold values 0 or 1
- vertex_ids: int32 [8, 4, 2, 2, 4], P('bx', 'by'), may hold values from 0 to 127, as said below
- coarse_inverse: float32 [128, 128], P('bx'), as said below
Outputs:
- precond: float32 [16, 8, 16, 512], P('bx', 'by')
- next_vector: float32 [16, 8, 16, 512], P('bx', 'by')
- hessen: float32 [5], replicated
The draws below stay inside these ranges and needn't reach their ends.
Inputs may be any that keep to these rules, and one draw needn't show every extreme that they name: `modes`: each of the three matrices is orthogonal. `vertex_ids`: entry [p, q, a, b, l] is the number of the coarse vertex at corner (p + a, q + b) of the brick grid, taken with wraparound, on level l along the third dimension; bricks beside one another share their corner vertices, and every number is used. `coarse_inverse`: symmetric and positive definite.
All inputs are finite; a program needn't handle non-finite values. No bound on the sum of `mask` on one device may be relied on, other than what follows from the above.
Results may differ from the reference program's by a relative error of at most 0.0022.
Values sent between devices are 32-bit elements; how exact they have to be, the bound alone decides.
No kernel may reach another device: no remote copies, remote signals or barrier semaphores. Data moves between devices by JAX's collectives and lax.ppermute only.
A program may use at most 128 MiB of HBM per device.

```python
import math
import jax
import jax.numpy as jnp
from jax import lax

PTS = 8
EX = 2
EY = 2
EZ = 16
KV = 4
CGZ = 4
GX = 16
GY = 8
NV = 128
N_BX = 8
N_BY = 4


def draw_basis(key, part):
    noise_key = jax.random.fold_in(key, 11)
    share_key = jax.random.fold_in(key, 12)
    sign_key = jax.random.fold_in(key, 13)
    shape = (KV, GX, GY, EZ, PTS ** 3)
    raw = jax.random.truncated_normal(noise_key, -6.0, 6.0, shape, jnp.float32)
    share = jax.random.uniform(share_key, (KV - 1,), jnp.float32, 0.35, 0.75)
    signs = jnp.where(jax.random.bernoulli(sign_key, 0.5, (KV - 1,)), 1.0, -1.0).astype(jnp.float32)
    share = share * signs
    keep = jnp.concatenate([jnp.sqrt(1.0 - share * share), jnp.ones((1,), jnp.float32)])
    along = jnp.concatenate([share, jnp.zeros((1,), jnp.float32)])
    mixed = raw * keep[:, None, None, None, None] + along[:, None, None, None, None] * raw[KV - 1][None]
    return jnp.clip(mixed, -6.0, 6.0)


def draw_modes(key, part):
    raw = jax.random.normal(key, (3, PTS, PTS), jnp.float32)
    ortho, upper = jnp.linalg.qr(raw)
    return ortho


def draw_vertex_ids(key, part):
    bricks_x = GX // EX
    bricks_y = GY // EY
    order = jax.random.permutation(key, bricks_x * bricks_y * CGZ).astype(jnp.int32)
    order = order.reshape(bricks_x, bricks_y, CGZ)
    outer = []
    for shift_x in range(2):
        inner = []
        for shift_y in range(2):
            inner.append(jnp.roll(jnp.roll(order, -shift_x, axis=0), -shift_y, axis=1))
        outer.append(jnp.stack(inner, axis=2))
    return jnp.stack(outer, axis=2)


def draw_coarse_inverse(key, part):
    raw = jax.random.normal(key, (NV, NV), jnp.float32)
    return (raw + raw.T) / (2.0 * jnp.sqrt(jnp.float32(NV))) + 2.0 * jnp.eye(NV, dtype=jnp.float32)


def set_ends(values, own_key, low, top_value):
    shape = values.shape
    spot = [jax.random.randint(jax.random.fold_in(own_key, axis), (), 0, shape[axis]) for axis in range(len(shape))]
    values = values.at[tuple(spot)].set(low)
    longest = shape.index(max(shape))
    spot[longest] = (spot[longest] + 1) % shape[longest]
    return values.at[tuple(spot)].set(top_value)


def block_scale(key, extent, split, smallest, top_value):
    def one(position, shards_of):
        steps = jax.random.uniform(jax.random.fold_in(jax.random.fold_in(key, 6), position), (shards_of,), jnp.float32, smallest / len(split), top_value / len(split))
        return jnp.repeat(jnp.exp(steps), extent[position] // shards_of).reshape((-1,) + (1,) * (len(extent) - position - 1))

    level = one(*split[0])
    for cut in split[1:]:
        level = level * one(*cut)
    return level


def setup_inputs(seed: int = 0) -> dict:
    key_list = jax.random.split(jax.random.key(seed), 8)
    return {
        "basis": draw_basis(jax.random.fold_in(key_list[7], 71), 0),
        "coef": jnp.clip(jnp.exp(math.log(4.0) - 2.0794415 * jax.random.uniform(key_list[1], (GX, GY, EZ), jnp.float32) ** block_scale(key_list[1], (GX, GY, EZ), ((0, 8), (1, 4)), -0.2, 0.2)), 0.5, 4.0),
        "modes": draw_modes(jax.random.fold_in(key_list[7], 71), 0),
        "eigen": jnp.clip(jnp.exp(jax.random.uniform(key_list[3], (3, PTS), jnp.float32, math.log(0.2), math.log(20.0))), 0.2, 20.0),
        "mask": set_ends((jax.random.randint(key_list[4], (GX, GY, EZ), 0, 8) < 7).astype(jnp.int32), jax.random.fold_in(key_list[4], 1), 0, 1),
        "vertex_ids": draw_vertex_ids(jax.random.fold_in(key_list[7], 71), 0),
        "coarse_inverse": draw_coarse_inverse(jax.random.fold_in(key_list[7], 71), 0),
    }


PENALTY = 2.0
SHIFT = 1.0
EPSILON = 1e-06
HIGHEST = lax.Precision.HIGHEST

def tensor_modes(modes):
    return jnp.kron(jnp.kron(modes[0], modes[1]), modes[2])

def mode_values(eigen):
    return (eigen[0][:, None, None] + eigen[1][None, :, None] + eigen[2][None, None, :]).reshape(PTS ** 3)

def face_count():
    points = jnp.arange(PTS)
    on_edge = ((points == 0) | (points == PTS - 1)).astype(jnp.float32)
    return (on_edge[:, None, None] + on_edge[None, :, None] + on_edge[None, None, :]).reshape(PTS ** 3)

def hat_weights(elements, levels):
    place = (jnp.arange(elements)[:, None] * (PTS - 1) + jnp.arange(PTS)[None, :]).astype(jnp.float32)
    place = place / float(elements * (PTS - 1)) * float(levels - 1)
    return jnp.maximum(0.0, 1.0 - jnp.abs(place[..., None] - jnp.arange(levels).astype(jnp.float32)))

def assemble(prev_x, next_x, prev_y, next_y, prev_z, next_z):
    middle = [jnp.zeros_like(prev_x)] * (PTS - 2)
    summed = jnp.stack([prev_x] + middle + [next_x], axis=-3)
    summed = summed + jnp.stack([prev_y] + middle + [next_y], axis=-2)
    summed = summed + jnp.stack([prev_z] + middle + [next_z], axis=-1)
    return summed.reshape(summed.shape[:-3] + (PTS ** 3,))

def neighbors(values):
    layers = values.reshape(values.shape[:-1] + (PTS, PTS, PTS))
    next_x = jnp.roll(layers[..., 0, :, :], -1, axis=0)
    prev_x = jnp.roll(layers[..., PTS - 1, :, :], 1, axis=0)
    next_y = jnp.roll(layers[..., :, 0, :], -1, axis=1)
    prev_y = jnp.roll(layers[..., :, PTS - 1, :], 1, axis=1)
    top_z = layers[..., PTS - 1]
    bottom_z = layers[..., 0]
    zeros_face = jnp.zeros_like(top_z[:, :, :1])
    prev_z = jnp.concatenate([zeros_face, top_z[:, :, :-1]], axis=2)
    next_z = jnp.concatenate([bottom_z[:, :, 1:], zeros_face], axis=2)
    return assemble(prev_x, next_x, prev_y, next_y, prev_z, next_z)

def reference(basis, coef, modes, eigen, mask, vertex_ids, coarse_inverse):
    nodes = PTS ** 3
    modal_basis = tensor_modes(modes)
    modal_low = modal_basis.astype(jnp.bfloat16)
    spectrum = mode_values(eigen)
    current = basis[KV - 1]
    shape = current.shape
    active = mask.astype(jnp.float32)[..., None]
    extended = (current + neighbors(current)).astype(jnp.bfloat16).reshape(-1, nodes)
    modal_coef = jnp.dot(extended.astype(jnp.float32), modal_low.astype(jnp.float32), preferred_element_type=jnp.float32)
    divisor = coef.reshape(-1, 1) * spectrum[None, :] + SHIFT
    modal_coef = (modal_coef / divisor).astype(jnp.bfloat16)
    smooth = jnp.dot(modal_coef.astype(jnp.float32), modal_low.T.astype(jnp.float32), preferred_element_type=jnp.float32).reshape(shape) * active
    weight_x = hat_weights(EX, 2)
    weight_y = hat_weights(EY, 2)
    weight_z = hat_weights(EZ, CGZ)
    scale = 1.0 / math.sqrt(EX * EY * EZ * nodes)
    bricks = current.reshape(N_BX, EX, N_BY, EY, EZ, PTS, PTS, PTS)
    brick_sums = jnp.einsum('pxqyzijk,xia,yjb,zkl->pqabl', bricks, weight_x, weight_y, weight_z, precision=HIGHEST) * scale
    coarse = jax.ops.segment_sum(brick_sums.reshape(-1), vertex_ids.reshape(-1), num_segments=NV)
    solved = jnp.dot(coarse_inverse, coarse, precision=HIGHEST)
    corner_values = solved[vertex_ids]
    prolonged = jnp.einsum('pqabl,xia,yjb,zkl->pxqyzijk', corner_values, weight_x, weight_y, weight_z, precision=HIGHEST)
    precond = smooth + active * prolonged.reshape(shape)
    flattened = precond.reshape(-1, nodes)
    modal_image = jnp.dot(flattened, modal_basis, precision=HIGHEST) * spectrum[None, :] * coef.reshape(-1, 1)
    local_image = jnp.dot(modal_image, modal_basis.T, precision=HIGHEST).reshape(shape)
    image = active * (local_image + PENALTY * (face_count() * precond - neighbors(precond)))
    total_points = float(GX * GY * EZ * nodes)

    def project(vector):
        return jnp.sum(vector * image)
    proj = lax.map(project, basis) / total_points
    residual = image - jnp.tensordot(proj, basis, axes=1, precision=HIGHEST)
    beta = jnp.sqrt(jnp.sum(residual * residual) / total_points + EPSILON)
    next_vector = residual / beta
    hessen = jnp.concatenate([proj, beta[None]])
    return (precond, next_vector, hessen)
```

```python
import functools
import math

import jax
import jax.numpy as jnp
from jax import lax
from jax.experimental import pallas as pl
from jax.experimental.pallas import tpu as pltpu
from jax.sharding import PartitionSpec as P

PTS = 8
NODES = PTS**3
KV = 4
CGZ = 4
EX = 2
EY = 2
EZ = 16
LANES = 128

PENALTY = 2.0
SHIFT = 1.0
EPSILON = 1e-06
HIGHEST = lax.Precision.HIGHEST
F32 = jnp.float32
BF16 = jnp.bfloat16


def lane_ids(rows, lanes):
    return lax.broadcasted_iota(jnp.int32, (rows, lanes), 1)


def row_ids(rows, lanes):
    return lax.broadcasted_iota(jnp.int32, (rows, lanes), 0)


def roll_chunks(x, shift):
    shift = shift % LANES
    if shift == 0:
        return x
    pieces = [
        pltpu.roll(x[:, c : c + LANES], shift, 1) for c in range(0, x.shape[1], LANES)
    ]
    return pieces[0] if len(pieces) == 1 else jnp.concatenate(pieces, axis=1)


def column(row):
    wide = jnp.broadcast_to(row, (EZ, EZ))
    keep = row_ids(EZ, EZ) == lane_ids(EZ, EZ)
    return jnp.sum(jnp.where(keep, wide, jnp.zeros_like(wide)), axis=1, keepdims=True)


def columns(ref):
    return [[column(ref[x, y : y + 1, :].astype(F32)) for y in range(EY)] for x in range(EX)]


def blocks_of(parts):
    return [part[8 * b : 8 * b + 8] for part in parts for b in range(EZ // 8)]


def pack_x(parts, high):
    low_half = lane_ids(8, LANES) < 64
    offset = NODES - LANES if high else 0
    cut = [block[:, offset : offset + LANES] for block in blocks_of(parts)]
    out = []
    for m in range(2):
        even = pltpu.roll(cut[2 * m], 64, 1) if high else cut[2 * m]
        odd = cut[2 * m + 1] if high else pltpu.roll(cut[2 * m + 1], 64, 1)
        out.append(jnp.where(low_half, even, odd))
    return jnp.concatenate(out, axis=1)


def unpack_x(packed, high):
    low_half = lane_ids(8, LANES) < 64
    zero = jnp.zeros((8, LANES), F32)
    groups = []
    for g in range(2):
        rows = []
        for b in (2 * g, 2 * g + 1):
            chunk = packed[:, LANES * (b // 2) : LANES * (b // 2) + LANES]
            if (b % 2 == 0) == high:
                chunk = pltpu.roll(chunk, 64, 1)
            chunk = jnp.where(low_half, zero, chunk) if high else jnp.where(low_half, chunk, zero)
            rows.append(
                jnp.concatenate([zero] * 3 + [chunk] if high else [chunk] + [zero] * 3, axis=1)
            )
        groups.append(jnp.concatenate(rows, axis=0))
    return groups


def pack_y(parts, high):
    slot = lane_ids(8, NODES) // PTS % PTS
    from_slot = PTS - 1 if high else 0
    total = jnp.zeros((8, NODES), F32)
    for b, block in enumerate(blocks_of(parts)):
        total = jnp.where(slot == b, roll_chunks(block, PTS * (b - from_slot)), total)
    lower, upper = total[:, :256], roll_chunks(total[:, 256:], 32)
    return jnp.where(slot[:, :256] < 4, lower, upper)


def unpack_y(packed, high):
    slot = lane_ids(8, LANES) // PTS % PTS
    to_slot = PTS - 1 if high else 0
    zero = jnp.zeros((8, LANES), F32)
    groups = []
    for g in range(2):
        rows = []
        for b in (2 * g, 2 * g + 1):
            chunks = []
            for c in range(4):
                source = packed[:, LANES * (c % 2) : LANES * (c % 2) + LANES]
                moved = roll_chunks(source, PTS * (to_slot - b - 4 * (c // 2)))
                chunks.append(jnp.where(slot == to_slot, moved, zero))
            rows.append(jnp.concatenate(chunks, axis=1))
        groups.append(jnp.concatenate(rows, axis=0))
    return groups


def pack_all(groups):
    return [
        pack_x([groups[EX - 1][y] for y in range(EY)], True),
        pack_x([groups[0][y] for y in range(EY)], False),
        pack_y([groups[x][EY - 1] for x in range(EX)], True),
        pack_y([groups[x][0] for x in range(EX)], False),
    ]


def unpack_all(packed):
    left = unpack_x(packed[0], False)
    right = unpack_x(packed[1], True)
    front = unpack_y(packed[2], False)
    back = unpack_y(packed[3], True)
    out = [[None] * EY for _ in range(EX)]
    for x in range(EX):
        for y in range(EY):
            terms = []
            if x == 0:
                terms.append(left[y])
            if x == EX - 1:
                terms.append(right[y])
            if y == 0:
                terms.append(front[x])
            if y == EY - 1:
                terms.append(back[x])
            out[x][y] = functools.reduce(jnp.add, terms)
    return out


def own_neighbors(groups):
    lane = lane_ids(EZ, NODES)
    row = row_ids(EZ, NODES)
    i, j, k = lane // (PTS * PTS), lane // PTS % PTS, lane % PTS
    low_z = jnp.logical_and(k == 0, row > 0)
    high_z = jnp.logical_and(k == PTS - 1, row < EZ - 1)
    zero = jnp.zeros((EZ, NODES), F32)
    pad = jnp.zeros((EZ, NODES - LANES), F32)
    low_half = lane_ids(EZ, LANES) < 64
    zero_chunk = jnp.zeros((EZ, LANES), F32)
    out = [[None] * EY for _ in range(EX)]
    for x in range(EX):
        for y in range(EY):
            here = groups[x][y]
            total = jnp.where(low_z, roll_chunks(pltpu.roll(here, 1, 0), 1 - PTS), zero)
            total = total + jnp.where(
                high_z, roll_chunks(pltpu.roll(here, EZ - 1, 0), PTS - 1), zero
            )
            if y > 0:
                moved = roll_chunks(groups[x][y - 1], PTS - PTS * PTS)
                total = total + jnp.where(j == 0, moved, zero)
            if y < EY - 1:
                moved = roll_chunks(groups[x][y + 1], PTS * PTS - PTS)
                total = total + jnp.where(j == PTS - 1, moved, zero)
            if x > 0:
                chunk = pltpu.roll(groups[x - 1][y][:, NODES - LANES :], 64, 1)
                chunk = jnp.where(low_half, chunk, zero_chunk)
                total = total + jnp.concatenate([chunk, pad], axis=1)
            if x < EX - 1:
                chunk = pltpu.roll(groups[x + 1][y][:, :LANES], 64, 1)
                chunk = jnp.where(low_half, zero_chunk, chunk)
                total = total + jnp.concatenate([pad, chunk], axis=1)
            out[x][y] = total
    return out


def load_groups(ref, *lead):
    return [[ref[(*lead, x, y)] for y in range(EY)] for x in range(EX)]


def stack(groups):
    return jnp.concatenate([groups[x][y] for x in range(EX) for y in range(EY)], axis=0)


def unstack(whole):
    return [
        [whole[(x * EY + y) * EZ : (x * EY + y + 1) * EZ] for y in range(EY)] for x in range(EX)
    ]


def hat(place, span, levels, level):
    place = place.astype(F32) / float(span) * float(levels - 1)
    return jnp.maximum(0.0, 1.0 - jnp.abs(place - float(level)))


def hat_z():
    lane, row = lane_ids(EZ, NODES), row_ids(EZ, NODES)
    place = row * (PTS - 1) + lane % PTS
    return [hat(place, EZ * (PTS - 1), CGZ, level) for level in range(CGZ)]


def hat_x(x, a, rows=1):
    place = x * (PTS - 1) + lane_ids(rows, NODES) // (PTS * PTS)
    return hat(place, EX * (PTS - 1), 2, a)


def hat_y(y, b, rows=1):
    place = y * (PTS - 1) + lane_ids(rows, NODES) // PTS % PTS
    return hat(place, EY * (PTS - 1), 2, b)


def face_count(rows):
    lane = lane_ids(rows, NODES)
    total = jnp.zeros((rows, NODES), F32)
    for part in (lane // (PTS * PTS), lane // PTS % PTS, lane % PTS):
        edge = jnp.logical_or(part == 0, part == PTS - 1)
        total = total + jnp.where(edge, 1.0, 0.0)
    return total


def all_sum(x):
    return jnp.sum(jnp.sum(x, axis=0, keepdims=True), axis=1, keepdims=True)


def coarse_row(current, ids_ref, count, scale):
    weight_z = hat_z()
    lane = lane_ids(1, count)
    out = jnp.zeros((1, count), F32)
    for level in range(CGZ):
        sums = [[None] * EY for _ in range(EX)]
        for x in range(EX):
            for y in range(EY):
                sums[x][y] = jnp.sum(current[x][y] * weight_z[level], axis=0, keepdims=True)
        for a in range(2):
            for b in range(2):
                total = jnp.zeros((1, NODES), F32)
                for x in range(EX):
                    for y in range(EY):
                        total = total + sums[x][y] * (hat_x(x, a) * hat_y(y, b))
                value = jnp.sum(total, axis=1, keepdims=True) * scale
                out = out + jnp.where(lane == ids_ref[0, 0, a, b, level], value, 0.0)
    return out


def start_kernel(scale, count, rows, peers, with_inverse, *refs):
    current_ref, mask_ref, ids_ref, inverse_ref = refs[:4]
    row_ref, xp_ref, xm_ref, yp_ref, ym_ref = refs[4:]
    current = load_groups(current_ref, 0)
    active = columns(mask_ref)
    wide = [[jnp.broadcast_to(active[x][y], (EZ, NODES)) for y in range(EY)] for x in range(EX)]
    faces, masks = pack_all(current), pack_all(wide)
    for ref, face, part in zip((xp_ref, xm_ref, yp_ref, ym_ref), faces, masks):
        ref[0:8, :] = face
        ref[8:16, :] = part
    row = coarse_row(current, ids_ref, count, scale)
    if with_inverse:
        first = lax.axis_index("by") * rows
        pieces = [inverse_ref[pl.ds(first + r, 1), :] for r in range(rows)]
        row = jnp.concatenate([row] + pieces, axis=1)
    row_ref[...] = jnp.broadcast_to(row, (peers, row.shape[1]))


def expand(matrix, stride):
    pick = (lane_ids(PTS, NODES) // stride % PTS == row_ids(PTS, NODES)).astype(F32)
    return jnp.dot(matrix, pick, precision=HIGHEST, preferred_element_type=F32)


def tables_kernel(modes_ref, eigen_ref, sb_ref, st_ref, lh_ref, ll_ref):
    strides = (PTS * PTS, PTS, 1)
    eye = (row_ids(PTS, PTS) == lane_ids(PTS, PTS)).astype(F32)
    straight, turned, stiff, unit = [], [], [], []
    for d in range(3):
        mode = modes_ref[d]
        turn = lax.dot_general(
            mode, eye, (((0,), (0,)), ((), ())), precision=HIGHEST, preferred_element_type=F32
        )
        scaled = mode * eigen_ref[d : d + 1, :]
        one = jnp.dot(scaled, turn, precision=HIGHEST, preferred_element_type=F32)
        straight.append(expand(mode, strides[d]))
        turned.append(expand(turn, strides[d]))
        stiff.append(expand(one, strides[d]))
        unit.append(expand(eye, strides[d]))
    for i in range(PTS):
        for j in range(PTS):
            rows = slice((i * PTS + j) * PTS, (i * PTS + j + 1) * PTS)
            pair = straight[0][i : i + 1] * straight[1][j : j + 1]
            sb_ref[rows, :] = (pair * straight[2]).astype(BF16)
            pair = turned[0][i : i + 1] * turned[1][j : j + 1]
            st_ref[rows, :] = (pair * turned[2]).astype(BF16)
            both = unit[0][i : i + 1] * unit[1][j : j + 1]
            either = stiff[0][i : i + 1] * unit[1][j : j + 1] + unit[0][i : i + 1] * stiff[1][j : j + 1]
            full = either * unit[2] + both * stiff[2]
            head = full.astype(BF16)
            lh_ref[rows, :] = head
            ll_ref[rows, :] = (full - head.astype(F32)).astype(BF16)


def spectrum_row(eigen_ref):
    out = jnp.zeros((1, NODES), F32)
    for d, stride in enumerate((PTS * PTS, PTS, 1)):
        pick = (lane_ids(PTS, NODES) // stride % PTS == row_ids(PTS, NODES)).astype(F32)
        out = out + jnp.dot(
            eigen_ref[d : d + 1, :], pick, precision=HIGHEST, preferred_element_type=F32
        )
    return out


def smooth_kernel(*refs):
    current_ref, coef_ref, mask_ref, eigen_ref, sb_ref, st_ref = refs[:6]
    halo = [ref[0:8, :] for ref in refs[6:10]]
    smooth_ref, *send = refs[10:]
    current = load_groups(current_ref, 0)
    inside, outside = own_neighbors(current), unpack_all(halo)
    coef, active = columns(coef_ref), columns(mask_ref)
    extended = [
        [current[x][y] + (inside[x][y] + outside[x][y]) for y in range(EY)] for x in range(EX)
    ]
    modal = jnp.dot(stack(extended).astype(BF16), sb_ref[...], preferred_element_type=F32)
    modal = unstack(modal)
    spectrum = spectrum_row(eigen_ref)
    modal = [
        [modal[x][y] / (coef[x][y] * spectrum + SHIFT) for y in range(EY)] for x in range(EX)
    ]
    smooth = jnp.dot(stack(modal).astype(BF16), st_ref[...], preferred_element_type=F32)
    smooth = unstack(smooth)
    smooth = [[smooth[x][y] * active[x][y] for y in range(EY)] for x in range(EX)]
    for x in range(EX):
        for y in range(EY):
            smooth_ref[x, y] = smooth[x][y]
    for ref, face in zip(send, pack_all(smooth)):
        ref[...] = face


def stiff_apply(groups, lh_ref, ll_ref):
    whole = stack(groups)
    head = whole.astype(BF16)
    tail = (whole - head.astype(F32)).astype(BF16)
    rows = whole.shape[0]
    both = jnp.dot(jnp.concatenate([head, tail], axis=0), lh_ref[...], preferred_element_type=F32)
    low = jnp.dot(head, ll_ref[...], preferred_element_type=F32)
    return unstack(both[:rows] + (both[rows:] + low))


def image_kernel(count, rows, peers, *refs):
    basis_ref, smooth_ref, coef_ref, mask_ref, ids_ref, got_ref, lh_ref, ll_ref = refs[:8]
    face_refs, mask_refs = refs[8:12], refs[12:16]
    precond_ref, image_ref, row_ref = refs[16:]
    coef, active = columns(coef_ref), columns(mask_ref)
    coarse = jnp.sum(got_ref[:, :count], axis=0, keepdims=True)
    solved = jnp.zeros((1, count), F32) if rows else coarse
    lane = lane_ids(1, count)
    picker_lane = lane_ids(peers, count)
    picker_row = row_ids(peers, count)
    for r in range(rows):
        pick = (picker_lane == picker_row * rows + r).astype(F32)
        part = jnp.sum(pick * coarse, axis=1, keepdims=True)
        block = got_ref[:, count * (r + 1) : count * (r + 2)]
        solved = solved + jnp.sum(part * block, axis=0, keepdims=True)
    weight_z = hat_z()
    field = [[jnp.zeros((EZ, NODES), F32) for _ in range(EY)] for _ in range(EX)]
    for a in range(2):
        for b in range(2):
            along = jnp.zeros((EZ, NODES), F32)
            for level in range(CGZ):
                hit = jnp.where(lane == ids_ref[0, 0, a, b, level], solved, 0.0)
                along = along + weight_z[level] * jnp.sum(hit, axis=1, keepdims=True)
            for x in range(EX):
                for y in range(EY):
                    field[x][y] = field[x][y] + along * (hat_x(x, a) * hat_y(y, b))
    smooth = load_groups(smooth_ref)
    precond = [
        [smooth[x][y] + active[x][y] * field[x][y] for y in range(EY)] for x in range(EX)
    ]
    stiff = stiff_apply(precond, lh_ref, ll_ref)
    inside = own_neighbors(precond)
    outside = unpack_all([ref[...] for ref in face_refs])
    open_faces = unpack_all([ref[8:16, :] for ref in mask_refs])
    counts = face_count(EZ)
    dots = [jnp.zeros((EZ, NODES), F32) for _ in range(KV + 1)]
    for x in range(EX):
        for y in range(EY):
            across = outside[x][y] + open_faces[x][y] * field[x][y]
            image = active[x][y] * (
                coef[x][y] * stiff[x][y]
                + PENALTY * (counts * precond[x][y] - (inside[x][y] + across))
            )
            precond_ref[x, y] = precond[x][y]
            image_ref[x, y] = image
            for v in range(KV):
                dots[v] = dots[v] + basis_ref[v, x, y] * image
            dots[KV] = dots[KV] + image * image
    values = [all_sum(d) for d in dots]
    basis = [load_groups(basis_ref, v) for v in range(KV)]
    for v in range(KV):
        for u in range(v, KV):
            total = jnp.zeros((EZ, NODES), F32)
            for x in range(EX):
                for y in range(EY):
                    total = total + basis[v][x][y] * basis[u][x][y]
            values.append(all_sum(total))
    row = jnp.zeros((1, LANES), F32)
    row_lane = lane_ids(1, LANES)
    for position, value in enumerate(values):
        row = jnp.where(row_lane == position, value, row)
    row_ref[...] = jnp.broadcast_to(row, (peers, LANES))


def finish_kernel(total_points, basis_ref, image_ref, got_ref, next_ref, hessen_ref):
    sums = jnp.sum(got_ref[...], axis=0, keepdims=True) / total_points
    lane = lane_ids(1, LANES)

    def pick(position):
        return jnp.sum(jnp.where(lane == position, sums, 0.0), axis=1, keepdims=True)

    proj = [pick(v) for v in range(KV)]
    square = pick(KV)
    position = KV + 1
    quad = jnp.zeros((1, 1), F32)
    for v in range(KV):
        for u in range(v, KV):
            factor = 1.0 if u == v else 2.0
            quad = quad + factor * proj[v] * proj[u] * pick(position)
            position += 1
    dot = functools.reduce(jnp.add, [p * p for p in proj])
    beta = jnp.sqrt(square - 2.0 * dot + quad + EPSILON)
    for x in range(EX):
        for y in range(EY):
            residual = image_ref[x, y]
            for v in range(KV):
                residual = residual - proj[v] * basis_ref[v, x, y]
            next_ref[x, y] = residual / beta
    for v, value in enumerate(proj + [beta]):
        hessen_ref[v] = jnp.sum(value)


def spec(kind=pltpu.VMEM):
    return pl.BlockSpec(memory_space=kind)


def call(kernel, outs, in_specs, args, out_specs=None, flops=1000000):
    return pl.pallas_call(
        kernel,
        out_shape=[jax.ShapeDtypeStruct(shape, dtype) for shape, dtype in outs],
        in_specs=in_specs,
        grid=(1,),
        out_specs=out_specs or [spec() for _ in outs],
        cost_estimate=pl.CostEstimate(flops=flops, bytes_accessed=1000000, transcendentals=0),
    )(*args)


def exchange(sends):
    out = []
    for (axis, up), send in zip((("bx", True), ("bx", False), ("by", True), ("by", False)), sends):
        size = lax.axis_size(axis)
        ring = [(i, (i + 1) % size) for i in range(size)]
        if not up:
            ring = [(j, i) for i, j in ring]
        out.append(lax.ppermute(send, axis, ring))
    return out


def body(basis, coef, modes, eigen, mask, vertex_ids, coarse_inverse):
    assert coef.shape == (EX, EY, EZ) and basis.shape[0] == KV
    size_x, size_y = lax.axis_size("bx"), lax.axis_size("by")
    peers = size_x * size_y
    count = coarse_inverse.shape[1]
    points = EX * EY * EZ * NODES
    rows = coarse_inverse.shape[0] // size_y
    with_inverse = peers * count * (rows + 1) * 4 <= 4 << 20
    current_spec = pl.BlockSpec((1, EX, EY, EZ, NODES), lambda step: (KV - 1, 0, 0, 0, 0))
    field = ((EX, EY, EZ, NODES), F32)
    width = count * (rows + 1) if with_inverse else count
    row, *sends = call(
        functools.partial(start_kernel, 1.0 / math.sqrt(points), count, rows, peers, with_inverse),
        [((peers if with_inverse else 1, width), F32)] + [((16, 256), F32)] * 4,
        [current_spec, spec(), spec(pltpu.SMEM), spec() if with_inverse else spec(pl.ANY)],
        (basis, mask, vertex_ids, coarse_inverse),
    ) if with_inverse else call(
        functools.partial(start_kernel, 1.0 / math.sqrt(points), count, rows, 1, with_inverse),
        [((1, width), F32)] + [((16, 256), F32)] * 4,
        [current_spec, spec(), spec(pltpu.SMEM), spec(pl.ANY)],
        (basis, mask, vertex_ids, coarse_inverse),
    )
    if with_inverse:
        got = lax.all_to_all(row, ("bx", "by"), 0, 0, tiled=True)
    else:
        coarse = lax.psum(row, ("bx", "by"))
        solved = jnp.dot(coarse_inverse, coarse[0], precision=HIGHEST)
        solved = lax.all_gather(solved, "bx", axis=0, tiled=True)
        got = solved[None]
    halo = exchange(sends)
    square = ((NODES, NODES), BF16)
    tables = call(tables_kernel, [square] * 4, [spec(), spec()], (modes, eigen))
    smooth, *sends = call(
        smooth_kernel,
        [field] + [((8, 256), F32)] * 4,
        [current_spec] + [spec()] * 9,
        (basis, coef, mask, eigen, tables[0], tables[1], *halo),
    )
    faces = exchange(sends)
    precond, image, row = call(
        functools.partial(image_kernel, count, rows if with_inverse else 0, peers),
        [field, field, ((peers, LANES), F32)],
        [spec()] * 4 + [spec(pltpu.SMEM)] + [spec()] * 11,
        (basis, smooth, coef, mask, vertex_ids, got, tables[2], tables[3], *faces, *halo),
    )
    got = lax.all_to_all(row, ("bx", "by"), 0, 0, tiled=True)
    next_vector, hessen = call(
        functools.partial(finish_kernel, float(points * peers)),
        [field, ((KV + 1,), F32)],
        [spec()] * 3,
        (basis, image, got),
        out_specs=[spec(), spec(pltpu.SMEM)],
    )
    return (precond, next_vector, hessen)


def solution(mesh):
    placed = (
        P(None, "bx", "by", None, None),
        P("bx", "by", None),
        P(),
        P(),
        P("bx", "by", None),
        P("bx", "by", None, None, None),
        P("bx", None),
    )
    return jax.shard_map(
        body,
        mesh=mesh,
        in_specs=placed,
        out_specs=(P("bx", "by", None, None), P("bx", "by", None, None), P()),
        check_vma=False,
    )
```

```python
import functools
import math

import jax
import jax.numpy as jnp
from jax import lax
from jax.experimental import pallas as pl
from jax.experimental.pallas import tpu as pltpu
from jax.sharding import PartitionSpec as P

PTS = 8
NODES = PTS**3
KV = 4
CGZ = 4
EX = 2
EY = 2
EZ = 16
LANES = 128
HALF = 8
XY = 4 * EX * EY
VERTS = 4 * CGZ

PENALTY = 2.0
SHIFT = 1.0
EPSILON = 1e-06
HIGHEST = lax.Precision.HIGHEST
F32 = jnp.float32
BF16 = jnp.bfloat16


def lane_ids(rows, lanes):
    return lax.broadcasted_iota(jnp.int32, (rows, lanes), 1)


def row_ids(rows, lanes):
    return lax.broadcasted_iota(jnp.int32, (rows, lanes), 0)


def roll_chunks(x, shift):
    shift = shift % LANES
    if shift == 0:
        return x
    pieces = [
        pltpu.roll(x[:, c : c + LANES], shift, 1) for c in range(0, x.shape[1], LANES)
    ]
    return pieces[0] if len(pieces) == 1 else jnp.concatenate(pieces, axis=1)


def column(row):
    wide = jnp.broadcast_to(row, (EZ, EZ))
    keep = row_ids(EZ, EZ) == lane_ids(EZ, EZ)
    return jnp.sum(jnp.where(keep, wide, jnp.zeros_like(wide)), axis=1, keepdims=True)


def columns(ref):
    return [[column(ref[x, y : y + 1, :].astype(F32)) for y in range(EY)] for x in range(EX)]


def blocks_of(parts):
    return [part[8 * b : 8 * b + 8] for part in parts for b in range(EZ // 8)]


def pack_x(parts, high):
    low_half = lane_ids(8, LANES) < 64
    offset = NODES - LANES if high else 0
    cut = [block[:, offset : offset + LANES] for block in blocks_of(parts)]
    out = []
    for m in range(2):
        even = pltpu.roll(cut[2 * m], 64, 1) if high else cut[2 * m]
        odd = cut[2 * m + 1] if high else pltpu.roll(cut[2 * m + 1], 64, 1)
        out.append(jnp.where(low_half, even, odd))
    return jnp.concatenate(out, axis=1)


def unpack_x(packed, high):
    low_half = lane_ids(8, LANES) < 64
    zero = jnp.zeros((8, LANES), F32)
    groups = []
    for g in range(2):
        rows = []
        for b in (2 * g, 2 * g + 1):
            chunk = packed[:, LANES * (b // 2) : LANES * (b // 2) + LANES]
            if (b % 2 == 0) == high:
                chunk = pltpu.roll(chunk, 64, 1)
            chunk = jnp.where(low_half, zero, chunk) if high else jnp.where(low_half, chunk, zero)
            rows.append(
                jnp.concatenate([zero] * 3 + [chunk] if high else [chunk] + [zero] * 3, axis=1)
            )
        groups.append(jnp.concatenate(rows, axis=0))
    return groups


def pack_y(parts, high):
    slot = lane_ids(8, NODES) // PTS % PTS
    from_slot = PTS - 1 if high else 0
    total = jnp.zeros((8, NODES), F32)
    for b, block in enumerate(blocks_of(parts)):
        total = jnp.where(slot == b, roll_chunks(block, PTS * (b - from_slot)), total)
    lower, upper = total[:, :256], roll_chunks(total[:, 256:], 32)
    return jnp.where(slot[:, :256] < 4, lower, upper)


def unpack_y(packed, high):
    slot = lane_ids(8, LANES) // PTS % PTS
    to_slot = PTS - 1 if high else 0
    zero = jnp.zeros((8, LANES), F32)
    groups = []
    for g in range(2):
        rows = []
        for b in (2 * g, 2 * g + 1):
            chunks = []
            for c in range(4):
                source = packed[:, LANES * (c % 2) : LANES * (c % 2) + LANES]
                moved = roll_chunks(source, PTS * (to_slot - b - 4 * (c // 2)))
                chunks.append(jnp.where(slot == to_slot, moved, zero))
            rows.append(jnp.concatenate(chunks, axis=1))
        groups.append(jnp.concatenate(rows, axis=0))
    return groups


def pack_all(groups):
    return [
        pack_x([groups[EX - 1][y] for y in range(EY)], True),
        pack_x([groups[0][y] for y in range(EY)], False),
        pack_y([groups[x][EY - 1] for x in range(EX)], True),
        pack_y([groups[x][0] for x in range(EX)], False),
    ]


def unpack_all(packed):
    left = unpack_x(packed[0], False)
    right = unpack_x(packed[1], True)
    front = unpack_y(packed[2], False)
    back = unpack_y(packed[3], True)
    out = [[None] * EY for _ in range(EX)]
    for x in range(EX):
        for y in range(EY):
            terms = []
            if x == 0:
                terms.append(left[y])
            if x == EX - 1:
                terms.append(right[y])
            if y == 0:
                terms.append(front[x])
            if y == EY - 1:
                terms.append(back[x])
            out[x][y] = functools.reduce(jnp.add, terms)
    return out


def own_neighbors(groups):
    lane = lane_ids(EZ, NODES)
    row = row_ids(EZ, NODES)
    i, j, k = lane // (PTS * PTS), lane // PTS % PTS, lane % PTS
    low_z = jnp.logical_and(k == 0, row > 0)
    high_z = jnp.logical_and(k == PTS - 1, row < EZ - 1)
    zero = jnp.zeros((EZ, NODES), F32)
    pad = jnp.zeros((EZ, NODES - LANES), F32)
    low_half = lane_ids(EZ, LANES) < 64
    zero_chunk = jnp.zeros((EZ, LANES), F32)
    out = [[None] * EY for _ in range(EX)]
    for x in range(EX):
        for y in range(EY):
            here = groups[x][y]
            total = jnp.where(low_z, roll_chunks(pltpu.roll(here, 1, 0), 1 - PTS), zero)
            total = total + jnp.where(
                high_z, roll_chunks(pltpu.roll(here, EZ - 1, 0), PTS - 1), zero
            )
            if y > 0:
                moved = roll_chunks(groups[x][y - 1], PTS - PTS * PTS)
                total = total + jnp.where(j == 0, moved, zero)
            if y < EY - 1:
                moved = roll_chunks(groups[x][y + 1], PTS * PTS - PTS)
                total = total + jnp.where(j == PTS - 1, moved, zero)
            if x > 0:
                chunk = pltpu.roll(groups[x - 1][y][:, NODES - LANES :], 64, 1)
                chunk = jnp.where(low_half, chunk, zero_chunk)
                total = total + jnp.concatenate([chunk, pad], axis=1)
            if x < EX - 1:
                chunk = pltpu.roll(groups[x + 1][y][:, :LANES], 64, 1)
                chunk = jnp.where(low_half, zero_chunk, chunk)
                total = total + jnp.concatenate([pad, chunk], axis=1)
            out[x][y] = total
    return out


def load_groups(ref, *lead):
    return [[ref[(*lead, x, y)] for y in range(EY)] for x in range(EX)]


def stack(groups):
    return jnp.concatenate([groups[x][y] for x in range(EX) for y in range(EY)], axis=0)


def unstack(whole):
    return [
        [whole[(x * EY + y) * EZ : (x * EY + y + 1) * EZ] for y in range(EY)] for x in range(EX)
    ]


def hat(place, span, levels, level):
    place = place.astype(F32) / float(span) * float(levels - 1)
    return jnp.maximum(0.0, 1.0 - jnp.abs(place - float(level)))


def hat_z():
    lane, row = lane_ids(EZ, NODES), row_ids(EZ, NODES)
    place = row * (PTS - 1) + lane % PTS
    return [hat(place, EZ * (PTS - 1), CGZ, level) for level in range(CGZ)]


def hat_x(x, a, rows=1):
    place = x * (PTS - 1) + lane_ids(rows, NODES) // (PTS * PTS)
    return hat(place, EX * (PTS - 1), 2, a)


def hat_y(y, b, rows=1):
    place = y * (PTS - 1) + lane_ids(rows, NODES) // PTS % PTS
    return hat(place, EY * (PTS - 1), 2, b)


def face_count(rows):
    lane = lane_ids(rows, NODES)
    total = jnp.zeros((rows, NODES), F32)
    for part in (lane // (PTS * PTS), lane // PTS % PTS, lane % PTS):
        edge = jnp.logical_or(part == 0, part == PTS - 1)
        total = total + jnp.where(edge, 1.0, 0.0)
    return total


def all_sum(x):
    return jnp.sum(jnp.sum(x, axis=0, keepdims=True), axis=1, keepdims=True)


def coarse_row(current, ids_ref, count, scale):
    weight_z = hat_z()
    lane = lane_ids(1, count)
    out = jnp.zeros((1, count), F32)
    for level in range(CGZ):
        sums = [[None] * EY for _ in range(EX)]
        for x in range(EX):
            for y in range(EY):
                sums[x][y] = jnp.sum(current[x][y] * weight_z[level], axis=0, keepdims=True)
        for a in range(2):
            for b in range(2):
                total = jnp.zeros((1, NODES), F32)
                for x in range(EX):
                    for y in range(EY):
                        total = total + sums[x][y] * (hat_x(x, a) * hat_y(y, b))
                value = jnp.sum(total, axis=1, keepdims=True) * scale
                out = out + jnp.where(lane == ids_ref[0, 0, a, b, level], value, 0.0)
    return out


def send_faces(basis_ref, mask_ref, outs):
    current = load_groups(basis_ref, KV - 1)
    active = columns(mask_ref)
    wide = [[jnp.broadcast_to(active[x][y], (EZ, NODES)) for y in range(EY)] for x in range(EX)]
    for ref, face, part in zip(outs, pack_all(current), pack_all(wide)):
        ref[0:8, :] = face
        ref[8:16, :] = part
    return current


def start_kernel(scale, count, basis_ref, mask_ref, ids_ref, row_ref, *outs):
    current = send_faces(basis_ref, mask_ref, outs)
    row_ref[...] = coarse_row(current, ids_ref, count, scale)


def faces_kernel(basis_ref, mask_ref, *outs):
    send_faces(basis_ref, mask_ref, outs)


def expand(matrix, stride):
    pick = (lane_ids(PTS, NODES) // stride % PTS == row_ids(PTS, NODES)).astype(F32)
    return jnp.dot(matrix, pick, precision=HIGHEST, preferred_element_type=F32)


def tables_kernel(modes_ref, eigen_ref, sb_ref, st_ref, lh_ref, ll_ref, xy_ref, z_ref):
    strides = (PTS * PTS, PTS, 1)
    eye = (row_ids(PTS, PTS) == lane_ids(PTS, PTS)).astype(F32)
    straight, turned, stiff, unit = [], [], [], []
    for d in range(3):
        mode = modes_ref[d]
        turn = lax.dot_general(
            mode, eye, (((0,), (0,)), ((), ())), precision=HIGHEST, preferred_element_type=F32
        )
        scaled = mode * eigen_ref[d : d + 1, :]
        one = jnp.dot(scaled, turn, precision=HIGHEST, preferred_element_type=F32)
        straight.append(expand(mode, strides[d]))
        turned.append(expand(turn, strides[d]))
        stiff.append(expand(one, strides[d]))
        unit.append(expand(eye, strides[d]))
    for i in range(PTS):
        for j in range(PTS):
            rows = slice((i * PTS + j) * PTS, (i * PTS + j + 1) * PTS)
            pair = straight[0][i : i + 1] * straight[1][j : j + 1]
            sb_ref[rows, :] = (pair * straight[2]).astype(BF16)
            pair = turned[0][i : i + 1] * turned[1][j : j + 1]
            st_ref[rows, :] = (pair * turned[2]).astype(BF16)
            both = unit[0][i : i + 1] * unit[1][j : j + 1]
            either = stiff[0][i : i + 1] * unit[1][j : j + 1] + unit[0][i : i + 1] * stiff[1][j : j + 1]
            full = either * unit[2] + both * stiff[2]
            head = full.astype(BF16)
            lh_ref[rows, :] = head
            ll_ref[rows, :] = (full - head.astype(F32)).astype(BF16)
    point, row = lane_ids(PTS, PTS), row_ids(PTS, PTS)
    pairs = (row < 2 * EX, row // 2 * (PTS - 1) + point, row % 2)
    short = jnp.maximum(
        0.0,
        1.0 - jnp.abs(pairs[1].astype(F32) / float(EX * (PTS - 1)) - pairs[2].astype(F32)),
    )
    short = jnp.where(pairs[0], short, 0.0)
    stiff_x = jnp.dot(short, stiff[0], precision=HIGHEST, preferred_element_type=F32)
    stiff_y = jnp.dot(short, stiff[1], precision=HIGHEST, preferred_element_type=F32)
    for a in range(2):
        for b in range(2):
            for x in range(EX):
                for y in range(EY):
                    at = ((a * 2 + b) * EX + x) * EY + y
                    plain_x, plain_y = hat_x(x, a), hat_y(y, b)
                    xy_ref[at : at + 1, :] = plain_x * plain_y
                    xy_ref[XY + at : XY + at + 1, :] = (
                        stiff_x[x * 2 + a : x * 2 + a + 1] * plain_y
                        + plain_x * stiff_y[y * 2 + b : y * 2 + b + 1]
                    )
    place = row_ids(EZ, PTS) * (PTS - 1) + lane_ids(EZ, PTS)
    for level, weight in enumerate(hat_z()):
        z_ref[level * EZ : (level + 1) * EZ, :] = weight
        tall = hat(place, EZ * (PTS - 1), CGZ, level)
        z_ref[(CGZ + level) * EZ : (CGZ + level + 1) * EZ, :] = jnp.dot(
            tall, stiff[2], precision=HIGHEST, preferred_element_type=F32
        )


def spectrum_row(eigen_ref):
    out = jnp.zeros((1, NODES), F32)
    for d, stride in enumerate((PTS * PTS, PTS, 1)):
        pick = (lane_ids(PTS, NODES) // stride % PTS == row_ids(PTS, NODES)).astype(F32)
        out = out + jnp.dot(
            eigen_ref[d : d + 1, :], pick, precision=HIGHEST, preferred_element_type=F32
        )
    return out


def smooth_kernel(*refs):
    basis_ref, coef_ref, mask_ref, eigen_ref, sb_ref, st_ref = refs[:6]
    halo = [ref[0:8, :] for ref in refs[6:10]]
    smooth_ref, *send = refs[10:]
    current = load_groups(basis_ref, KV - 1)
    inside, outside = own_neighbors(current), unpack_all(halo)
    coef, active = columns(coef_ref), columns(mask_ref)
    extended = [
        [current[x][y] + (inside[x][y] + outside[x][y]) for y in range(EY)] for x in range(EX)
    ]
    modal = jnp.dot(stack(extended).astype(BF16), sb_ref[...], preferred_element_type=F32)
    modal = unstack(modal)
    spectrum = spectrum_row(eigen_ref)
    modal = [
        [modal[x][y] / (coef[x][y] * spectrum + SHIFT) for y in range(EY)] for x in range(EX)
    ]
    smooth = jnp.dot(stack(modal).astype(BF16), st_ref[...], preferred_element_type=F32)
    smooth = unstack(smooth)
    smooth = [[smooth[x][y] * active[x][y] for y in range(EY)] for x in range(EX)]
    for x in range(EX):
        for y in range(EY):
            smooth_ref[x, y] = smooth[x][y]
    for ref, face in zip(send, pack_all(smooth)):
        ref[...] = face


def stiff_apply(groups, lh_ref, ll_ref):
    whole = stack(groups)
    head = whole.astype(BF16)
    tail = (whole - head.astype(F32)).astype(BF16)
    rows = whole.shape[0]
    both = jnp.dot(jnp.concatenate([head, tail], axis=0), lh_ref[...], preferred_element_type=F32)
    low = jnp.dot(head, ll_ref[...], preferred_element_type=F32)
    return unstack(both[:rows] + (both[rows:] + low))


def image_kernel(count, *refs):
    basis_ref, smooth_ref, coef_ref, mask_ref, ids_ref, got_ref, lh_ref, ll_ref = refs[:8]
    face_refs, mask_refs = refs[8:12], refs[12:16]
    precond_ref, image_ref, row_ref = refs[16:]
    coef, active = columns(coef_ref), columns(mask_ref)
    solved = got_ref[...]
    lane = lane_ids(1, count)
    weight_z = hat_z()
    field = [[jnp.zeros((EZ, NODES), F32) for _ in range(EY)] for _ in range(EX)]
    for a in range(2):
        for b in range(2):
            along = jnp.zeros((EZ, NODES), F32)
            for level in range(CGZ):
                hit = jnp.where(lane == ids_ref[0, 0, a, b, level], solved, 0.0)
                along = along + weight_z[level] * jnp.sum(hit, axis=1, keepdims=True)
            for x in range(EX):
                for y in range(EY):
                    field[x][y] = field[x][y] + along * (hat_x(x, a) * hat_y(y, b))
    smooth = load_groups(smooth_ref)
    precond = [
        [smooth[x][y] + active[x][y] * field[x][y] for y in range(EY)] for x in range(EX)
    ]
    stiff = stiff_apply(precond, lh_ref, ll_ref)
    inside = own_neighbors(precond)
    outside = unpack_all([ref[...] for ref in face_refs])
    open_faces = unpack_all([ref[8:16, :] for ref in mask_refs])
    counts = face_count(EZ)
    dots = [jnp.zeros((EZ, NODES), F32) for _ in range(KV + 1)]
    for x in range(EX):
        for y in range(EY):
            across = outside[x][y] + open_faces[x][y] * field[x][y]
            image = active[x][y] * (
                coef[x][y] * stiff[x][y]
                + PENALTY * (counts * precond[x][y] - (inside[x][y] + across))
            )
            precond_ref[x, y] = precond[x][y]
            image_ref[x, y] = image
            for v in range(KV):
                dots[v] = dots[v] + basis_ref[v, x, y] * image
            dots[KV] = dots[KV] + image * image
    values = [all_sum(d) for d in dots]
    basis = [load_groups(basis_ref, v) for v in range(KV)]
    for v in range(KV):
        for u in range(v, KV):
            total = jnp.zeros((EZ, NODES), F32)
            for x in range(EX):
                for y in range(EY):
                    total = total + basis[v][x][y] * basis[u][x][y]
            values.append(all_sum(total))
    row = jnp.zeros((1, LANES), F32)
    row_lane = lane_ids(1, LANES)
    for position, value in enumerate(values):
        row = jnp.where(row_lane == position, value, row)
    row_ref[...] = row


def finish_kernel(total_points, basis_ref, image_ref, got_ref, next_ref, hessen_ref):
    sums = got_ref[...] / total_points
    lane = lane_ids(1, LANES)

    def pick(position):
        return jnp.sum(jnp.where(lane == position, sums, 0.0), axis=1, keepdims=True)

    proj = [pick(v) for v in range(KV)]
    square = pick(KV)
    position = KV + 1
    quad = jnp.zeros((1, 1), F32)
    for v in range(KV):
        for u in range(v, KV):
            factor = 1.0 if u == v else 2.0
            quad = quad + factor * proj[v] * proj[u] * pick(position)
            position += 1
    dot = functools.reduce(jnp.add, [p * p for p in proj])
    beta = jnp.sqrt(square - 2.0 * dot + quad + EPSILON)
    for x in range(EX):
        for y in range(EY):
            residual = image_ref[x, y]
            for v in range(KV):
                residual = residual - proj[v] * basis_ref[v, x, y]
            next_ref[x, y] = residual / beta
    for v, value in enumerate(proj + [beta]):
        hessen_ref[v] = jnp.sum(value)


def levels_of(half):
    found = []
    for level in range(CGZ):
        for point in range(half * HALF * (PTS - 1), (half * HALF + HALF - 1) * (PTS - 1) + PTS):
            if abs(point * (CGZ - 1) / (EZ * (PTS - 1)) - level) < 1.0 + 1e-3:
                found.append(level)
                break
    return found


def lane_sums(x):
    return lax.dot_general(
        jnp.ones((8, LANES), F32),
        x,
        (((1,), (1,)), ((), ())),
        precision=HIGHEST,
        preferred_element_type=F32,
    )


def fold(acc):
    return jnp.sum(acc, axis=0, keepdims=True)


def pieces_of(half):
    for x in range(EX):
        for y in range(EY):
            for c in range(NODES // LANES):
                yield x, y, slice(half * HALF, half * HALF + HALF), slice(c * LANES, (c + 1) * LANES)


def products(left, right, halves, out_row):
    accs = {}
    for half in halves:
        lefts, rights = left(half), right(half)
        for piece in pieces_of(half):
            own = {v: load(*piece) for v, load in lefts.items()}
            other = own if rights is None else {w: load(*piece) for w, load in rights.items()}
            for v, first in own.items():
                for w, second in other.items():
                    if rights is None and w < v:
                        continue
                    term = first * second
                    accs[v, w] = accs[v, w] + term if (v, w) in accs else term
    for (v, w), acc in accs.items():
        out_row(v, w, fold(acc))


def fields_kernel(scale, basis_ref, coef_ref, mask_ref, *refs):
    mask_refs, (xy_ref, z_ref) = refs[:4], refs[4:6]
    early_ref, field_ref, wall_ref, rows_ref = refs[6:]
    coef, active = columns(coef_ref), columns(mask_ref)
    wide = [[jnp.broadcast_to(active[x][y], (EZ, NODES)) for y in range(EY)] for x in range(EX)]
    inside, outside = own_neighbors(wide), unpack_all([ref[8:16, :] for ref in mask_refs])
    counts = face_count(EZ)
    halves = range(EZ // HALF)
    levels = [levels_of(half) for half in halves]
    for x in range(EX):
        for y in range(EY):
            wall = active[x][y] * PENALTY * (counts - (inside[x][y] + outside[x][y]))
            wall_ref[x, y] = wall
            weight = active[x][y] * coef[x][y]
            for half in halves:
                rows = slice(half * HALF, half * HALF + HALF)
                for ab in range(4):
                    at = (ab * EX + x) * EY + y
                    plain = xy_ref[at : at + 1, :]
                    first = weight[rows] * xy_ref[XY + at : XY + at + 1, :] + wall[rows] * plain
                    second = weight[rows] * plain
                    for level in levels[half]:
                        tall = slice(level * EZ + half * HALF, level * EZ + half * HALF + HALF)
                        stiff = slice((CGZ + level) * EZ + half * HALF, (CGZ + level) * EZ + half * HALF + HALF)
                        field_ref[ab * CGZ + level, x, y, rows, :] = (
                            z_ref[tall, :] * first + z_ref[stiff, :] * second
                        )
    rows_ref[...] = jnp.zeros_like(rows_ref)

    def fields(ab):
        def at(half):
            return {
                ab * CGZ + level: (lambda x, y, r, c, v=ab * CGZ + level: field_ref[v, x, y, r, c])
                for level in levels[half]
            }

        return at

    def vectors(half):
        return {v: (lambda x, y, r, c, v=v: basis_ref[v, x, y, r, c]) for v in range(KV)}

    def put(row, value):
        rows_ref[row : row + 1, :] = value

    position = {}
    for v in range(KV):
        for u in range(v, KV):
            position[v, u] = len(position)
    products(vectors, lambda half: None, halves, lambda v, u, s: put(96 + position[v, u], s))
    for ab in range(4):
        products(vectors, fields(ab), halves, lambda v, w, s: put(v * VERTS + w, s))
        products(fields(ab), lambda half: None, halves, lambda v, w, s: put(LANES + v * VERTS + w, s))
        for other in range(ab + 1, 4):
            products(fields(ab), fields(other), halves, lambda v, w, s: put(LANES + v * VERTS + w, s))
    for level in range(CGZ):
        sums = [[None] * EY for _ in range(EX)]
        for x in range(EX):
            for y in range(EY):
                sums[x][y] = fold(basis_ref[KV - 1, x, y] * z_ref[level * EZ : (level + 1) * EZ, :])
        for ab in range(4):
            total = jnp.zeros((1, NODES), F32)
            for x in range(EX):
                for y in range(EY):
                    at = (ab * EX + x) * EY + y
                    total = total + sums[x][y] * xy_ref[at : at + 1, :]
            parts = [total[:, c : c + LANES] for c in range(0, NODES, LANES)]
            put(64 + ab * CGZ + level, functools.reduce(jnp.add, parts) * scale)
    early_ref[...] = lane_sums(rows_ref[...])


def base_kernel(rows, peers, *refs):
    basis_ref, smooth_ref, coef_ref, mask_ref, ids_ref, inverse_ref, lh_ref, ll_ref = refs[:8]
    face_refs, early_ref, field_ref = refs[8:12], refs[12], refs[13]
    base_ref, send_ref, rows_ref = refs[14:]
    coef, active = columns(coef_ref), columns(mask_ref)
    smooth = load_groups(smooth_ref)
    stiff = stiff_apply(smooth, lh_ref, ll_ref)
    inside = own_neighbors(smooth)
    outside = unpack_all([ref[...] for ref in face_refs])
    counts = face_count(EZ)
    for x in range(EX):
        for y in range(EY):
            base_ref[x, y] = active[x][y] * (
                coef[x][y] * stiff[x][y]
                + PENALTY * (counts * smooth[x][y] - (inside[x][y] + outside[x][y]))
            )
    rows_ref[...] = jnp.zeros_like(rows_ref)
    halves = range(EZ // HALF)

    def base(half):
        return {KV: (lambda x, y, r, c: base_ref[x, y, r, c])}

    def vectors(half):
        found = {v: (lambda x, y, r, c, v=v: basis_ref[v, x, y, r, c]) for v in range(KV)}
        found.update(base(half))
        return found

    def fields(part):
        def at(half):
            return {
                v: (lambda x, y, r, c, v=v: field_ref[v, x, y, r, c])
                for v in range(part * 8, part * 8 + 8)
                if v % CGZ in levels_of(half)
            }

        return at

    def put(row, value):
        rows_ref[row : row + 1, :] = value

    products(base, vectors, halves, lambda v, w, s: put(w, s))
    for part in range(VERTS // 8):
        products(base, fields(part), halves, lambda v, w, s: put(VERTS + w, s))
    late = lane_sums(rows_ref[...])
    lane, row = lane_ids(8, LANES), row_ids(8, LANES)
    early = early_ref[...]
    tile = early[:, :LANES]
    for a in range(2):
        for b in range(2):
            for level in range(CGZ):
                at = 80 + (a * 2 + b) * CGZ + level
                tile = jnp.where(lane == at, ids_ref[0, 0, a, b, level].astype(F32), tile)
    tile = jnp.where(row == 1, early[:, LANES : 2 * LANES], tile)
    tile = jnp.where(row == 2, early[:, 2 * LANES :], tile)
    tile = jnp.where(row == 3, late, tile)
    first = lax.axis_index("by") * rows
    for r in range(rows):
        tile = jnp.where(row == 4 + r, inverse_ref[pl.ds(first + r, 1), :], tile)
    for peer in range(peers):
        send_ref[8 * peer : 8 * peer + 8, :] = tile


def close_kernel(total_points, rows, peers, *refs):
    basis_ref, smooth_ref, base_ref, wall_ref, coef_ref, mask_ref, ids_ref = refs[:7]
    xy_ref, z_ref, got_ref, precond_ref, next_ref, hessen_ref = refs[7:]
    lane, row = lane_ids(peers, LANES), row_ids(peers, LANES)

    def got(r):
        return got_ref[pl.ds(r, peers, stride=8), :]

    sums, late = got(0), got(3)
    number = lane.astype(F32)
    hits = [number == sums[:, 80 + v : 81 + v] for v in range(VERTS)]
    coarse = jnp.zeros((peers, LANES), F32)
    for v in range(VERTS):
        coarse = coarse + jnp.where(hits[v], sums[:, 64 + v : 65 + v], 0.0)
    coarse = fold(coarse)
    solved = jnp.zeros((peers, LANES), F32)
    for r in range(rows):
        part = jnp.where(lane == row * rows + r, coarse, 0.0)
        solved = solved + jnp.sum(part, axis=1, keepdims=True) * got(4 + r)
    solved = fold(solved)
    spread = jnp.zeros((peers, LANES), F32)
    wide = [jnp.zeros((peers, LANES), F32) for _ in range(2)]
    for v in range(VERTS):
        value = jnp.sum(jnp.where(hits[v], solved, 0.0), axis=1, keepdims=True)
        spread = jnp.where(lane % VERTS == v, value, spread)
        part = v * VERTS // LANES
        wide[part] = jnp.where(lane // VERTS == v - part * 8, value, wide[part])
    upper = [lane % VERTS > lane // VERTS + part * 8 for part in range(2)]
    twice = [jnp.where(u, 2.0, 1.0) for u in upper]
    quad = (got(1) * wide[0] * twice[0] + got(2) * wide[1] * twice[1]) * spread
    linear = fold(sums * spread)
    late_sum = fold(late)
    in_g = jnp.logical_and(lane >= VERTS, lane < 2 * VERTS)
    square = quad + jnp.where(in_g, 2.0 * late * spread, 0.0) + jnp.where(lane == KV, late, 0.0)
    square = jnp.sum(fold(square), axis=1, keepdims=True) / total_points
    line = lane_ids(1, LANES)
    proj = []
    for v in range(KV):
        term = jnp.where(line // VERTS == v, linear, 0.0) + jnp.where(line == v, late_sum, 0.0)
        proj.append(jnp.sum(term, axis=1, keepdims=True) / total_points)
    pair = jnp.zeros((1, LANES), F32)
    position = 96
    for v in range(KV):
        for u in range(v, KV):
            factor = 1.0 if u == v else 2.0
            pair = jnp.where(line == position, factor * proj[v] * proj[u], pair)
            position += 1
    gram = jnp.sum(pair * fold(sums), axis=1, keepdims=True) / total_points
    dot = functools.reduce(jnp.add, [p * p for p in proj])
    beta = jnp.sqrt(square - 2.0 * dot + gram + EPSILON)
    coef, active = columns(coef_ref), columns(mask_ref)
    along, bent = [], []
    for a in range(2):
        for b in range(2):
            plain = jnp.zeros((EZ, NODES), F32)
            stiff = jnp.zeros((EZ, NODES), F32)
            for level in range(CGZ):
                hit = jnp.where(line == ids_ref[0, 0, a, b, level], solved, 0.0)
                value = jnp.sum(hit, axis=1, keepdims=True)
                plain = plain + value * z_ref[level * EZ : (level + 1) * EZ, :]
                stiff = stiff + value * z_ref[(CGZ + level) * EZ : (CGZ + level + 1) * EZ, :]
            along.append(plain)
            bent.append(stiff)
    for x in range(EX):
        for y in range(EY):
            field = jnp.zeros((EZ, NODES), F32)
            image = jnp.zeros((EZ, NODES), F32)
            for ab in range(4):
                at = (ab * EX + x) * EY + y
                plain = xy_ref[at : at + 1, :]
                field = field + along[ab] * plain
                image = image + (along[ab] * xy_ref[XY + at : XY + at + 1, :] + bent[ab] * plain)
            precond_ref[x, y] = smooth_ref[x, y] + active[x][y] * field
            residual = (
                base_ref[x, y] + (active[x][y] * coef[x][y]) * image + wall_ref[x, y] * field
            )
            for v in range(KV):
                residual = residual - proj[v] * basis_ref[v, x, y]
            next_ref[x, y] = residual / beta
    for v, value in enumerate(proj + [beta]):
        hessen_ref[v] = jnp.sum(value)


def spec(kind=pltpu.VMEM):
    return pl.BlockSpec(memory_space=kind)


def call(kernel, outs, in_specs, args, out_specs=None, scratch=()):
    return pl.pallas_call(
        kernel,
        out_shape=[jax.ShapeDtypeStruct(shape, dtype) for shape, dtype in outs],
        in_specs=in_specs,
        out_specs=out_specs or [spec() for _ in outs],
        scratch_shapes=scratch,
        cost_estimate=pl.CostEstimate(flops=1000000, bytes_accessed=1000000, transcendentals=0),
    )(*args)


def exchange(sends):
    out = []
    for (axis, up), send in zip((("bx", True), ("bx", False), ("by", True), ("by", False)), sends):
        size = lax.axis_size(axis)
        ring = [(i, (i + 1) % size) for i in range(size)]
        if not up:
            ring = [(j, i) for i, j in ring]
        out.append(lax.ppermute(send, axis, ring))
    return out


def smooth_part(basis, coef, modes, eigen, mask, sends):
    halo = exchange(sends)
    square = ((NODES, NODES), BF16)
    tables = call(
        tables_kernel,
        [square] * 4 + [((2 * XY, NODES), F32), ((2 * CGZ * EZ, NODES), F32)],
        [spec()] * 2,
        (modes, eigen),
    )
    smooth, *sends = call(
        smooth_kernel,
        [FIELD] + [((8, 256), F32)] * 4,
        [spec()] * 10,
        (basis, coef, mask, eigen, tables[0], tables[1], *halo),
    )
    return halo, tables, smooth, exchange(sends)


FIELD = ((EX, EY, EZ, NODES), F32)
SENDS = [((16, 256), F32)] * 4


def one_exchange(basis, coef, modes, eigen, mask, vertex_ids, coarse_inverse):
    peers = lax.axis_size("bx") * lax.axis_size("by")
    rows = coarse_inverse.shape[1] // peers
    points = EX * EY * EZ * NODES
    sends = call(faces_kernel, SENDS, [spec()] * 2, (basis, mask))
    halo, tables, smooth, faces = smooth_part(basis, coef, modes, eigen, mask, sends)
    early, fields, wall = call(
        functools.partial(fields_kernel, 1.0 / math.sqrt(points)),
        [((8, 3 * LANES), F32), ((VERTS,) + FIELD[0], F32), FIELD],
        [spec()] * 9,
        (basis, coef, mask, *halo, tables[4], tables[5]),
        scratch=[pltpu.VMEM((3 * LANES, LANES), F32)],
    )
    base, row = call(
        functools.partial(base_kernel, rows, peers),
        [FIELD, ((8 * peers, LANES), F32)],
        [spec()] * 4 + [spec(pltpu.SMEM)] + [spec()] * 9,
        (basis, smooth, coef, mask, vertex_ids, coarse_inverse, *tables[2:4], *faces, early, fields),
        scratch=[pltpu.VMEM((LANES, LANES), F32)],
    )
    got = lax.all_to_all(row, ("bx", "by"), 0, 0, tiled=True)
    return call(
        functools.partial(close_kernel, float(points * peers), rows, peers),
        [FIELD, FIELD, ((KV + 1,), F32)],
        [spec()] * 6 + [spec(pltpu.SMEM)] + [spec()] * 3,
        (basis, smooth, base, wall, coef, mask, vertex_ids, tables[4], tables[5], got),
        out_specs=[spec(), spec(), spec(pltpu.SMEM)],
    )


def two_exchanges(basis, coef, modes, eigen, mask, vertex_ids, coarse_inverse):
    peers = lax.axis_size("bx") * lax.axis_size("by")
    count = coarse_inverse.shape[1]
    points = EX * EY * EZ * NODES
    row, *sends = call(
        functools.partial(start_kernel, 1.0 / math.sqrt(points), count),
        [((1, count), F32)] + SENDS,
        [spec()] * 2 + [spec(pltpu.SMEM)],
        (basis, mask, vertex_ids),
    )
    coarse = lax.psum(row, ("bx", "by"))
    solved = jnp.dot(coarse_inverse, coarse[0], precision=HIGHEST)
    solved = lax.all_gather(solved, "bx", axis=0, tiled=True)[None]
    halo, tables, smooth, faces = smooth_part(basis, coef, modes, eigen, mask, sends)
    precond, image, row = call(
        functools.partial(image_kernel, count),
        [FIELD, FIELD, ((1, LANES), F32)],
        [spec()] * 4 + [spec(pltpu.SMEM)] + [spec()] * 11,
        (basis, smooth, coef, mask, vertex_ids, solved, tables[2], tables[3], *faces, *halo),
    )
    row = lax.psum(row, ("bx", "by"))
    next_vector, hessen = call(
        functools.partial(finish_kernel, float(points * peers)),
        [FIELD, ((KV + 1,), F32)],
        [spec()] * 3,
        (basis, image, row),
        out_specs=[spec(), spec(pltpu.SMEM)],
    )
    return precond, next_vector, hessen


def body(basis, coef, modes, eigen, mask, vertex_ids, coarse_inverse):
    assert coef.shape == (EX, EY, EZ) and basis.shape[0] == KV
    peers = lax.axis_size("bx") * lax.axis_size("by")
    count = coarse_inverse.shape[1]
    small = count == LANES and count == 4 * peers
    steps = one_exchange if small else two_exchanges
    return tuple(steps(basis, coef, modes, eigen, mask, vertex_ids, coarse_inverse))


def solution(mesh):
    placed = (
        P(None, "bx", "by", None, None),
        P("bx", "by", None),
        P(),
        P(),
        P("bx", "by", None),
        P("bx", "by", None, None, None),
        P("bx", None),
    )
    return jax.shard_map(
        body,
        mesh=mesh,
        in_specs=placed,
        out_specs=(P("bx", "by", None, None), P("bx", "by", None, None), P()),
        check_vma=False,
    )
```

```python
import functools
import math

import jax
import jax.numpy as jnp
from jax import lax
from jax.experimental import pallas as pl
from jax.experimental.pallas import tpu as pltpu
from jax.sharding import PartitionSpec as P


PTS = 8
NODES = PTS**3
KV = 4
CGZ = 4
EX = 2
EY = 2
EZ = 16
LANES = 128
VMEM_BYTES = 12 << 20
HALF = 8
XY = 4 * EX * EY
VERTS = 4 * CGZ

PENALTY = 2.0
SHIFT = 1.0
EPSILON = 1e-06
HIGHEST = lax.Precision.HIGHEST
F32 = jnp.float32
BF16 = jnp.bfloat16


def lane_ids(rows, lanes):
    return lax.broadcasted_iota(jnp.int32, (rows, lanes), 1)


def row_ids(rows, lanes):
    return lax.broadcasted_iota(jnp.int32, (rows, lanes), 0)


def roll_chunks(x, shift):
    shift = shift % LANES
    if shift == 0:
        return x
    pieces = [
        pltpu.roll(x[:, c : c + LANES], shift, 1) for c in range(0, x.shape[1], LANES)
    ]
    return pieces[0] if len(pieces) == 1 else jnp.concatenate(pieces, axis=1)


def column(row):
    wide = jnp.broadcast_to(row, (EZ, EZ))
    keep = row_ids(EZ, EZ) == lane_ids(EZ, EZ)
    return jnp.sum(jnp.where(keep, wide, jnp.zeros_like(wide)), axis=1, keepdims=True)


def columns(ref):
    return [[column(ref[x, y : y + 1, :].astype(F32)) for y in range(EY)] for x in range(EX)]


def blocks_of(parts):
    return [part[8 * b : 8 * b + 8] for part in parts for b in range(EZ // 8)]


def pack_x(parts, high):
    low_half = lane_ids(8, LANES) < 64
    offset = NODES - LANES if high else 0
    cut = [block[:, offset : offset + LANES] for block in blocks_of(parts)]
    out = []
    for m in range(2):
        even = pltpu.roll(cut[2 * m], 64, 1) if high else cut[2 * m]
        odd = cut[2 * m + 1] if high else pltpu.roll(cut[2 * m + 1], 64, 1)
        out.append(jnp.where(low_half, even, odd))
    return jnp.concatenate(out, axis=1)


def unpack_x(packed, high):
    low_half = lane_ids(8, LANES) < 64
    zero = jnp.zeros((8, LANES), F32)
    groups = []
    for g in range(2):
        rows = []
        for b in (2 * g, 2 * g + 1):
            chunk = packed[:, LANES * (b // 2) : LANES * (b // 2) + LANES]
            if (b % 2 == 0) == high:
                chunk = pltpu.roll(chunk, 64, 1)
            chunk = jnp.where(low_half, zero, chunk) if high else jnp.where(low_half, chunk, zero)
            rows.append(
                jnp.concatenate([zero] * 3 + [chunk] if high else [chunk] + [zero] * 3, axis=1)
            )
        groups.append(jnp.concatenate(rows, axis=0))
    return groups


def pack_y(parts, high):
    slot = lane_ids(8, NODES) // PTS % PTS
    from_slot = PTS - 1 if high else 0
    total = jnp.zeros((8, NODES), F32)
    for b, block in enumerate(blocks_of(parts)):
        total = jnp.where(slot == b, roll_chunks(block, PTS * (b - from_slot)), total)
    lower, upper = total[:, :256], roll_chunks(total[:, 256:], 32)
    return jnp.where(slot[:, :256] < 4, lower, upper)


def unpack_y(packed, high):
    slot = lane_ids(8, LANES) // PTS % PTS
    to_slot = PTS - 1 if high else 0
    zero = jnp.zeros((8, LANES), F32)
    groups = []
    for g in range(2):
        rows = []
        for b in (2 * g, 2 * g + 1):
            chunks = []
            for c in range(4):
                source = packed[:, LANES * (c % 2) : LANES * (c % 2) + LANES]
                moved = roll_chunks(source, PTS * (to_slot - b - 4 * (c // 2)))
                chunks.append(jnp.where(slot == to_slot, moved, zero))
            rows.append(jnp.concatenate(chunks, axis=1))
        groups.append(jnp.concatenate(rows, axis=0))
    return groups


def pack_all(groups):
    return [
        pack_x([groups[EX - 1][y] for y in range(EY)], True),
        pack_x([groups[0][y] for y in range(EY)], False),
        pack_y([groups[x][EY - 1] for x in range(EX)], True),
        pack_y([groups[x][0] for x in range(EX)], False),
    ]


def unpack_all(packed):
    left = unpack_x(packed[0], False)
    right = unpack_x(packed[1], True)
    front = unpack_y(packed[2], False)
    back = unpack_y(packed[3], True)
    out = [[None] * EY for _ in range(EX)]
    for x in range(EX):
        for y in range(EY):
            terms = []
            if x == 0:
                terms.append(left[y])
            if x == EX - 1:
                terms.append(right[y])
            if y == 0:
                terms.append(front[x])
            if y == EY - 1:
                terms.append(back[x])
            out[x][y] = functools.reduce(jnp.add, terms)
    return out


def own_neighbors(groups):
    lane = lane_ids(EZ, NODES)
    row = row_ids(EZ, NODES)
    j, k = lane // PTS % PTS, lane % PTS
    low_z = jnp.logical_and(k == 0, row > 0)
    high_z = jnp.logical_and(k == PTS - 1, row < EZ - 1)
    zero = jnp.zeros((EZ, NODES), F32)
    pad = jnp.zeros((EZ, NODES - LANES), F32)
    low_half = lane_ids(EZ, LANES) < 64
    zero_chunk = jnp.zeros((EZ, LANES), F32)
    out = [[None] * EY for _ in range(EX)]
    for x in range(EX):
        for y in range(EY):
            here = groups[x][y]
            total = jnp.where(low_z, roll_chunks(pltpu.roll(here, 1, 0), 1 - PTS), zero)
            total = total + jnp.where(
                high_z, roll_chunks(pltpu.roll(here, EZ - 1, 0), PTS - 1), zero
            )
            if y > 0:
                moved = roll_chunks(groups[x][y - 1], PTS - PTS * PTS)
                total = total + jnp.where(j == 0, moved, zero)
            if y < EY - 1:
                moved = roll_chunks(groups[x][y + 1], PTS * PTS - PTS)
                total = total + jnp.where(j == PTS - 1, moved, zero)
            if x > 0:
                chunk = pltpu.roll(groups[x - 1][y][:, NODES - LANES :], 64, 1)
                chunk = jnp.where(low_half, chunk, zero_chunk)
                total = total + jnp.concatenate([chunk, pad], axis=1)
            if x < EX - 1:
                chunk = pltpu.roll(groups[x + 1][y][:, :LANES], 64, 1)
                chunk = jnp.where(low_half, zero_chunk, chunk)
                total = total + jnp.concatenate([pad, chunk], axis=1)
            out[x][y] = total
    return out


def load_groups(ref, *lead):
    return [[ref[(*lead, x, y)] for y in range(EY)] for x in range(EX)]


def stack(groups):
    return jnp.concatenate([groups[x][y] for x in range(EX) for y in range(EY)], axis=0)


def unstack(whole):
    return [
        [whole[(x * EY + y) * EZ : (x * EY + y + 1) * EZ] for y in range(EY)] for x in range(EX)
    ]


def hat(place, span, levels, level):
    place = place.astype(F32) / float(span) * float(levels - 1)
    return jnp.maximum(0.0, 1.0 - jnp.abs(place - float(level)))


def hat_z():
    lane, row = lane_ids(EZ, NODES), row_ids(EZ, NODES)
    place = row * (PTS - 1) + lane % PTS
    return [hat(place, EZ * (PTS - 1), CGZ, level) for level in range(CGZ)]


def hat_x(x, a, rows=1):
    place = x * (PTS - 1) + lane_ids(rows, NODES) // (PTS * PTS)
    return hat(place, EX * (PTS - 1), 2, a)


def hat_y(y, b, rows=1):
    place = y * (PTS - 1) + lane_ids(rows, NODES) // PTS % PTS
    return hat(place, EY * (PTS - 1), 2, b)


def face_count(rows):
    lane = lane_ids(rows, NODES)
    total = jnp.zeros((rows, NODES), F32)
    for part in (lane // (PTS * PTS), lane // PTS % PTS, lane % PTS):
        edge = jnp.logical_or(part == 0, part == PTS - 1)
        total = total + jnp.where(edge, 1.0, 0.0)
    return total


def all_sum(x):
    return jnp.sum(jnp.sum(x, axis=0, keepdims=True), axis=1, keepdims=True)


def coarse_row(current, ids_ref, count, scale):
    weight_z = hat_z()
    lane = lane_ids(1, count)
    out = jnp.zeros((1, count), F32)
    for level in range(CGZ):
        sums = [[None] * EY for _ in range(EX)]
        for x in range(EX):
            for y in range(EY):
                sums[x][y] = jnp.sum(current[x][y] * weight_z[level], axis=0, keepdims=True)
        for a in range(2):
            for b in range(2):
                total = jnp.zeros((1, NODES), F32)
                for x in range(EX):
                    for y in range(EY):
                        total = total + sums[x][y] * (hat_x(x, a) * hat_y(y, b))
                value = jnp.sum(total, axis=1, keepdims=True) * scale
                out = out + jnp.where(lane == ids_ref[0, 0, a, b, level], value, 0.0)
    return out


def send_faces(basis_ref, mask_ref, outs):
    current = load_groups(basis_ref, KV - 1)
    active = columns(mask_ref)
    wide = [[jnp.broadcast_to(active[x][y], (EZ, NODES)) for y in range(EY)] for x in range(EX)]
    for ref, face, part in zip(outs, pack_all(current), pack_all(wide)):
        ref[0:8, :] = face
        ref[8:16, :] = part
    return current


def start_kernel(scale, count, basis_ref, mask_ref, ids_ref, row_ref, *outs):
    current = send_faces(basis_ref, mask_ref, outs)
    row_ref[...] = coarse_row(current, ids_ref, count, scale)


def load_kernel(*refs):
    basis_hbm, mask_hbm, coef_hbm, modes_hbm, eigen_hbm, ids_hbm, inverse_hbm = refs[:7]
    basis_ref, mask_ref, coef_ref, modes_ref, eigen_ref, inverse_ref, ids_ref = refs[7:14]
    outs, ids_scratch, sems = refs[14:18], refs[18], refs[19]
    older = slice(0, KV - 1)
    copies = [
        pltpu.make_async_copy(source, target, sems.at[n])
        for n, (source, target) in enumerate(
            (
                (basis_hbm.at[KV - 1], basis_ref.at[KV - 1]),
                (mask_hbm, mask_ref),
                (basis_hbm.at[older], basis_ref.at[older]),
                (coef_hbm, coef_ref),
                (modes_hbm, modes_ref),
                (eigen_hbm, eigen_ref),
                (ids_hbm, ids_scratch),
                (inverse_hbm, inverse_ref),
            )
        )
    ]
    for copy in copies:
        copy.start()
    copies[0].wait()
    copies[1].wait()
    send_faces(basis_ref, mask_ref, outs)
    for copy in copies[2:]:
        copy.wait()
    lane = lane_ids(1, LANES)
    row = jnp.zeros((1, LANES), F32)
    for a in range(2):
        for b in range(2):
            short = ids_scratch[0, 0, a, b : b + 1, :].astype(F32)
            for level in range(CGZ):
                row = jnp.where(lane == 80 + (a * 2 + b) * CGZ + level, short[:, level : level + 1], row)
    ids_ref[...] = jnp.broadcast_to(row, (8, LANES))


def expand(matrix, stride):
    pick = (lane_ids(PTS, NODES) // stride % PTS == row_ids(PTS, NODES)).astype(F32)
    return jnp.dot(matrix, pick, precision=HIGHEST, preferred_element_type=F32)


def tables_kernel(modes_ref, eigen_ref, sb_ref, st_ref, lh_ref, ll_ref, xy_ref, z_ref):
    strides = (PTS * PTS, PTS, 1)
    eye = (row_ids(PTS, PTS) == lane_ids(PTS, PTS)).astype(F32)
    straight, turned, stiff, unit = [], [], [], []
    for d in range(3):
        mode = modes_ref[d]
        turn = lax.dot_general(
            mode, eye, (((0,), (0,)), ((), ())), precision=HIGHEST, preferred_element_type=F32
        )
        scaled = mode * eigen_ref[d : d + 1, :]
        one = jnp.dot(scaled, turn, precision=HIGHEST, preferred_element_type=F32)
        straight.append(expand(mode, strides[d]))
        turned.append(expand(turn, strides[d]))
        stiff.append(expand(one, strides[d]))
        unit.append(expand(eye, strides[d]))
    for i in range(PTS):
        for j in range(PTS):
            rows = slice((i * PTS + j) * PTS, (i * PTS + j + 1) * PTS)
            pair = straight[0][i : i + 1] * straight[1][j : j + 1]
            sb_ref[rows, :] = (pair * straight[2]).astype(BF16)
            pair = turned[0][i : i + 1] * turned[1][j : j + 1]
            st_ref[rows, :] = (pair * turned[2]).astype(BF16)
            both = unit[0][i : i + 1] * unit[1][j : j + 1]
            either = stiff[0][i : i + 1] * unit[1][j : j + 1] + unit[0][i : i + 1] * stiff[1][j : j + 1]
            full = either * unit[2] + both * stiff[2]
            head = full.astype(BF16)
            lh_ref[rows, :] = head
            ll_ref[rows, :] = (full - head.astype(F32)).astype(BF16)
    point, row = lane_ids(PTS, PTS), row_ids(PTS, PTS)
    pairs = (row < 2 * EX, row // 2 * (PTS - 1) + point, row % 2)
    short = jnp.maximum(
        0.0,
        1.0 - jnp.abs(pairs[1].astype(F32) / float(EX * (PTS - 1)) - pairs[2].astype(F32)),
    )
    short = jnp.where(pairs[0], short, 0.0)
    stiff_x = jnp.dot(short, stiff[0], precision=HIGHEST, preferred_element_type=F32)
    stiff_y = jnp.dot(short, stiff[1], precision=HIGHEST, preferred_element_type=F32)
    for a in range(2):
        for b in range(2):
            for x in range(EX):
                for y in range(EY):
                    at = ((a * 2 + b) * EX + x) * EY + y
                    plain_x, plain_y = hat_x(x, a), hat_y(y, b)
                    xy_ref[at : at + 1, :] = plain_x * plain_y
                    xy_ref[XY + at : XY + at + 1, :] = (
                        stiff_x[x * 2 + a : x * 2 + a + 1] * plain_y
                        + plain_x * stiff_y[y * 2 + b : y * 2 + b + 1]
                    )
    place = row_ids(EZ, PTS) * (PTS - 1) + lane_ids(EZ, PTS)
    for level, weight in enumerate(hat_z()):
        z_ref[level * EZ : (level + 1) * EZ, :] = weight
        tall = hat(place, EZ * (PTS - 1), CGZ, level)
        z_ref[(CGZ + level) * EZ : (CGZ + level + 1) * EZ, :] = jnp.dot(
            tall, stiff[2], precision=HIGHEST, preferred_element_type=F32
        )


def spectrum_row(eigen_ref):
    out = jnp.zeros((1, NODES), F32)
    for d, stride in enumerate((PTS * PTS, PTS, 1)):
        pick = (lane_ids(PTS, NODES) // stride % PTS == row_ids(PTS, NODES)).astype(F32)
        out = out + jnp.dot(
            eigen_ref[d : d + 1, :], pick, precision=HIGHEST, preferred_element_type=F32
        )
    return out


def smooth_kernel(*refs):
    basis_ref, coef_ref, mask_ref, eigen_ref, sb_ref, st_ref = refs[:6]
    halo = [ref[0:8, :] for ref in refs[6:10]]
    smooth_ref, *send = refs[10:]
    current = load_groups(basis_ref, KV - 1)
    inside, outside = own_neighbors(current), unpack_all(halo)
    coef, active = columns(coef_ref), columns(mask_ref)
    extended = [
        [current[x][y] + (inside[x][y] + outside[x][y]) for y in range(EY)] for x in range(EX)
    ]
    modal = jnp.dot(stack(extended).astype(BF16), sb_ref[...], preferred_element_type=F32)
    modal = unstack(modal)
    spectrum = spectrum_row(eigen_ref)
    modal = [
        [modal[x][y] / (coef[x][y] * spectrum + SHIFT) for y in range(EY)] for x in range(EX)
    ]
    smooth = jnp.dot(stack(modal).astype(BF16), st_ref[...], preferred_element_type=F32)
    smooth = unstack(smooth)
    smooth = [[smooth[x][y] * active[x][y] for y in range(EY)] for x in range(EX)]
    for x in range(EX):
        for y in range(EY):
            smooth_ref[x, y] = smooth[x][y]
    for ref, face in zip(send, pack_all(smooth)):
        ref[...] = face


def stiff_apply(groups, lh_ref, ll_ref):
    whole = stack(groups)
    head = whole.astype(BF16)
    tail = (whole - head.astype(F32)).astype(BF16)
    rows = whole.shape[0]
    both = jnp.dot(jnp.concatenate([head, tail], axis=0), lh_ref[...], preferred_element_type=F32)
    low = jnp.dot(head, ll_ref[...], preferred_element_type=F32)
    return unstack(both[:rows] + (both[rows:] + low))


def image_kernel(count, *refs):
    basis_ref, smooth_ref, coef_ref, mask_ref, ids_ref, got_ref, lh_ref, ll_ref = refs[:8]
    face_refs, mask_refs = refs[8:12], refs[12:16]
    precond_ref, image_ref, row_ref = refs[16:]
    coef, active = columns(coef_ref), columns(mask_ref)
    solved = got_ref[...]
    lane = lane_ids(1, count)
    weight_z = hat_z()
    field = [[jnp.zeros((EZ, NODES), F32) for _ in range(EY)] for _ in range(EX)]
    for a in range(2):
        for b in range(2):
            along = jnp.zeros((EZ, NODES), F32)
            for level in range(CGZ):
                hit = jnp.where(lane == ids_ref[0, 0, a, b, level], solved, 0.0)
                along = along + weight_z[level] * jnp.sum(hit, axis=1, keepdims=True)
            for x in range(EX):
                for y in range(EY):
                    field[x][y] = field[x][y] + along * (hat_x(x, a) * hat_y(y, b))
    smooth = load_groups(smooth_ref)
    precond = [
        [smooth[x][y] + active[x][y] * field[x][y] for y in range(EY)] for x in range(EX)
    ]
    stiff = stiff_apply(precond, lh_ref, ll_ref)
    inside = own_neighbors(precond)
    outside = unpack_all([ref[...] for ref in face_refs])
    open_faces = unpack_all([ref[8:16, :] for ref in mask_refs])
    counts = face_count(EZ)
    dots = [jnp.zeros((EZ, NODES), F32) for _ in range(KV + 1)]
    for x in range(EX):
        for y in range(EY):
            across = outside[x][y] + open_faces[x][y] * field[x][y]
            image = active[x][y] * (
                coef[x][y] * stiff[x][y]
                + PENALTY * (counts * precond[x][y] - (inside[x][y] + across))
            )
            precond_ref[x, y] = precond[x][y]
            image_ref[x, y] = image
            for v in range(KV):
                dots[v] = dots[v] + basis_ref[v, x, y] * image
            dots[KV] = dots[KV] + image * image
    values = [all_sum(d) for d in dots]
    basis = [load_groups(basis_ref, v) for v in range(KV)]
    for v in range(KV):
        for u in range(v, KV):
            total = jnp.zeros((EZ, NODES), F32)
            for x in range(EX):
                for y in range(EY):
                    total = total + basis[v][x][y] * basis[u][x][y]
            values.append(all_sum(total))
    row = jnp.zeros((1, LANES), F32)
    row_lane = lane_ids(1, LANES)
    for position, value in enumerate(values):
        row = jnp.where(row_lane == position, value, row)
    row_ref[...] = row


def finish_kernel(total_points, basis_ref, image_ref, got_ref, next_ref, hessen_ref):
    sums = got_ref[...] / total_points
    lane = lane_ids(1, LANES)

    def pick(position):
        return jnp.sum(jnp.where(lane == position, sums, 0.0), axis=1, keepdims=True)

    proj = [pick(v) for v in range(KV)]
    square = pick(KV)
    position = KV + 1
    quad = jnp.zeros((1, 1), F32)
    for v in range(KV):
        for u in range(v, KV):
            factor = 1.0 if u == v else 2.0
            quad = quad + factor * proj[v] * proj[u] * pick(position)
            position += 1
    dot = functools.reduce(jnp.add, [p * p for p in proj])
    beta = jnp.sqrt(square - 2.0 * dot + quad + EPSILON)
    for x in range(EX):
        for y in range(EY):
            residual = image_ref[x, y]
            for v in range(KV):
                residual = residual - proj[v] * basis_ref[v, x, y]
            next_ref[x, y] = residual / beta
    for v, value in enumerate(proj + [beta]):
        hessen_ref[v] = jnp.sum(value)


def levels_of(half):
    found = []
    for level in range(CGZ):
        for point in range(half * HALF * (PTS - 1), (half * HALF + HALF - 1) * (PTS - 1) + PTS):
            if abs(point * (CGZ - 1) / (EZ * (PTS - 1)) - level) < 1.0 + 1e-3:
                found.append(level)
                break
    return found


def lane_sums(x):
    return lax.dot_general(
        jnp.ones((8, LANES), F32),
        x,
        (((1,), (1,)), ((), ())),
        precision=HIGHEST,
        preferred_element_type=F32,
    )


def fold(acc):
    return jnp.sum(acc, axis=0, keepdims=True)


def pieces_of(half):
    for x in range(EX):
        for y in range(EY):
            for c in range(NODES // LANES):
                yield x, y, slice(half * HALF, half * HALF + HALF), slice(c * LANES, (c + 1) * LANES)


def products(left, right, halves, out_row):
    accs = {}
    for half in halves:
        lefts, rights = left(half), right(half)
        for piece in pieces_of(half):
            own = {v: load(*piece) for v, load in lefts.items()}
            other = own if rights is None else {w: load(*piece) for w, load in rights.items()}
            for v, first in own.items():
                for w, second in other.items():
                    if rights is None and w < v:
                        continue
                    term = first * second
                    accs[v, w] = accs[v, w] + term if (v, w) in accs else term
    for (v, w), acc in accs.items():
        out_row(v, w, fold(acc))


def fields_kernel(scale, basis_ref, coef_ref, mask_ref, *refs):
    mask_refs, (xy_ref, z_ref) = refs[:4], refs[4:6]
    early_ref, field_ref, wall_ref, rows_ref = refs[6:]
    coef, active = columns(coef_ref), columns(mask_ref)
    wide = [[jnp.broadcast_to(active[x][y], (EZ, NODES)) for y in range(EY)] for x in range(EX)]
    inside, outside = own_neighbors(wide), unpack_all([ref[8:16, :] for ref in mask_refs])
    counts = face_count(EZ)
    halves = range(EZ // HALF)
    levels = [levels_of(half) for half in halves]
    for x in range(EX):
        for y in range(EY):
            wall = active[x][y] * PENALTY * (counts - (inside[x][y] + outside[x][y]))
            wall_ref[x, y] = wall
            weight = active[x][y] * coef[x][y]
            for half in halves:
                rows = slice(half * HALF, half * HALF + HALF)
                for ab in range(4):
                    at = (ab * EX + x) * EY + y
                    plain = xy_ref[at : at + 1, :]
                    first = weight[rows] * xy_ref[XY + at : XY + at + 1, :] + wall[rows] * plain
                    second = weight[rows] * plain
                    for level in levels[half]:
                        tall = slice(level * EZ + half * HALF, level * EZ + half * HALF + HALF)
                        stiff = slice((CGZ + level) * EZ + half * HALF, (CGZ + level) * EZ + half * HALF + HALF)
                        field_ref[ab * CGZ + level, x, y, rows, :] = (
                            z_ref[tall, :] * first + z_ref[stiff, :] * second
                        )
    rows_ref[...] = jnp.zeros_like(rows_ref)

    def fields(ab):
        def at(half):
            return {
                ab * CGZ + level: (lambda x, y, r, c, v=ab * CGZ + level: field_ref[v, x, y, r, c])
                for level in levels[half]
            }

        return at

    def vectors(half):
        return {v: (lambda x, y, r, c, v=v: basis_ref[v, x, y, r, c]) for v in range(KV)}

    def put(row, value):
        rows_ref[row : row + 1, :] = value

    position = {}
    for v in range(KV):
        for u in range(v, KV):
            position[v, u] = len(position)
    products(vectors, lambda half: None, halves, lambda v, u, s: put(96 + position[v, u], s))
    for ab in range(4):
        products(vectors, fields(ab), halves, lambda v, w, s: put(v * VERTS + w, s))
        products(fields(ab), lambda half: None, halves, lambda v, w, s: put(LANES + v * VERTS + w, s))
        for other in range(ab + 1, 4):
            products(fields(ab), fields(other), halves, lambda v, w, s: put(LANES + v * VERTS + w, s))
    for level in range(CGZ):
        sums = [[None] * EY for _ in range(EX)]
        for x in range(EX):
            for y in range(EY):
                sums[x][y] = fold(basis_ref[KV - 1, x, y] * z_ref[level * EZ : (level + 1) * EZ, :])
        for ab in range(4):
            total = jnp.zeros((1, NODES), F32)
            for x in range(EX):
                for y in range(EY):
                    at = (ab * EX + x) * EY + y
                    total = total + sums[x][y] * xy_ref[at : at + 1, :]
            parts = [total[:, c : c + LANES] for c in range(0, NODES, LANES)]
            put(64 + ab * CGZ + level, functools.reduce(jnp.add, parts) * scale)
    early_ref[...] = lane_sums(rows_ref[...])


def base_kernel(rows, peers, *refs):
    basis_ref, smooth_ref, coef_ref, mask_ref, ids_ref, inverse_ref, lh_ref, ll_ref = refs[:8]
    face_refs, early_ref, field_ref = refs[8:12], refs[12], refs[13]
    base_ref, send_ref, rows_ref = refs[14:]
    coef, active = columns(coef_ref), columns(mask_ref)
    smooth = load_groups(smooth_ref)
    stiff = stiff_apply(smooth, lh_ref, ll_ref)
    inside = own_neighbors(smooth)
    outside = unpack_all([ref[...] for ref in face_refs])
    counts = face_count(EZ)
    for x in range(EX):
        for y in range(EY):
            base_ref[x, y] = active[x][y] * (
                coef[x][y] * stiff[x][y]
                + PENALTY * (counts * smooth[x][y] - (inside[x][y] + outside[x][y]))
            )
    rows_ref[...] = jnp.zeros_like(rows_ref)
    halves = range(EZ // HALF)

    def base(half):
        return {KV: (lambda x, y, r, c: base_ref[x, y, r, c])}

    def vectors(half):
        found = {v: (lambda x, y, r, c, v=v: basis_ref[v, x, y, r, c]) for v in range(KV)}
        found.update(base(half))
        return found

    def fields(part):
        def at(half):
            return {
                v: (lambda x, y, r, c, v=v: field_ref[v, x, y, r, c])
                for v in range(part * 8, part * 8 + 8)
                if v % CGZ in levels_of(half)
            }

        return at

    def put(row, value):
        rows_ref[row : row + 1, :] = value

    products(base, vectors, halves, lambda v, w, s: put(w, s))
    for part in range(VERTS // 8):
        products(base, fields(part), halves, lambda v, w, s: put(VERTS + w, s))
    late = lane_sums(rows_ref[...])
    lane, row = lane_ids(8, LANES), row_ids(8, LANES)
    early = early_ref[...]
    tile = early[:, :LANES]
    tile = jnp.where(jnp.logical_and(lane >= 80, lane < 80 + VERTS), ids_ref[...], tile)
    tile = jnp.where(row == 1, early[:, LANES : 2 * LANES], tile)
    tile = jnp.where(row == 2, early[:, 2 * LANES :], tile)
    tile = jnp.where(row == 3, late, tile)
    first = lax.axis_index("by") * rows
    for r in range(rows):
        tile = jnp.where(row == 4 + r, inverse_ref[pl.ds(first + r, 1), :], tile)
    for peer in range(peers):
        send_ref[8 * peer : 8 * peer + 8, :] = tile


def close_kernel(total_points, rows, peers, *refs):
    basis_ref, smooth_ref, base_ref, wall_ref, coef_ref, mask_ref, ids_ref = refs[:7]
    xy_ref, z_ref, got_ref, precond_ref, next_ref, hessen_ref = refs[7:]
    lane, row = lane_ids(peers, LANES), row_ids(peers, LANES)

    def got(r):
        return got_ref[pl.ds(r, peers, stride=8), :]

    sums, late = got(0), got(3)
    number = lane.astype(F32)
    hits = [number == sums[:, 80 + v : 81 + v] for v in range(VERTS)]
    coarse = jnp.zeros((peers, LANES), F32)
    for v in range(VERTS):
        coarse = coarse + jnp.where(hits[v], sums[:, 64 + v : 65 + v], 0.0)
    coarse = fold(coarse)
    solved = jnp.zeros((peers, LANES), F32)
    for r in range(rows):
        part = jnp.where(lane == row * rows + r, coarse, 0.0)
        solved = solved + jnp.sum(part, axis=1, keepdims=True) * got(4 + r)
    solved = fold(solved)
    spread = jnp.zeros((peers, LANES), F32)
    wide = [jnp.zeros((peers, LANES), F32) for _ in range(2)]
    for v in range(VERTS):
        value = jnp.sum(jnp.where(hits[v], solved, 0.0), axis=1, keepdims=True)
        spread = jnp.where(lane % VERTS == v, value, spread)
        part = v * VERTS // LANES
        wide[part] = jnp.where(lane // VERTS == v - part * 8, value, wide[part])
    upper = [lane % VERTS > lane // VERTS + part * 8 for part in range(2)]
    twice = [jnp.where(u, 2.0, 1.0) for u in upper]
    quad = (got(1) * wide[0] * twice[0] + got(2) * wide[1] * twice[1]) * spread
    linear = fold(sums * spread)
    late_sum = fold(late)
    in_g = jnp.logical_and(lane >= VERTS, lane < 2 * VERTS)
    square = quad + jnp.where(in_g, 2.0 * late * spread, 0.0) + jnp.where(lane == KV, late, 0.0)
    square = jnp.sum(fold(square), axis=1, keepdims=True) / total_points
    line = lane_ids(1, LANES)
    proj = []
    for v in range(KV):
        term = jnp.where(line // VERTS == v, linear, 0.0) + jnp.where(line == v, late_sum, 0.0)
        proj.append(jnp.sum(term, axis=1, keepdims=True) / total_points)
    pair = jnp.zeros((1, LANES), F32)
    position = 96
    for v in range(KV):
        for u in range(v, KV):
            factor = 1.0 if u == v else 2.0
            pair = jnp.where(line == position, factor * proj[v] * proj[u], pair)
            position += 1
    gram = jnp.sum(pair * fold(sums), axis=1, keepdims=True) / total_points
    dot = functools.reduce(jnp.add, [p * p for p in proj])
    beta = jnp.sqrt(square - 2.0 * dot + gram + EPSILON)
    coef, active = columns(coef_ref), columns(mask_ref)
    along, bent = [], []
    for a in range(2):
        for b in range(2):
            plain = jnp.zeros((EZ, NODES), F32)
            stiff = jnp.zeros((EZ, NODES), F32)
            for level in range(CGZ):
                at = 80 + (a * 2 + b) * CGZ + level
                hit = jnp.where(line.astype(F32) == ids_ref[0:1, at : at + 1], solved, 0.0)
                value = jnp.sum(hit, axis=1, keepdims=True)
                plain = plain + value * z_ref[level * EZ : (level + 1) * EZ, :]
                stiff = stiff + value * z_ref[(CGZ + level) * EZ : (CGZ + level + 1) * EZ, :]
            along.append(plain)
            bent.append(stiff)
    for x in range(EX):
        for y in range(EY):
            field = jnp.zeros((EZ, NODES), F32)
            image = jnp.zeros((EZ, NODES), F32)
            for ab in range(4):
                at = (ab * EX + x) * EY + y
                plain = xy_ref[at : at + 1, :]
                field = field + along[ab] * plain
                image = image + (along[ab] * xy_ref[XY + at : XY + at + 1, :] + bent[ab] * plain)
            precond_ref[x, y] = smooth_ref[x, y] + active[x][y] * field
            residual = (
                base_ref[x, y] + (active[x][y] * coef[x][y]) * image + wall_ref[x, y] * field
            )
            for v in range(KV):
                residual = residual - proj[v] * basis_ref[v, x, y]
            next_ref[x, y] = residual / beta
    for v, value in enumerate(proj + [beta]):
        hessen_ref[v] = jnp.sum(value)


def spec(kind=pltpu.VMEM):
    return pl.BlockSpec(memory_space=kind)


def call(kernel, outs, in_specs, args, out_specs=None, scratch=(), cost=1000000):
    return pl.pallas_call(
        kernel,
        out_shape=[jax.ShapeDtypeStruct(shape, dtype) for shape, dtype in outs],
        in_specs=in_specs,
        out_specs=out_specs or [spec() for _ in outs],
        scratch_shapes=scratch,
        compiler_params=pltpu.CompilerParams(vmem_limit_bytes=VMEM_BYTES),
        cost_estimate=pl.CostEstimate(flops=cost, bytes_accessed=cost, transcendentals=0),
    )(*args)


def exchange(sends):
    out = [None] * 4
    for place in (3, 2, 1, 0):
        axis = "bx" if place < 2 else "by"
        size = lax.axis_size(axis)
        ring = [(i, (i + 1) % size) for i in range(size)]
        if place % 2:
            ring = [(j, i) for i, j in ring]
        out[place] = lax.ppermute(sends[place], axis, ring)
    return out


def smooth_part(basis, coef, modes, eigen, mask, sends):
    halo = exchange(sends)
    square = ((NODES, NODES), BF16)
    tables = call(
        tables_kernel,
        [square] * 4 + [((2 * XY, NODES), F32), ((2 * CGZ * EZ, NODES), F32)],
        [spec()] * 2,
        (modes, eigen),
    )
    smooth, *sends = call(
        smooth_kernel,
        [FIELD] + [((8, 256), F32)] * 4,
        [spec()] * 10,
        (basis, coef, mask, eigen, tables[0], tables[1], *halo),
    )
    return halo, tables, smooth, exchange(sends)


FIELD = ((EX, EY, EZ, NODES), F32)
SENDS = [((16, 256), F32)] * 4


def one_exchange(basis, coef, modes, eigen, mask, vertex_ids, coarse_inverse):
    peers = lax.axis_size("bx") * lax.axis_size("by")
    rows = coarse_inverse.shape[1] // peers
    points = EX * EY * EZ * NODES
    *local, a, b, c, d = call(
        load_kernel,
        [(x.shape, x.dtype) for x in (basis, mask, coef, modes, eigen, coarse_inverse)]
        + [((8, LANES), F32)]
        + SENDS,
        [spec(pltpu.HBM)] * 7,
        tuple(pltpu.with_memory_space_constraint(x, pltpu.HBM) for x in (basis, mask, coef, modes, eigen, vertex_ids, coarse_inverse)),
        scratch=[pltpu.VMEM(vertex_ids.shape, vertex_ids.dtype), pltpu.SemaphoreType.DMA((8,))],
    )
    basis, mask, coef, modes, eigen, coarse_inverse, ids = local
    halo, tables, smooth, faces = smooth_part(basis, coef, modes, eigen, mask, (a, b, c, d))
    early, fields, wall = call(
        functools.partial(fields_kernel, 1.0 / math.sqrt(points)),
        [((8, 3 * LANES), F32), ((VERTS,) + FIELD[0], F32), FIELD],
        [spec()] * 9,
        (basis, coef, mask, *halo, tables[4], tables[5]),
        scratch=[pltpu.VMEM((3 * LANES, LANES), F32)],
    )
    base, row = call(
        functools.partial(base_kernel, rows, peers),
        [FIELD, ((8 * peers, LANES), F32)],
        [spec()] * 14,
        (basis, smooth, coef, mask, ids, coarse_inverse, *tables[2:4], *faces, early, fields),
        scratch=[pltpu.VMEM((LANES, LANES), F32)],
    )
    got = lax.all_to_all(row, ("bx", "by"), 0, 0, tiled=True)
    return call(
        functools.partial(close_kernel, float(points * peers), rows, peers),
        [FIELD, FIELD, ((KV + 1,), F32)],
        [spec()] * 10,
        (basis, smooth, base, wall, coef, mask, ids, tables[4], tables[5], got),
        out_specs=[spec(), spec(), spec(pltpu.SMEM)],
    )


def two_exchanges(basis, coef, modes, eigen, mask, vertex_ids, coarse_inverse):
    peers = lax.axis_size("bx") * lax.axis_size("by")
    count = coarse_inverse.shape[1]
    points = EX * EY * EZ * NODES
    row, *sends = call(
        functools.partial(start_kernel, 1.0 / math.sqrt(points), count),
        [((1, count), F32)] + SENDS,
        [spec()] * 2 + [spec(pltpu.SMEM)],
        (basis, mask, vertex_ids),
    )
    coarse = lax.psum(row, ("bx", "by"))
    solved = jnp.dot(coarse_inverse, coarse[0], precision=HIGHEST)
    solved = lax.all_gather(solved, "bx", axis=0, tiled=True)[None]
    halo, tables, smooth, faces = smooth_part(basis, coef, modes, eigen, mask, sends)
    precond, image, row = call(
        functools.partial(image_kernel, count),
        [FIELD, FIELD, ((1, LANES), F32)],
        [spec()] * 4 + [spec(pltpu.SMEM)] + [spec()] * 11,
        (basis, smooth, coef, mask, vertex_ids, solved, tables[2], tables[3], *faces, *halo),
    )
    row = lax.psum(row, ("bx", "by"))
    next_vector, hessen = call(
        functools.partial(finish_kernel, float(points * peers)),
        [FIELD, ((KV + 1,), F32)],
        [spec()] * 3,
        (basis, image, row),
        out_specs=[spec(), spec(pltpu.SMEM)],
    )
    return precond, next_vector, hessen


def body(basis, coef, modes, eigen, mask, vertex_ids, coarse_inverse):
    assert coef.shape == (EX, EY, EZ) and basis.shape[0] == KV
    peers = lax.axis_size("bx") * lax.axis_size("by")
    count = coarse_inverse.shape[1]
    small = count == LANES and count == 4 * peers
    steps = one_exchange if small else two_exchanges
    return tuple(steps(basis, coef, modes, eigen, mask, vertex_ids, coarse_inverse))


def solution(mesh):
    placed = (
        P(None, "bx", "by", None, None),
        P("bx", "by", None),
        P(),
        P(),
        P("bx", "by", None),
        P("bx", "by", None, None, None),
        P("bx", None),
    )
    return jax.shard_map(
        body,
        mesh=mesh,
        in_specs=placed,
        out_specs=(P("bx", "by", None, None), P("bx", "by", None, None), P()),
        check_vma=False,
    )
```

```python
import functools
import math

import jax
import jax.numpy as jnp
from jax import lax
from jax.experimental import pallas as pl
from jax.experimental.pallas import tpu as pltpu
from jax.sharding import PartitionSpec as P


PTS = 8
NODES = PTS**3
KV = 4
CGZ = 4
EX = 2
EY = 2
EZ = 16
LANES = 128
VMEM_BYTES = 12 << 20
HALF = 8
XY = 4 * EX * EY
AT_G, AT_FAR, AT_R, AT_SUM, AT_GRAM, AT_ID = 64, 80, 88, 96, 112, 122
SENT = 2
VERTS = 4 * CGZ

PENALTY = 2.0
SHIFT = 1.0
EPSILON = 1e-06
HIGHEST = lax.Precision.HIGHEST
F32 = jnp.float32
BF16 = jnp.bfloat16


def lane_ids(rows, lanes):
    return lax.broadcasted_iota(jnp.int32, (rows, lanes), 1)


def row_ids(rows, lanes):
    return lax.broadcasted_iota(jnp.int32, (rows, lanes), 0)


def roll_chunks(x, shift):
    shift = shift % LANES
    if shift == 0:
        return x
    pieces = [
        pltpu.roll(x[:, c : c + LANES], shift, 1) for c in range(0, x.shape[1], LANES)
    ]
    return pieces[0] if len(pieces) == 1 else jnp.concatenate(pieces, axis=1)


def column(row):
    wide = jnp.broadcast_to(row, (EZ, EZ))
    keep = row_ids(EZ, EZ) == lane_ids(EZ, EZ)
    return jnp.sum(jnp.where(keep, wide, jnp.zeros_like(wide)), axis=1, keepdims=True)


def columns(ref):
    return [[column(ref[x, y : y + 1, :].astype(F32)) for y in range(EY)] for x in range(EX)]


def blocks_of(parts):
    return [part[8 * b : 8 * b + 8] for part in parts for b in range(EZ // 8)]


def pack_x(parts, high):
    low_half = lane_ids(8, LANES) < 64
    offset = NODES - LANES if high else 0
    cut = [block[:, offset : offset + LANES] for block in blocks_of(parts)]
    out = []
    for m in range(2):
        even = pltpu.roll(cut[2 * m], 64, 1) if high else cut[2 * m]
        odd = cut[2 * m + 1] if high else pltpu.roll(cut[2 * m + 1], 64, 1)
        out.append(jnp.where(low_half, even, odd))
    return jnp.concatenate(out, axis=1)


def unpack_x(packed, high):
    low_half = lane_ids(8, LANES) < 64
    zero = jnp.zeros((8, LANES), F32)
    groups = []
    for g in range(2):
        rows = []
        for b in (2 * g, 2 * g + 1):
            chunk = packed[:, LANES * (b // 2) : LANES * (b // 2) + LANES]
            if (b % 2 == 0) == high:
                chunk = pltpu.roll(chunk, 64, 1)
            chunk = jnp.where(low_half, zero, chunk) if high else jnp.where(low_half, chunk, zero)
            rows.append(
                jnp.concatenate([zero] * 3 + [chunk] if high else [chunk] + [zero] * 3, axis=1)
            )
        groups.append(jnp.concatenate(rows, axis=0))
    return groups


def pack_y(parts, high):
    slot = lane_ids(8, NODES) // PTS % PTS
    from_slot = PTS - 1 if high else 0
    total = jnp.zeros((8, NODES), F32)
    for b, block in enumerate(blocks_of(parts)):
        total = jnp.where(slot == b, roll_chunks(block, PTS * (b - from_slot)), total)
    lower, upper = total[:, :256], roll_chunks(total[:, 256:], 32)
    return jnp.where(slot[:, :256] < 4, lower, upper)


def unpack_y(packed, high):
    slot = lane_ids(8, LANES) // PTS % PTS
    to_slot = PTS - 1 if high else 0
    zero = jnp.zeros((8, LANES), F32)
    groups = []
    for g in range(2):
        rows = []
        for b in (2 * g, 2 * g + 1):
            chunks = []
            for c in range(4):
                source = packed[:, LANES * (c % 2) : LANES * (c % 2) + LANES]
                moved = roll_chunks(source, PTS * (to_slot - b - 4 * (c // 2)))
                chunks.append(jnp.where(slot == to_slot, moved, zero))
            rows.append(jnp.concatenate(chunks, axis=1))
        groups.append(jnp.concatenate(rows, axis=0))
    return groups


def pack_all(groups):
    right = pack_x([groups[EX - 1][y] for y in range(EY)], True)
    left = pack_x([groups[0][y] for y in range(EY)], False)
    back = pack_y([groups[x][EY - 1] for x in range(EX)], True)
    front = pack_y([groups[x][0] for x in range(EX)], False)
    return [*pair_up(right, left, "bx"), *pair_up(back, front, "by")]


def pair_up(first, second, axis):
    place = jnp.full(first.shape, lax.rem(lax.axis_index(axis), 2), jnp.int32)
    even = place == 0
    return jnp.where(even, first, second), jnp.where(even, second, first)


def unpack_all(packed):
    right, left = pair_up(packed[0], packed[1], "bx")
    back, front = pair_up(packed[2], packed[3], "by")
    packed = (left, right, front, back)
    left = unpack_x(packed[0], False)
    right = unpack_x(packed[1], True)
    front = unpack_y(packed[2], False)
    back = unpack_y(packed[3], True)
    out = [[None] * EY for _ in range(EX)]
    for x in range(EX):
        for y in range(EY):
            terms = []
            if x == 0:
                terms.append(left[y])
            if x == EX - 1:
                terms.append(right[y])
            if y == 0:
                terms.append(front[x])
            if y == EY - 1:
                terms.append(back[x])
            out[x][y] = functools.reduce(jnp.add, terms)
    return out


def own_neighbors(groups):
    lane = lane_ids(EZ, NODES)
    row = row_ids(EZ, NODES)
    j, k = lane // PTS % PTS, lane % PTS
    low_z = jnp.logical_and(k == 0, row > 0)
    high_z = jnp.logical_and(k == PTS - 1, row < EZ - 1)
    zero = jnp.zeros((EZ, NODES), F32)
    pad = jnp.zeros((EZ, NODES - LANES), F32)
    low_half = lane_ids(EZ, LANES) < 64
    zero_chunk = jnp.zeros((EZ, LANES), F32)
    out = [[None] * EY for _ in range(EX)]
    for x in range(EX):
        for y in range(EY):
            here = groups[x][y]
            total = jnp.where(low_z, roll_chunks(pltpu.roll(here, 1, 0), 1 - PTS), zero)
            total = total + jnp.where(
                high_z, roll_chunks(pltpu.roll(here, EZ - 1, 0), PTS - 1), zero
            )
            if y > 0:
                moved = roll_chunks(groups[x][y - 1], PTS - PTS * PTS)
                total = total + jnp.where(j == 0, moved, zero)
            if y < EY - 1:
                moved = roll_chunks(groups[x][y + 1], PTS * PTS - PTS)
                total = total + jnp.where(j == PTS - 1, moved, zero)
            if x > 0:
                chunk = pltpu.roll(groups[x - 1][y][:, NODES - LANES :], 64, 1)
                chunk = jnp.where(low_half, chunk, zero_chunk)
                total = total + jnp.concatenate([chunk, pad], axis=1)
            if x < EX - 1:
                chunk = pltpu.roll(groups[x + 1][y][:, :LANES], 64, 1)
                chunk = jnp.where(low_half, zero_chunk, chunk)
                total = total + jnp.concatenate([pad, chunk], axis=1)
            out[x][y] = total
    return out


def load_groups(ref, *lead):
    return [[ref[(*lead, x, y)] for y in range(EY)] for x in range(EX)]


def stack(groups):
    return jnp.concatenate([groups[x][y] for x in range(EX) for y in range(EY)], axis=0)


def unstack(whole):
    return [
        [whole[(x * EY + y) * EZ : (x * EY + y + 1) * EZ] for y in range(EY)] for x in range(EX)
    ]


def hat(place, span, levels, level):
    place = place.astype(F32) / float(span) * float(levels - 1)
    return jnp.maximum(0.0, 1.0 - jnp.abs(place - float(level)))


def hat_z():
    lane, row = lane_ids(EZ, NODES), row_ids(EZ, NODES)
    place = row * (PTS - 1) + lane % PTS
    return [hat(place, EZ * (PTS - 1), CGZ, level) for level in range(CGZ)]


def hat_x(x, a, rows=1):
    place = x * (PTS - 1) + lane_ids(rows, NODES) // (PTS * PTS)
    return hat(place, EX * (PTS - 1), 2, a)


def hat_y(y, b, rows=1):
    place = y * (PTS - 1) + lane_ids(rows, NODES) // PTS % PTS
    return hat(place, EY * (PTS - 1), 2, b)


def face_count(rows):
    lane = lane_ids(rows, NODES)
    total = jnp.zeros((rows, NODES), F32)
    for part in (lane // (PTS * PTS), lane // PTS % PTS, lane % PTS):
        edge = jnp.logical_or(part == 0, part == PTS - 1)
        total = total + jnp.where(edge, 1.0, 0.0)
    return total


def all_sum(x):
    return jnp.sum(jnp.sum(x, axis=0, keepdims=True), axis=1, keepdims=True)


def coarse_row(current, ids_ref, count, scale):
    weight_z = hat_z()
    lane = lane_ids(1, count)
    out = jnp.zeros((1, count), F32)
    for level in range(CGZ):
        sums = [[None] * EY for _ in range(EX)]
        for x in range(EX):
            for y in range(EY):
                sums[x][y] = jnp.sum(current[x][y] * weight_z[level], axis=0, keepdims=True)
        for a in range(2):
            for b in range(2):
                total = jnp.zeros((1, NODES), F32)
                for x in range(EX):
                    for y in range(EY):
                        total = total + sums[x][y] * (hat_x(x, a) * hat_y(y, b))
                value = jnp.sum(total, axis=1, keepdims=True) * scale
                out = out + jnp.where(lane == ids_ref[0, 0, a, b, level], value, 0.0)
    return out


def send_faces(basis_ref, mask_ref, outs):
    current = load_groups(basis_ref, KV - 1)
    active = columns(mask_ref)
    wide = [[jnp.broadcast_to(active[x][y], (EZ, NODES)) for y in range(EY)] for x in range(EX)]
    for ref, face, part in zip(outs, pack_all(current), pack_all(wide)):
        ref[0:8, :] = face
        ref[8:16, :] = part
    return current


def start_kernel(scale, count, basis_ref, mask_ref, ids_ref, row_ref, *outs):
    current = send_faces(basis_ref, mask_ref, outs)
    row_ref[...] = coarse_row(current, ids_ref, count, scale)


def load_kernel(*refs):
    basis_hbm, mask_hbm, coef_hbm, modes_hbm, eigen_hbm, ids_hbm, inverse_hbm = refs[:7]
    basis_ref, mask_ref, coef_ref, modes_ref, eigen_ref, inverse_ref, ids_ref = refs[7:14]
    outs, ids_scratch, sems = refs[14:18], refs[18], refs[19]
    older = slice(0, KV - 1)
    copies = [
        pltpu.make_async_copy(source, target, sems.at[n])
        for n, (source, target) in enumerate(
            (
                (basis_hbm.at[KV - 1], basis_ref.at[KV - 1]),
                (mask_hbm, mask_ref),
                (basis_hbm.at[older], basis_ref.at[older]),
                (coef_hbm, coef_ref),
                (modes_hbm, modes_ref),
                (eigen_hbm, eigen_ref),
                (ids_hbm, ids_scratch),
                (inverse_hbm, inverse_ref),
            )
        )
    ]
    for copy in copies:
        copy.start()
    copies[0].wait()
    copies[1].wait()
    send_faces(basis_ref, mask_ref, outs)
    for copy in copies[2:]:
        copy.wait()
    lane = lane_ids(1, LANES)
    row = jnp.zeros((1, LANES), F32)
    short = ids_scratch[0, 0, 0, 0:1, :].astype(F32)
    for level in range(CGZ):
        row = jnp.where(lane == AT_ID + level, short[:, level : level + 1], row)
    ids_ref[...] = jnp.broadcast_to(row, (8, LANES))


def expand(matrix, stride):
    pick = (lane_ids(PTS, NODES) // stride % PTS == row_ids(PTS, NODES)).astype(F32)
    return jnp.dot(matrix, pick, precision=HIGHEST, preferred_element_type=F32)


def tables_kernel(modes_ref, eigen_ref, sb_ref, lh_ref, ll_ref, lx_ref, xy_ref, z_ref):
    strides = (PTS * PTS, PTS, 1)
    eye = (row_ids(PTS, PTS) == lane_ids(PTS, PTS)).astype(F32)
    straight, stiff, unit = [], [], []
    for d in range(3):
        mode = modes_ref[d]
        turn = lax.dot_general(
            mode, eye, (((0,), (0,)), ((), ())), precision=HIGHEST, preferred_element_type=F32
        )
        scaled = mode * eigen_ref[d : d + 1, :]
        one = jnp.dot(scaled, turn, precision=HIGHEST, preferred_element_type=F32)
        straight.append(expand(mode, strides[d]))
        stiff.append(expand(one, strides[d]))
        unit.append(expand(eye, strides[d]))
    for i in range(PTS):
        for j in range(PTS):
            rows = slice((i * PTS + j) * PTS, (i * PTS + j + 1) * PTS)
            pair = straight[0][i : i + 1] * straight[1][j : j + 1]
            sb_ref[rows, :] = (pair * straight[2]).astype(BF16)
    lane = lane_ids(8, LANES)
    for half in range(2):
        for j in range(PTS):
            rows = slice((half * PTS + j) * PTS, (half * PTS + j + 1) * PTS)
            full = stiff[1][j : j + 1, :LANES] * unit[2][:, :LANES]
            full = full + unit[1][j : j + 1, :LANES] * stiff[2][:, :LANES]
            full = jnp.where(lane // 64 == half, full, 0.0)
            head = full.astype(BF16)
            lh_ref[rows, :] = head
            ll_ref[rows, :] = (full - head.astype(F32)).astype(BF16)
    low_half = lane_ids(1, NODES) % LANES < 64
    for c in range(NODES // LANES):
        even, odd = stiff[0][2 * c : 2 * c + 1], stiff[0][2 * c + 1 : 2 * c + 2]
        lx_ref[c : c + 1, :] = jnp.where(low_half, even, odd)
        lx_ref[c + 4 : c + 5, :] = jnp.where(low_half, odd, even)
    point, row = lane_ids(PTS, PTS), row_ids(PTS, PTS)
    pairs = (row < 2 * EX, row // 2 * (PTS - 1) + point, row % 2)
    short = jnp.maximum(
        0.0,
        1.0 - jnp.abs(pairs[1].astype(F32) / float(EX * (PTS - 1)) - pairs[2].astype(F32)),
    )
    short = jnp.where(pairs[0], short, 0.0)
    stiff_x = jnp.dot(short, stiff[0], precision=HIGHEST, preferred_element_type=F32)
    stiff_y = jnp.dot(short, stiff[1], precision=HIGHEST, preferred_element_type=F32)
    for a in range(2):
        for b in range(2):
            for x in range(EX):
                for y in range(EY):
                    at = ((a * 2 + b) * EX + x) * EY + y
                    plain_x, plain_y = hat_x(x, a), hat_y(y, b)
                    xy_ref[at : at + 1, :] = plain_x * plain_y
                    xy_ref[XY + at : XY + at + 1, :] = (
                        stiff_x[x * 2 + a : x * 2 + a + 1] * plain_y
                        + plain_x * stiff_y[y * 2 + b : y * 2 + b + 1]
                    )
    place = row_ids(EZ, PTS) * (PTS - 1) + lane_ids(EZ, PTS)
    for level, weight in enumerate(hat_z()):
        z_ref[level * EZ : (level + 1) * EZ, :] = weight
        tall = hat(place, EZ * (PTS - 1), CGZ, level)
        z_ref[(CGZ + level) * EZ : (CGZ + level + 1) * EZ, :] = jnp.dot(
            tall, stiff[2], precision=HIGHEST, preferred_element_type=F32
        )


def spectrum_row(eigen_ref):
    out = jnp.zeros((1, NODES), F32)
    for d, stride in enumerate((PTS * PTS, PTS, 1)):
        pick = (lane_ids(PTS, NODES) // stride % PTS == row_ids(PTS, NODES)).astype(F32)
        out = out + jnp.dot(
            eigen_ref[d : d + 1, :], pick, precision=HIGHEST, preferred_element_type=F32
        )
    return out


def smooth_kernel(*refs):
    basis_ref, coef_ref, mask_ref, eigen_ref, sb_ref = refs[:5]
    halo = [ref[0:8, :] for ref in refs[5:9]]
    smooth_ref, *send = refs[9:]
    current = load_groups(basis_ref, KV - 1)
    inside, outside = own_neighbors(current), unpack_all(halo)
    coef, active = columns(coef_ref), columns(mask_ref)
    extended = [
        [current[x][y] + (inside[x][y] + outside[x][y]) for y in range(EY)] for x in range(EX)
    ]
    modal = jnp.dot(stack(extended).astype(BF16), sb_ref[...], preferred_element_type=F32)
    modal = unstack(modal)
    spectrum = spectrum_row(eigen_ref)
    modal = [
        [modal[x][y] / (coef[x][y] * spectrum + SHIFT) for y in range(EY)] for x in range(EX)
    ]
    smooth = lax.dot_general(
        stack(modal).astype(BF16),
        sb_ref[...],
        (((1,), (1,)), ((), ())),
        preferred_element_type=F32,
    )
    smooth = unstack(smooth)
    smooth = [[smooth[x][y] * active[x][y] for y in range(EY)] for x in range(EX)]
    for x in range(EX):
        for y in range(EY):
            smooth_ref[x, y] = smooth[x][y]
    for ref, face in zip(send, pack_all(smooth)):
        ref[...] = face


def stiff_apply(groups, lh_ref, ll_ref, lx_ref):
    whole = stack(groups)
    chunks = [whole[:, c : c + LANES] for c in range(0, NODES, LANES)]
    tall = jnp.concatenate(chunks, axis=0)
    head = tall.astype(BF16)
    tail = (tall - head.astype(F32)).astype(BF16)
    rows, size = tall.shape[0], whole.shape[0]
    both = jnp.dot(jnp.concatenate([head, tail], axis=0), lh_ref[...], preferred_element_type=F32)
    inner = both[:rows] + (both[rows:] + jnp.dot(head, ll_ref[...], preferred_element_type=F32))
    turned = [pltpu.roll(chunk, 64, 1) for chunk in chunks]
    out = []
    for c in range(len(chunks)):
        lanes = slice(c * LANES, (c + 1) * LANES)
        total = inner[c * size : (c + 1) * size]
        for d in range(len(chunks)):
            total = total + chunks[d] * lx_ref[d : d + 1, lanes]
            total = total + turned[d] * lx_ref[d + 4 : d + 5, lanes]
        out.append(total)
    return unstack(jnp.concatenate(out, axis=1))


def image_kernel(count, *refs):
    basis_ref, smooth_ref, coef_ref, mask_ref, ids_ref, got_ref, lh_ref, ll_ref, lx_ref = refs[:9]
    face_refs, mask_refs = refs[9:13], refs[13:17]
    precond_ref, image_ref, row_ref = refs[17:]
    coef, active = columns(coef_ref), columns(mask_ref)
    solved = got_ref[...]
    lane = lane_ids(1, count)
    weight_z = hat_z()
    field = [[jnp.zeros((EZ, NODES), F32) for _ in range(EY)] for _ in range(EX)]
    for a in range(2):
        for b in range(2):
            along = jnp.zeros((EZ, NODES), F32)
            for level in range(CGZ):
                hit = jnp.where(lane == ids_ref[0, 0, a, b, level], solved, 0.0)
                along = along + weight_z[level] * jnp.sum(hit, axis=1, keepdims=True)
            for x in range(EX):
                for y in range(EY):
                    field[x][y] = field[x][y] + along * (hat_x(x, a) * hat_y(y, b))
    smooth = load_groups(smooth_ref)
    precond = [
        [smooth[x][y] + active[x][y] * field[x][y] for y in range(EY)] for x in range(EX)
    ]
    stiff = stiff_apply(precond, lh_ref, ll_ref, lx_ref)
    inside = own_neighbors(precond)
    outside = unpack_all([ref[...] for ref in face_refs])
    open_faces = unpack_all([ref[8:16, :] for ref in mask_refs])
    counts = face_count(EZ)
    dots = [jnp.zeros((EZ, NODES), F32) for _ in range(KV + 1)]
    for x in range(EX):
        for y in range(EY):
            across = outside[x][y] + open_faces[x][y] * field[x][y]
            image = active[x][y] * (
                coef[x][y] * stiff[x][y]
                + PENALTY * (counts * precond[x][y] - (inside[x][y] + across))
            )
            precond_ref[x, y] = precond[x][y]
            image_ref[x, y] = image
            for v in range(KV):
                dots[v] = dots[v] + basis_ref[v, x, y] * image
            dots[KV] = dots[KV] + image * image
    values = [all_sum(d) for d in dots]
    basis = [load_groups(basis_ref, v) for v in range(KV)]
    for v in range(KV):
        for u in range(v, KV):
            total = jnp.zeros((EZ, NODES), F32)
            for x in range(EX):
                for y in range(EY):
                    total = total + basis[v][x][y] * basis[u][x][y]
            values.append(all_sum(total))
    row = jnp.zeros((1, LANES), F32)
    row_lane = lane_ids(1, LANES)
    for position, value in enumerate(values):
        row = jnp.where(row_lane == position, value, row)
    row_ref[...] = row


def finish_kernel(total_points, basis_ref, image_ref, got_ref, next_ref, hessen_ref):
    sums = got_ref[...] / total_points
    lane = lane_ids(1, LANES)

    def pick(position):
        return jnp.sum(jnp.where(lane == position, sums, 0.0), axis=1, keepdims=True)

    proj = [pick(v) for v in range(KV)]
    square = pick(KV)
    position = KV + 1
    quad = jnp.zeros((1, 1), F32)
    for v in range(KV):
        for u in range(v, KV):
            factor = 1.0 if u == v else 2.0
            quad = quad + factor * proj[v] * proj[u] * pick(position)
            position += 1
    dot = functools.reduce(jnp.add, [p * p for p in proj])
    beta = jnp.sqrt(square - 2.0 * dot + quad + EPSILON)
    for x in range(EX):
        for y in range(EY):
            residual = image_ref[x, y]
            for v in range(KV):
                residual = residual - proj[v] * basis_ref[v, x, y]
            next_ref[x, y] = residual / beta
    for v, value in enumerate(proj + [beta]):
        hessen_ref[v] = jnp.sum(value)


def levels_of(half):
    found = []
    for level in range(CGZ):
        for point in range(half * HALF * (PTS - 1), (half * HALF + HALF - 1) * (PTS - 1) + PTS):
            if abs(point * (CGZ - 1) / (EZ * (PTS - 1)) - level) < 1.0 + 1e-3:
                found.append(level)
                break
    return found


def lane_sums(x):
    return lax.dot_general(
        jnp.ones((8, LANES), F32),
        x,
        (((1,), (1,)), ((), ())),
        precision=HIGHEST,
        preferred_element_type=F32,
    )


def fold(acc):
    return jnp.sum(acc, axis=0, keepdims=True)


def pieces_of(half):
    for x in range(EX):
        for y in range(EY):
            for c in range(NODES // LANES):
                yield x, y, slice(half * HALF, half * HALF + HALF), slice(c * LANES, (c + 1) * LANES)


def products(left, right, halves, out_row):
    accs = {}
    for half in halves:
        lefts, rights = left(half), right(half)
        for piece in pieces_of(half):
            own = {v: load(*piece) for v, load in lefts.items()}
            other = own if rights is None else {w: load(*piece) for w, load in rights.items()}
            for v, first in own.items():
                for w, second in other.items():
                    if rights is None and w < v:
                        continue
                    term = first * second
                    accs[v, w] = accs[v, w] + term if (v, w) in accs else term
    for (v, w), acc in accs.items():
        out_row(v, w, fold(acc))


def fields_kernel(scale, basis_ref, coef_ref, mask_ref, *refs):
    mask_refs, (xy_ref, z_ref) = refs[:4], refs[4:6]
    early_ref, field_ref, wall_ref, rows_ref = refs[6:]
    coef, active = columns(coef_ref), columns(mask_ref)
    wide = [[jnp.broadcast_to(active[x][y], (EZ, NODES)) for y in range(EY)] for x in range(EX)]
    inside, outside = own_neighbors(wide), unpack_all([ref[8:16, :] for ref in mask_refs])
    counts = face_count(EZ)
    halves = range(EZ // HALF)
    levels = [levels_of(half) for half in halves]
    for x in range(EX):
        for y in range(EY):
            wall = active[x][y] * PENALTY * (counts - (inside[x][y] + outside[x][y]))
            wall_ref[x, y] = wall
            weight = active[x][y] * coef[x][y]
            for half in halves:
                rows = slice(half * HALF, half * HALF + HALF)
                for ab in range(4):
                    at = (ab * EX + x) * EY + y
                    plain = xy_ref[at : at + 1, :]
                    first = weight[rows] * xy_ref[XY + at : XY + at + 1, :] + wall[rows] * plain
                    second = weight[rows] * plain
                    for level in levels[half]:
                        tall = slice(level * EZ + half * HALF, level * EZ + half * HALF + HALF)
                        stiff = slice((CGZ + level) * EZ + half * HALF, (CGZ + level) * EZ + half * HALF + HALF)
                        field_ref[ab * CGZ + level, x, y, rows, :] = (
                            z_ref[tall, :] * first + z_ref[stiff, :] * second
                        )
    rows_ref[...] = jnp.zeros_like(rows_ref)

    def fields(ab):
        def at(half):
            return {
                ab * CGZ + level: (lambda x, y, r, c, v=ab * CGZ + level: field_ref[v, x, y, r, c])
                for level in levels[half]
            }

        return at

    def vectors(half):
        return {v: (lambda x, y, r, c, v=v: basis_ref[v, x, y, r, c]) for v in range(KV)}

    def put(row, value):
        rows_ref[row : row + 1, :] = value

    position = {}
    for v in range(KV):
        for u in range(v, KV):
            position[v, u] = len(position)

    def put_field(v, w, value):
        far = (w - v) % VERTS
        if far > VERTS // 2 or (far == VERTS // 2 and v > w):
            v, far = w, VERTS - far
        put(LANES + AT_FAR + v if far == VERTS // 2 else far * VERTS + v, value)

    products(vectors, lambda half: None, halves, lambda v, u, s: put(LANES + AT_GRAM + position[v, u], s))
    for ab in range(4):
        products(vectors, fields(ab), halves, lambda v, w, s: put(LANES + v * VERTS + w, s))
        products(fields(ab), lambda half: None, halves, put_field)
        for other in range(ab + 1, 4):
            products(fields(ab), fields(other), halves, put_field)
    for level in range(CGZ):
        sums = [[None] * EY for _ in range(EX)]
        for x in range(EX):
            for y in range(EY):
                sums[x][y] = fold(basis_ref[KV - 1, x, y] * z_ref[level * EZ : (level + 1) * EZ, :])
        for ab in range(4):
            total = jnp.zeros((1, NODES), F32)
            for x in range(EX):
                for y in range(EY):
                    at = (ab * EX + x) * EY + y
                    total = total + sums[x][y] * xy_ref[at : at + 1, :]
            parts = [total[:, c : c + LANES] for c in range(0, NODES, LANES)]
            put(LANES + AT_SUM + ab * CGZ + level, functools.reduce(jnp.add, parts) * scale)
    early_ref[...] = lane_sums(rows_ref[...])


def base_kernel(rows, peers, *refs):
    basis_ref, smooth_ref, coef_ref, mask_ref, ids_ref, inverse_ref = refs[:6]
    lh_ref, ll_ref, lx_ref = refs[6:9]
    face_refs, early_ref, field_ref = refs[9:13], refs[13], refs[14]
    base_ref, send_ref, rows_ref = refs[15:]
    coef, active = columns(coef_ref), columns(mask_ref)
    smooth = load_groups(smooth_ref)
    stiff = stiff_apply(smooth, lh_ref, ll_ref, lx_ref)
    inside = own_neighbors(smooth)
    outside = unpack_all([ref[...] for ref in face_refs])
    counts = face_count(EZ)
    for x in range(EX):
        for y in range(EY):
            base_ref[x, y] = active[x][y] * (
                coef[x][y] * stiff[x][y]
                + PENALTY * (counts * smooth[x][y] - (inside[x][y] + outside[x][y]))
            )
    rows_ref[...] = jnp.zeros_like(rows_ref)
    halves = range(EZ // HALF)

    def base(half):
        return {KV: (lambda x, y, r, c: base_ref[x, y, r, c])}

    def vectors(half):
        found = {v: (lambda x, y, r, c, v=v: basis_ref[v, x, y, r, c]) for v in range(KV)}
        found.update(base(half))
        return found

    def fields(part):
        def at(half):
            return {
                v: (lambda x, y, r, c, v=v: field_ref[v, x, y, r, c])
                for v in range(part * 8, part * 8 + 8)
                if v % CGZ in levels_of(half)
            }

        return at

    def put(row, value):
        rows_ref[row : row + 1, :] = value

    products(base, vectors, halves, lambda v, w, s: put(AT_R + w, s))
    for part in range(VERTS // 8):
        products(base, fields(part), halves, lambda v, w, s: put(AT_G + w, s))
    late = lane_sums(rows_ref[...])
    early = early_ref[...]
    first = lax.axis_index("by") * rows
    tile = jnp.concatenate(
        [early[0:1, :LANES], early[0:1, LANES:] + late[0:1] + ids_ref[0:1, :]]
        + [inverse_ref[pl.ds(first + r, 1), :] for r in range(rows)],
        axis=0,
    )
    size = SENT + rows
    for peer in range(peers):
        send_ref[size * peer : size * peer + size, :] = tile


def close_kernel(total_points, rows, peers, *refs):
    basis_ref, smooth_ref, base_ref, wall_ref, coef_ref, mask_ref = refs[:6]
    xy_ref, z_ref, got_ref, precond_hbm, next_hbm, hessen_ref = refs[6:12]
    precond_ref, next_ref, sems = refs[12:]
    lane, row = lane_ids(peers, LANES), row_ids(peers, LANES)
    side = lax.axis_size("by")

    def got(r):
        return got_ref[pl.ds(r, peers, stride=SENT + rows), :]

    def along_x(values, step):
        return pltpu.roll(values, (step * side) % peers, 0)

    def along_y(values, step):
        edge = row % side == (0 if step > 0 else side - 1)
        wrapped = pltpu.roll(values, (step * (1 - side)) % peers, 0)
        return jnp.where(edge, wrapped, pltpu.roll(values, step % peers, 0))

    def turn(values, lanes):
        return pltpu.roll(values, (-lanes) % LANES, 1)

    sums = got(1)
    corner = sums + along_x(turn(sums, 2 * CGZ), 1)
    other = turn(sums, CGZ) + along_x(turn(sums, 3 * CGZ), 1)
    corner = corner + along_y(other, 1)
    number = lane.astype(F32)
    hits = [number == sums[:, AT_ID + v : AT_ID + v + 1] for v in range(CGZ)]
    coarse = jnp.zeros((peers, LANES), F32)
    for v in range(CGZ):
        coarse = coarse + jnp.where(hits[v], corner[:, AT_SUM + v : AT_SUM + v + 1], 0.0)
    coarse = fold(coarse)
    solved = jnp.zeros((peers, LANES), F32)
    for r in range(rows):
        part = jnp.where(lane == row * rows + r, coarse, 0.0)
        solved = solved + jnp.sum(part, axis=1, keepdims=True) * got(SENT + r)
    solved = fold(solved)
    near = jnp.zeros((peers, LANES), F32)
    for v in range(CGZ):
        value = jnp.sum(jnp.where(hits[v], solved, 0.0), axis=1, keepdims=True)
        near = jnp.where(lane % CGZ == v, value, near)
    right = along_x(near, -1)
    quarter = lane % VERTS // CGZ
    lower = jnp.where(quarter < 2, near, right)
    spread = jnp.where(quarter % 2 == 0, lower, along_y(lower, -1))
    me = lax.axis_index("bx") * side + lax.axis_index("by")
    own = fold(jnp.where(row == me, spread, 0.0))
    coef, active = columns(coef_ref), columns(mask_ref)
    along, bent = [], []
    for ab in range(4):
        plain = jnp.zeros((EZ, NODES), F32)
        stiff = jnp.zeros((EZ, NODES), F32)
        for level in range(CGZ):
            value = own[:, ab * CGZ + level : ab * CGZ + level + 1]
            plain = plain + value * z_ref[level * EZ : (level + 1) * EZ, :]
            stiff = stiff + value * z_ref[(CGZ + level) * EZ : (CGZ + level + 1) * EZ, :]
        along.append(plain)
        bent.append(stiff)
    copies, fields = [], []
    for x in range(EX):
        for y in range(EY):
            field = jnp.zeros((EZ, NODES), F32)
            for ab in range(4):
                at = (ab * EX + x) * EY + y
                field = field + along[ab] * xy_ref[at : at + 1, :]
            precond_ref[x, y] = smooth_ref[x, y] + active[x][y] * field
            n = len(copies)
            copies.append(
                pltpu.make_async_copy(precond_ref.at[x, y], precond_hbm.at[x, y], sems.at[n])
            )
            copies[-1].start()
            fields.append(field)
    group = lane // VERTS
    shifted = spread
    for far in range(1, VERTS // 2):
        shifted = jnp.where(group == far, turn(spread, far), shifted)
    weight = jnp.where(group == 0, 1.0, 2.0)
    square = got(0) * spread * shifted * weight
    scaled = sums * spread
    square = square + jnp.where(group == AT_G // VERTS, 2.0 * scaled, 0.0)
    distant = jnp.logical_and(lane >= AT_FAR, lane < AT_FAR + VERTS // 2)
    square = square + jnp.where(distant, 2.0 * scaled * turn(spread, VERTS // 2), 0.0)
    square = square + jnp.where(lane == AT_R + KV, sums, 0.0)
    square = jnp.sum(fold(square), axis=1, keepdims=True) / total_points
    linear, plain = fold(scaled), fold(sums)
    line = lane_ids(1, LANES)
    proj = []
    for v in range(KV):
        term = jnp.where(line // VERTS == v, linear, 0.0) + jnp.where(line == AT_R + v, plain, 0.0)
        proj.append(jnp.sum(term, axis=1, keepdims=True) / total_points)
    pair = jnp.zeros((1, LANES), F32)
    position = AT_GRAM
    for v in range(KV):
        for u in range(v, KV):
            factor = 1.0 if u == v else 2.0
            pair = jnp.where(line == position, factor * proj[v] * proj[u], pair)
            position += 1
    gram = jnp.sum(pair * plain, axis=1, keepdims=True) / total_points
    dot = functools.reduce(jnp.add, [p * p for p in proj])
    beta = jnp.sqrt(square - 2.0 * dot + gram + EPSILON)
    inverse = 1.0 / beta
    for x in range(EX):
        for y in range(EY):
            image = jnp.zeros((EZ, NODES), F32)
            for ab in range(4):
                at = (ab * EX + x) * EY + y
                image = image + (
                    along[ab] * xy_ref[XY + at : XY + at + 1, :] + bent[ab] * xy_ref[at : at + 1, :]
                )
            residual = base_ref[x, y] + (active[x][y] * coef[x][y]) * image
            residual = residual + wall_ref[x, y] * fields[x * EY + y]
            for v in range(KV):
                residual = residual - proj[v] * basis_ref[v, x, y]
            next_ref[x, y] = residual * inverse
            n = len(copies)
            copies.append(pltpu.make_async_copy(next_ref.at[x, y], next_hbm.at[x, y], sems.at[n]))
            copies[-1].start()
    result = jnp.zeros((1, LANES), F32)
    for v, value in enumerate(proj + [beta]):
        result = jnp.where(line == v, value, result)
    hessen_ref[...] = result[:, : KV + 1]
    for copy in copies:
        copy.wait()


def spec(kind=pltpu.VMEM):
    return pl.BlockSpec(memory_space=kind)


def call(kernel, outs, in_specs, args, out_specs=None, scratch=(), cost=1000000):
    return pl.pallas_call(
        kernel,
        out_shape=[jax.ShapeDtypeStruct(shape, dtype) for shape, dtype in outs],
        in_specs=in_specs,
        out_specs=out_specs or [spec() for _ in outs],
        scratch_shapes=scratch,
        compiler_params=pltpu.CompilerParams(vmem_limit_bytes=VMEM_BYTES),
        cost_estimate=pl.CostEstimate(flops=cost, bytes_accessed=cost, transcendentals=0),
    )(*args)


def exchange(sends):
    out = [None] * 4
    for place in range(4):
        axis = "bx" if place < 2 else "by"
        size = lax.axis_size(axis)
        assert size % 2 == 0
        pairs = [(i, (i + 1) % size) for i in range(place % 2, size, 2)]
        pairs = pairs + [(j, i) for i, j in pairs]
        out[place] = lax.ppermute(sends[place], axis, pairs)
    return out


def smooth_part(basis, coef, modes, eigen, mask, sends):
    halo = exchange(sends)
    square = ((NODES, NODES), BF16)
    tables = call(
        tables_kernel,
        [square]
        + [((LANES, LANES), BF16)] * 2
        + [((8, NODES), F32), ((2 * XY, NODES), F32), ((2 * CGZ * EZ, NODES), F32)],
        [spec()] * 2,
        (modes, eigen),
    )
    smooth, *sends = call(
        smooth_kernel,
        [FIELD] + [((8, 256), F32)] * 4,
        [spec()] * 9,
        (basis, coef, mask, eigen, tables[0], *halo),
    )
    return halo, tables, smooth, exchange(sends)


FIELD = ((EX, EY, EZ, NODES), F32)
SENDS = [((16, 256), F32)] * 4


def one_exchange(basis, coef, modes, eigen, mask, vertex_ids, coarse_inverse):
    peers = lax.axis_size("bx") * lax.axis_size("by")
    rows = coarse_inverse.shape[1] // peers
    points = EX * EY * EZ * NODES
    *local, a, b, c, d = call(
        load_kernel,
        [(x.shape, x.dtype) for x in (basis, mask, coef, modes, eigen, coarse_inverse)]
        + [((8, LANES), F32)]
        + SENDS,
        [spec(pltpu.HBM)] * 7,
        tuple(pltpu.with_memory_space_constraint(x, pltpu.HBM) for x in (basis, mask, coef, modes, eigen, vertex_ids, coarse_inverse)),
        scratch=[pltpu.VMEM(vertex_ids.shape, vertex_ids.dtype), pltpu.SemaphoreType.DMA((8,))],
    )
    basis, mask, coef, modes, eigen, coarse_inverse, ids = local
    halo, tables, smooth, faces = smooth_part(basis, coef, modes, eigen, mask, (a, b, c, d))
    early, fields, wall = call(
        functools.partial(fields_kernel, 1.0 / math.sqrt(points)),
        [((8, 2 * LANES), F32), ((VERTS,) + FIELD[0], F32), FIELD],
        [spec()] * 9,
        (basis, coef, mask, *halo, tables[4], tables[5]),
        scratch=[pltpu.VMEM((2 * LANES, LANES), F32)],
    )
    base, row = call(
        functools.partial(base_kernel, rows, peers),
        [FIELD, (((SENT + rows) * peers, LANES), F32)],
        [spec()] * 15,
        (basis, smooth, coef, mask, ids, coarse_inverse, *tables[1:4], *faces, early, fields),
        scratch=[pltpu.VMEM((LANES, LANES), F32)],
    )
    row = row.reshape(peers, SENT + rows, 1, LANES)
    got = lax.all_to_all(row, ("bx", "by"), 0, 0).reshape((SENT + rows) * peers, LANES)
    precond, next_vector, hessen = call(
        functools.partial(close_kernel, float(points * peers), rows, peers),
        [FIELD, FIELD, ((1, KV + 1), F32)],
        [spec()] * 9,
        (basis, smooth, base, wall, coef, mask, tables[4], tables[5], got),
        out_specs=[spec(pltpu.HBM), spec(pltpu.HBM), spec()],
        scratch=[pltpu.VMEM(*FIELD), pltpu.VMEM(*FIELD), pltpu.SemaphoreType.DMA((2 * EX * EY,))],
    )
    return precond, next_vector, hessen.reshape(KV + 1)


def two_exchanges(basis, coef, modes, eigen, mask, vertex_ids, coarse_inverse):
    peers = lax.axis_size("bx") * lax.axis_size("by")
    count = coarse_inverse.shape[1]
    points = EX * EY * EZ * NODES
    row, *sends = call(
        functools.partial(start_kernel, 1.0 / math.sqrt(points), count),
        [((1, count), F32)] + SENDS,
        [spec()] * 2 + [spec(pltpu.SMEM)],
        (basis, mask, vertex_ids),
    )
    coarse = lax.psum(row, ("bx", "by"))
    solved = jnp.dot(coarse_inverse, coarse[0], precision=HIGHEST)
    solved = lax.all_gather(solved, "bx", axis=0, tiled=True)[None]
    halo, tables, smooth, faces = smooth_part(basis, coef, modes, eigen, mask, sends)
    precond, image, row = call(
        functools.partial(image_kernel, count),
        [FIELD, FIELD, ((1, LANES), F32)],
        [spec()] * 4 + [spec(pltpu.SMEM)] + [spec()] * 12,
        (basis, smooth, coef, mask, vertex_ids, solved, *tables[1:4], *faces, *halo),
    )
    row = lax.psum(row, ("bx", "by"))
    next_vector, hessen = call(
        functools.partial(finish_kernel, float(points * peers)),
        [FIELD, ((KV + 1,), F32)],
        [spec()] * 3,
        (basis, image, row),
        out_specs=[spec(), spec(pltpu.SMEM)],
    )
    return precond, next_vector, hessen


def body(basis, coef, modes, eigen, mask, vertex_ids, coarse_inverse):
    assert coef.shape == (EX, EY, EZ) and basis.shape[0] == KV
    peers = lax.axis_size("bx") * lax.axis_size("by")
    count = coarse_inverse.shape[1]
    small = count == LANES and count == 4 * peers
    steps = one_exchange if small else two_exchanges
    return tuple(steps(basis, coef, modes, eigen, mask, vertex_ids, coarse_inverse))


def solution(mesh):
    placed = (
        P(None, "bx", "by", None, None),
        P("bx", "by", None),
        P(),
        P(),
        P("bx", "by", None),
        P("bx", "by", None, None, None),
        P("bx", None),
    )
    return jax.shard_map(
        body,
        mesh=mesh,
        in_specs=placed,
        out_specs=(P("bx", "by", None, None), P("bx", "by", None, None), P()),
        check_vma=False,
    )
```

```python
import functools
import math

import jax
import jax.numpy as jnp
from jax import lax
from jax.experimental import pallas as pl
from jax.experimental.pallas import tpu as pltpu
from jax.sharding import PartitionSpec as P


PTS = 8
NODES = PTS**3
KV = 4
CGZ = 4
EX = 2
EY = 2
EZ = 16
LANES = 128
VMEM_BYTES = 12 << 20
HALF = 8
XY = 4 * EX * EY
AT_G, AT_FAR, AT_R, AT_SUM, AT_GRAM, AT_ID = 64, 80, 88, 96, 112, 122
SENT = 2
VERTS = 4 * CGZ

PENALTY = 2.0
SHIFT = 1.0
EPSILON = 1e-06
HIGHEST = lax.Precision.HIGHEST
F32 = jnp.float32
BF16 = jnp.bfloat16


def lane_ids(rows, lanes):
    return lax.broadcasted_iota(jnp.int32, (rows, lanes), 1)


def row_ids(rows, lanes):
    return lax.broadcasted_iota(jnp.int32, (rows, lanes), 0)


def roll_chunks(x, shift):
    shift = shift % LANES
    if shift == 0:
        return x
    pieces = [
        pltpu.roll(x[:, c : c + LANES], shift, 1) for c in range(0, x.shape[1], LANES)
    ]
    return pieces[0] if len(pieces) == 1 else jnp.concatenate(pieces, axis=1)


def column(row):
    wide = jnp.broadcast_to(row, (EZ, EZ))
    keep = row_ids(EZ, EZ) == lane_ids(EZ, EZ)
    return jnp.sum(jnp.where(keep, wide, jnp.zeros_like(wide)), axis=1, keepdims=True)


def columns(ref):
    return [[column(ref[x, y : y + 1, :].astype(F32)) for y in range(EY)] for x in range(EX)]


def blocks_of(parts):
    return [part[8 * b : 8 * b + 8] for part in parts for b in range(EZ // 8)]


def pack_x(parts, high):
    low_half = lane_ids(8, LANES) < 64
    offset = NODES - LANES if high else 0
    cut = [block[:, offset : offset + LANES] for block in blocks_of(parts)]
    out = []
    for m in range(2):
        even = pltpu.roll(cut[2 * m], 64, 1) if high else cut[2 * m]
        odd = cut[2 * m + 1] if high else pltpu.roll(cut[2 * m + 1], 64, 1)
        out.append(jnp.where(low_half, even, odd))
    return jnp.concatenate(out, axis=1)


def unpack_x(packed, high):
    low_half = lane_ids(8, LANES) < 64
    zero = jnp.zeros((8, LANES), F32)
    groups = []
    for g in range(2):
        rows = []
        for b in (2 * g, 2 * g + 1):
            chunk = packed[:, LANES * (b // 2) : LANES * (b // 2) + LANES]
            if (b % 2 == 0) == high:
                chunk = pltpu.roll(chunk, 64, 1)
            chunk = jnp.where(low_half, zero, chunk) if high else jnp.where(low_half, chunk, zero)
            rows.append(
                jnp.concatenate([zero] * 3 + [chunk] if high else [chunk] + [zero] * 3, axis=1)
            )
        groups.append(jnp.concatenate(rows, axis=0))
    return groups


def pack_y(parts, high):
    slot = lane_ids(8, NODES) // PTS % PTS
    from_slot = PTS - 1 if high else 0
    total = jnp.zeros((8, NODES), F32)
    for b, block in enumerate(blocks_of(parts)):
        total = jnp.where(slot == b, roll_chunks(block, PTS * (b - from_slot)), total)
    lower, upper = total[:, :256], roll_chunks(total[:, 256:], 32)
    return jnp.where(slot[:, :256] < 4, lower, upper)


def unpack_y(packed, high):
    slot = lane_ids(8, LANES) // PTS % PTS
    to_slot = PTS - 1 if high else 0
    zero = jnp.zeros((8, LANES), F32)
    groups = []
    for g in range(2):
        rows = []
        for b in (2 * g, 2 * g + 1):
            chunks = []
            for c in range(4):
                source = packed[:, LANES * (c % 2) : LANES * (c % 2) + LANES]
                moved = roll_chunks(source, PTS * (to_slot - b - 4 * (c // 2)))
                chunks.append(jnp.where(slot == to_slot, moved, zero))
            rows.append(jnp.concatenate(chunks, axis=1))
        groups.append(jnp.concatenate(rows, axis=0))
    return groups


def pack_all(groups):
    right = pack_x([groups[EX - 1][y] for y in range(EY)], True)
    left = pack_x([groups[0][y] for y in range(EY)], False)
    back = pack_y([groups[x][EY - 1] for x in range(EX)], True)
    front = pack_y([groups[x][0] for x in range(EX)], False)
    return [*pair_up(right, left, "bx"), *pair_up(back, front, "by")]


def pair_up(first, second, axis):
    place = jnp.full(first.shape, lax.rem(lax.axis_index(axis), 2), jnp.int32)
    even = place == 0
    return jnp.where(even, first, second), jnp.where(even, second, first)


def unpack_all(packed):
    right, left = pair_up(packed[0], packed[1], "bx")
    back, front = pair_up(packed[2], packed[3], "by")
    packed = (left, right, front, back)
    left = unpack_x(packed[0], False)
    right = unpack_x(packed[1], True)
    front = unpack_y(packed[2], False)
    back = unpack_y(packed[3], True)
    out = [[None] * EY for _ in range(EX)]
    for x in range(EX):
        for y in range(EY):
            terms = []
            if x == 0:
                terms.append(left[y])
            if x == EX - 1:
                terms.append(right[y])
            if y == 0:
                terms.append(front[x])
            if y == EY - 1:
                terms.append(back[x])
            out[x][y] = functools.reduce(jnp.add, terms)
    return out


def own_neighbors(groups):
    lane = lane_ids(EZ, NODES)
    row = row_ids(EZ, NODES)
    j, k = lane // PTS % PTS, lane % PTS
    low_z = jnp.logical_and(k == 0, row > 0)
    high_z = jnp.logical_and(k == PTS - 1, row < EZ - 1)
    zero = jnp.zeros((EZ, NODES), F32)
    pad = jnp.zeros((EZ, NODES - LANES), F32)
    low_half = lane_ids(EZ, LANES) < 64
    zero_chunk = jnp.zeros((EZ, LANES), F32)
    out = [[None] * EY for _ in range(EX)]
    for x in range(EX):
        for y in range(EY):
            here = groups[x][y]
            total = jnp.where(low_z, roll_chunks(pltpu.roll(here, 1, 0), 1 - PTS), zero)
            total = total + jnp.where(
                high_z, roll_chunks(pltpu.roll(here, EZ - 1, 0), PTS - 1), zero
            )
            if y > 0:
                moved = roll_chunks(groups[x][y - 1], PTS - PTS * PTS)
                total = total + jnp.where(j == 0, moved, zero)
            if y < EY - 1:
                moved = roll_chunks(groups[x][y + 1], PTS * PTS - PTS)
                total = total + jnp.where(j == PTS - 1, moved, zero)
            if x > 0:
                chunk = pltpu.roll(groups[x - 1][y][:, NODES - LANES :], 64, 1)
                chunk = jnp.where(low_half, chunk, zero_chunk)
                total = total + jnp.concatenate([chunk, pad], axis=1)
            if x < EX - 1:
                chunk = pltpu.roll(groups[x + 1][y][:, :LANES], 64, 1)
                chunk = jnp.where(low_half, zero_chunk, chunk)
                total = total + jnp.concatenate([pad, chunk], axis=1)
            out[x][y] = total
    return out


def load_groups(ref, *lead):
    return [[ref[(*lead, x, y)] for y in range(EY)] for x in range(EX)]


def stack(groups):
    return jnp.concatenate([groups[x][y] for x in range(EX) for y in range(EY)], axis=0)


def unstack(whole):
    return [
        [whole[(x * EY + y) * EZ : (x * EY + y + 1) * EZ] for y in range(EY)] for x in range(EX)
    ]


def hat(place, span, levels, level):
    place = place.astype(F32) / float(span) * float(levels - 1)
    return jnp.maximum(0.0, 1.0 - jnp.abs(place - float(level)))


def hat_z():
    lane, row = lane_ids(EZ, NODES), row_ids(EZ, NODES)
    place = row * (PTS - 1) + lane % PTS
    return [hat(place, EZ * (PTS - 1), CGZ, level) for level in range(CGZ)]


def hat_x(x, a, rows=1):
    place = x * (PTS - 1) + lane_ids(rows, NODES) // (PTS * PTS)
    return hat(place, EX * (PTS - 1), 2, a)


def hat_y(y, b, rows=1):
    place = y * (PTS - 1) + lane_ids(rows, NODES) // PTS % PTS
    return hat(place, EY * (PTS - 1), 2, b)


def face_count(rows):
    lane = lane_ids(rows, NODES)
    total = jnp.zeros((rows, NODES), F32)
    for part in (lane // (PTS * PTS), lane // PTS % PTS, lane % PTS):
        edge = jnp.logical_or(part == 0, part == PTS - 1)
        total = total + jnp.where(edge, 1.0, 0.0)
    return total


def all_sum(x):
    return jnp.sum(jnp.sum(x, axis=0, keepdims=True), axis=1, keepdims=True)


def coarse_row(current, ids_ref, count, scale):
    weight_z = hat_z()
    lane = lane_ids(1, count)
    out = jnp.zeros((1, count), F32)
    for level in range(CGZ):
        sums = [[None] * EY for _ in range(EX)]
        for x in range(EX):
            for y in range(EY):
                sums[x][y] = jnp.sum(current[x][y] * weight_z[level], axis=0, keepdims=True)
        for a in range(2):
            for b in range(2):
                total = jnp.zeros((1, NODES), F32)
                for x in range(EX):
                    for y in range(EY):
                        total = total + sums[x][y] * (hat_x(x, a) * hat_y(y, b))
                value = jnp.sum(total, axis=1, keepdims=True) * scale
                out = out + jnp.where(lane == ids_ref[0, 0, a, b, level], value, 0.0)
    return out


def send_faces(basis_ref, mask_ref, outs):
    current = load_groups(basis_ref, KV - 1)
    active = columns(mask_ref)
    wide = [[jnp.broadcast_to(active[x][y], (EZ, NODES)) for y in range(EY)] for x in range(EX)]
    for ref, face, part in zip(outs, pack_all(current), pack_all(wide)):
        ref[0:8, :] = face
        ref[8:16, :] = part
    return current


def start_kernel(scale, count, basis_ref, mask_ref, ids_ref, row_ref, *outs):
    current = send_faces(basis_ref, mask_ref, outs)
    row_ref[...] = coarse_row(current, ids_ref, count, scale)


def load_kernel(*refs):
    basis_hbm, mask_hbm, coef_hbm, modes_hbm, eigen_hbm, ids_hbm, inverse_hbm = refs[:7]
    basis_ref, mask_ref, coef_ref, modes_ref, eigen_ref, inverse_ref, ids_ref = refs[7:14]
    outs, ids_scratch, sems = refs[14:18], refs[18], refs[19]
    older = slice(0, KV - 1)
    copies = [
        pltpu.make_async_copy(source, target, sems.at[n])
        for n, (source, target) in enumerate(
            (
                (basis_hbm.at[KV - 1], basis_ref.at[KV - 1]),
                (mask_hbm, mask_ref),
                (basis_hbm.at[older], basis_ref.at[older]),
                (coef_hbm, coef_ref),
                (modes_hbm, modes_ref),
                (eigen_hbm, eigen_ref),
                (ids_hbm, ids_scratch),
                (inverse_hbm, inverse_ref),
            )
        )
    ]
    for copy in copies:
        copy.start()
    copies[0].wait()
    copies[1].wait()
    send_faces(basis_ref, mask_ref, outs)
    for copy in copies[2:]:
        copy.wait()
    lane = lane_ids(1, LANES)
    row = jnp.zeros((1, LANES), F32)
    short = ids_scratch[0, 0, 0, 0:1, :].astype(F32)
    for level in range(CGZ):
        row = jnp.where(lane == AT_ID + level, short[:, level : level + 1], row)
    ids_ref[...] = jnp.broadcast_to(row, (8, LANES))


def picker(stride):
    return lane_ids(PTS, NODES) // stride % PTS == row_ids(PTS, NODES)


def expand(matrix, stride):
    pick = picker(stride).astype(F32).astype(BF16)
    out, rest = None, matrix
    for _ in range(3):
        part = rest.astype(BF16)
        rest = rest - part.astype(F32)
        term = jnp.dot(part, pick, preferred_element_type=F32)
        out = term if out is None else out + term
    return out


def tables_kernel(scale, modes_ref, eigen_ref, basis_ref, coef_ref, mask_ref, *refs):
    sb_ref, lh_ref, ll_ref, lx_ref, xy_ref, z_ref, extended_ref, divisor_ref, sums_ref = refs
    strides = (PTS * PTS, PTS, 1)
    straight, stiff, unit = [], [], []
    for d in range(3):
        mode = modes_ref[d]
        scaled = mode * eigen_ref[d : d + 1, :]
        one = lax.dot_general(
            scaled, mode, (((1,), (1,)), ((), ())), precision=HIGHEST, preferred_element_type=F32
        )
        straight.append(expand(mode, strides[d]))
        stiff.append(expand(one, strides[d]))
        unit.append(picker(strides[d]).astype(F32))
    for i in range(PTS):
        for j in range(PTS):
            rows = slice((i * PTS + j) * PTS, (i * PTS + j + 1) * PTS)
            pair = straight[0][i : i + 1] * straight[1][j : j + 1]
            sb_ref[rows, :] = (pair * straight[2]).astype(BF16)
    lane = lane_ids(8, LANES)
    for half in range(2):
        for j in range(PTS):
            rows = slice((half * PTS + j) * PTS, (half * PTS + j + 1) * PTS)
            full = stiff[1][j : j + 1, :LANES] * unit[2][:, :LANES]
            full = full + unit[1][j : j + 1, :LANES] * stiff[2][:, :LANES]
            full = jnp.where(lane // 64 == half, full, 0.0)
            head = full.astype(BF16)
            lh_ref[rows, :] = head
            ll_ref[rows, :] = (full - head.astype(F32)).astype(BF16)
    low_half = lane_ids(1, NODES) % LANES < 64
    for c in range(NODES // LANES):
        even, odd = stiff[0][2 * c : 2 * c + 1], stiff[0][2 * c + 1 : 2 * c + 2]
        lx_ref[c : c + 1, :] = jnp.where(low_half, even, odd)
        lx_ref[c + 4 : c + 5, :] = jnp.where(low_half, odd, even)
    point, row = lane_ids(PTS, PTS), row_ids(PTS, PTS)
    pairs = (row < 2 * EX, row // 2 * (PTS - 1) + point, row % 2)
    short = jnp.maximum(
        0.0,
        1.0 - jnp.abs(pairs[1].astype(F32) / float(EX * (PTS - 1)) - pairs[2].astype(F32)),
    )
    short = jnp.where(pairs[0], short, 0.0)
    stiff_x = jnp.dot(short, stiff[0], precision=HIGHEST, preferred_element_type=F32)
    stiff_y = jnp.dot(short, stiff[1], precision=HIGHEST, preferred_element_type=F32)
    for a in range(2):
        for b in range(2):
            for x in range(EX):
                for y in range(EY):
                    at = ((a * 2 + b) * EX + x) * EY + y
                    plain_x, plain_y = hat_x(x, a), hat_y(y, b)
                    xy_ref[at : at + 1, :] = plain_x * plain_y
                    xy_ref[XY + at : XY + at + 1, :] = (
                        stiff_x[x * 2 + a : x * 2 + a + 1] * plain_y
                        + plain_x * stiff_y[y * 2 + b : y * 2 + b + 1]
                    )
    place = row_ids(EZ, PTS) * (PTS - 1) + lane_ids(EZ, PTS)
    for level, weight in enumerate(hat_z()):
        z_ref[level * EZ : (level + 1) * EZ, :] = weight
        tall = hat(place, EZ * (PTS - 1), CGZ, level)
        z_ref[(CGZ + level) * EZ : (CGZ + level + 1) * EZ, :] = jnp.dot(
            tall, stiff[2], precision=HIGHEST, preferred_element_type=F32
        )
    spectrum = functools.reduce(
        jnp.add, [expand(eigen_ref[d : d + 1, :], strides[d]) for d in range(3)]
    )
    current = load_groups(basis_ref, KV - 1)
    inside = own_neighbors(current)
    coef = columns(coef_ref)
    for x in range(EX):
        for y in range(EY):
            extended_ref[x, y] = current[x][y] + inside[x][y]
            divisor_ref[x, y] = coef[x][y] * spectrum + SHIFT
    sums_ref[...] = jnp.zeros_like(sums_ref)
    halves = range(EZ // HALF)

    def vectors(half):
        return {v: (lambda x, y, r, c, v=v: basis_ref[v, x, y, r, c]) for v in range(KV)}

    def put(row, value):
        sums_ref[row : row + 1, :] = value

    position = {}
    for v in range(KV):
        for u in range(v, KV):
            position[v, u] = len(position)
    products(vectors, lambda half: None, halves, lambda v, u, s: put(AT_GRAM + position[v, u], s))
    for level in range(CGZ):
        sums = [[None] * EY for _ in range(EX)]
        for x in range(EX):
            for y in range(EY):
                sums[x][y] = fold(current[x][y] * z_ref[level * EZ : (level + 1) * EZ, :])
        for ab in range(4):
            total = jnp.zeros((1, NODES), F32)
            for x in range(EX):
                for y in range(EY):
                    at = (ab * EX + x) * EY + y
                    total = total + sums[x][y] * xy_ref[at : at + 1, :]
            parts = [total[:, c : c + LANES] for c in range(0, NODES, LANES)]
            put(AT_SUM + ab * CGZ + level, functools.reduce(jnp.add, parts) * scale)


def smooth_kernel(*refs):
    own_ref, divisor_ref, mask_ref, sb_ref = refs[:4]
    halo = [ref[0:8, :] for ref in refs[4:8]]
    smooth_ref, *send = refs[8:]
    own, outside = load_groups(own_ref), unpack_all(halo)
    active = columns(mask_ref)
    extended = [[own[x][y] + outside[x][y] for y in range(EY)] for x in range(EX)]
    modal = jnp.dot(stack(extended).astype(BF16), sb_ref[...], preferred_element_type=F32)
    modal = unstack(modal)
    modal = [[modal[x][y] / divisor_ref[x, y] for y in range(EY)] for x in range(EX)]
    smooth = lax.dot_general(
        stack(modal).astype(BF16),
        sb_ref[...],
        (((1,), (1,)), ((), ())),
        preferred_element_type=F32,
    )
    smooth = unstack(smooth)
    smooth = [[smooth[x][y] * active[x][y] for y in range(EY)] for x in range(EX)]
    for x in range(EX):
        for y in range(EY):
            smooth_ref[x, y] = smooth[x][y]
    for ref, face in zip(send, pack_all(smooth)):
        ref[...] = face


def stiff_apply(groups, lh_ref, ll_ref, lx_ref):
    whole = stack(groups)
    chunks = [whole[:, c : c + LANES] for c in range(0, NODES, LANES)]
    tall = jnp.concatenate(chunks, axis=0)
    head = tall.astype(BF16)
    tail = (tall - head.astype(F32)).astype(BF16)
    rows, size = tall.shape[0], whole.shape[0]
    both = jnp.dot(jnp.concatenate([head, tail], axis=0), lh_ref[...], preferred_element_type=F32)
    inner = both[:rows] + (both[rows:] + jnp.dot(head, ll_ref[...], preferred_element_type=F32))
    turned = [pltpu.roll(chunk, 64, 1) for chunk in chunks]
    out = []
    for c in range(len(chunks)):
        lanes = slice(c * LANES, (c + 1) * LANES)
        total = inner[c * size : (c + 1) * size]
        for d in range(len(chunks)):
            total = total + chunks[d] * lx_ref[d : d + 1, lanes]
            total = total + turned[d] * lx_ref[d + 4 : d + 5, lanes]
        out.append(total)
    return unstack(jnp.concatenate(out, axis=1))


def image_kernel(count, *refs):
    basis_ref, smooth_ref, coef_ref, mask_ref, ids_ref, got_ref, lh_ref, ll_ref, lx_ref = refs[:9]
    face_refs, mask_refs = refs[9:13], refs[13:17]
    precond_ref, image_ref, row_ref = refs[17:]
    coef, active = columns(coef_ref), columns(mask_ref)
    solved = got_ref[...]
    lane = lane_ids(1, count)
    weight_z = hat_z()
    field = [[jnp.zeros((EZ, NODES), F32) for _ in range(EY)] for _ in range(EX)]
    for a in range(2):
        for b in range(2):
            along = jnp.zeros((EZ, NODES), F32)
            for level in range(CGZ):
                hit = jnp.where(lane == ids_ref[0, 0, a, b, level], solved, 0.0)
                along = along + weight_z[level] * jnp.sum(hit, axis=1, keepdims=True)
            for x in range(EX):
                for y in range(EY):
                    field[x][y] = field[x][y] + along * (hat_x(x, a) * hat_y(y, b))
    smooth = load_groups(smooth_ref)
    precond = [
        [smooth[x][y] + active[x][y] * field[x][y] for y in range(EY)] for x in range(EX)
    ]
    stiff = stiff_apply(precond, lh_ref, ll_ref, lx_ref)
    inside = own_neighbors(precond)
    outside = unpack_all([ref[...] for ref in face_refs])
    open_faces = unpack_all([ref[8:16, :] for ref in mask_refs])
    counts = face_count(EZ)
    dots = [jnp.zeros((EZ, NODES), F32) for _ in range(KV + 1)]
    for x in range(EX):
        for y in range(EY):
            across = outside[x][y] + open_faces[x][y] * field[x][y]
            image = active[x][y] * (
                coef[x][y] * stiff[x][y]
                + PENALTY * (counts * precond[x][y] - (inside[x][y] + across))
            )
            precond_ref[x, y] = precond[x][y]
            image_ref[x, y] = image
            for v in range(KV):
                dots[v] = dots[v] + basis_ref[v, x, y] * image
            dots[KV] = dots[KV] + image * image
    values = [all_sum(d) for d in dots]
    basis = [load_groups(basis_ref, v) for v in range(KV)]
    for v in range(KV):
        for u in range(v, KV):
            total = jnp.zeros((EZ, NODES), F32)
            for x in range(EX):
                for y in range(EY):
                    total = total + basis[v][x][y] * basis[u][x][y]
            values.append(all_sum(total))
    row = jnp.zeros((1, LANES), F32)
    row_lane = lane_ids(1, LANES)
    for position, value in enumerate(values):
        row = jnp.where(row_lane == position, value, row)
    row_ref[...] = row


def finish_kernel(total_points, basis_ref, image_ref, got_ref, next_ref, hessen_ref):
    sums = got_ref[...] / total_points
    lane = lane_ids(1, LANES)

    def pick(position):
        return jnp.sum(jnp.where(lane == position, sums, 0.0), axis=1, keepdims=True)

    proj = [pick(v) for v in range(KV)]
    square = pick(KV)
    position = KV + 1
    quad = jnp.zeros((1, 1), F32)
    for v in range(KV):
        for u in range(v, KV):
            factor = 1.0 if u == v else 2.0
            quad = quad + factor * proj[v] * proj[u] * pick(position)
            position += 1
    dot = functools.reduce(jnp.add, [p * p for p in proj])
    beta = jnp.sqrt(square - 2.0 * dot + quad + EPSILON)
    for x in range(EX):
        for y in range(EY):
            residual = image_ref[x, y]
            for v in range(KV):
                residual = residual - proj[v] * basis_ref[v, x, y]
            next_ref[x, y] = residual / beta
    for v, value in enumerate(proj + [beta]):
        hessen_ref[v] = jnp.sum(value)


def levels_of(half):
    found = []
    for level in range(CGZ):
        for point in range(half * HALF * (PTS - 1), (half * HALF + HALF - 1) * (PTS - 1) + PTS):
            if abs(point * (CGZ - 1) / (EZ * (PTS - 1)) - level) < 1.0 + 1e-3:
                found.append(level)
                break
    return found


def lane_sums(x):
    return lax.dot_general(
        jnp.ones((8, LANES), F32),
        x,
        (((1,), (1,)), ((), ())),
        precision=HIGHEST,
        preferred_element_type=F32,
    )


def fold(acc):
    return jnp.sum(acc, axis=0, keepdims=True)


def pieces_of(half):
    for x in range(EX):
        for y in range(EY):
            for c in range(NODES // LANES):
                yield x, y, slice(half * HALF, half * HALF + HALF), slice(c * LANES, (c + 1) * LANES)


def products(left, right, halves, out_row):
    accs = {}
    for half in halves:
        lefts, rights = left(half), right(half)
        for piece in pieces_of(half):
            own = {v: load(*piece) for v, load in lefts.items()}
            other = own if rights is None else {w: load(*piece) for w, load in rights.items()}
            for v, first in own.items():
                for w, second in other.items():
                    if rights is None and w < v:
                        continue
                    term = first * second
                    accs[v, w] = accs[v, w] + term if (v, w) in accs else term
    for (v, w), acc in accs.items():
        out_row(v, w, fold(acc))


def fields_kernel(basis_ref, coef_ref, mask_ref, *refs):
    mask_refs, (xy_ref, z_ref) = refs[:4], refs[4:6]
    smooth_ref, lh_ref, ll_ref, lx_ref, sums_ref = refs[6:11]
    early_ref, field_ref, wall_ref, part_ref, rows_ref = refs[11:]
    coef, active = columns(coef_ref), columns(mask_ref)
    wide = [[jnp.broadcast_to(active[x][y], (EZ, NODES)) for y in range(EY)] for x in range(EX)]
    inside, outside = own_neighbors(wide), unpack_all([ref[8:16, :] for ref in mask_refs])
    counts = face_count(EZ)
    halves = range(EZ // HALF)
    levels = [levels_of(half) for half in halves]
    smooth = load_groups(smooth_ref)
    stiff_part = stiff_apply(smooth, lh_ref, ll_ref, lx_ref)
    inside_part = own_neighbors(smooth)
    for x in range(EX):
        for y in range(EY):
            wall = active[x][y] * PENALTY * (counts - (inside[x][y] + outside[x][y]))
            wall_ref[x, y] = wall
            part_ref[x, y] = active[x][y] * (
                coef[x][y] * stiff_part[x][y]
                + PENALTY * (counts * smooth[x][y] - inside_part[x][y])
            )
            weight = active[x][y] * coef[x][y]
            for half in halves:
                rows = slice(half * HALF, half * HALF + HALF)
                for ab in range(4):
                    at = (ab * EX + x) * EY + y
                    plain = xy_ref[at : at + 1, :]
                    first = weight[rows] * xy_ref[XY + at : XY + at + 1, :] + wall[rows] * plain
                    second = weight[rows] * plain
                    for level in levels[half]:
                        tall = slice(level * EZ + half * HALF, level * EZ + half * HALF + HALF)
                        stiff = slice((CGZ + level) * EZ + half * HALF, (CGZ + level) * EZ + half * HALF + HALF)
                        field_ref[ab * CGZ + level, x, y, rows, :] = (
                            z_ref[tall, :] * first + z_ref[stiff, :] * second
                        )
    rows_ref[:LANES, :] = jnp.zeros((LANES, LANES), F32)
    rows_ref[LANES:, :] = sums_ref[...]

    def fields(ab):
        def at(half):
            return {
                ab * CGZ + level: (lambda x, y, r, c, v=ab * CGZ + level: field_ref[v, x, y, r, c])
                for level in levels[half]
            }

        return at

    def vectors(half):
        return {v: (lambda x, y, r, c, v=v: basis_ref[v, x, y, r, c]) for v in range(KV)}

    def put(row, value):
        rows_ref[row : row + 1, :] = value

    def put_field(v, w, value):
        far = (w - v) % VERTS
        if far > VERTS // 2 or (far == VERTS // 2 and v > w):
            v, far = w, VERTS - far
        put(LANES + AT_FAR + v if far == VERTS // 2 else far * VERTS + v, value)

    for ab in range(4):
        products(vectors, fields(ab), halves, lambda v, w, s: put(LANES + v * VERTS + w, s))
        products(fields(ab), lambda half: None, halves, put_field)
        for other in range(ab + 1, 4):
            products(fields(ab), fields(other), halves, put_field)
    early_ref[...] = lane_sums(rows_ref[...])


def base_kernel(rows, peers, *refs):
    basis_ref, part_ref, mask_ref, ids_ref, inverse_ref = refs[:5]
    face_refs, early_ref, field_ref = refs[5:9], refs[9], refs[10]
    base_ref, send_ref, rows_ref = refs[11:]
    active = columns(mask_ref)
    outside = unpack_all([ref[...] for ref in face_refs])
    for x in range(EX):
        for y in range(EY):
            base_ref[x, y] = part_ref[x, y] - (PENALTY * active[x][y]) * outside[x][y]
    rows_ref[...] = jnp.zeros_like(rows_ref)
    halves = range(EZ // HALF)

    def base(half):
        return {KV: (lambda x, y, r, c: base_ref[x, y, r, c])}

    def vectors(half):
        found = {v: (lambda x, y, r, c, v=v: basis_ref[v, x, y, r, c]) for v in range(KV)}
        found.update(base(half))
        return found

    def fields(part):
        def at(half):
            return {
                v: (lambda x, y, r, c, v=v: field_ref[v, x, y, r, c])
                for v in range(part * 8, part * 8 + 8)
                if v % CGZ in levels_of(half)
            }

        return at

    def put(row, value):
        rows_ref[row : row + 1, :] = value

    products(base, vectors, halves, lambda v, w, s: put(AT_R + w, s))
    for part in range(VERTS // 8):
        products(base, fields(part), halves, lambda v, w, s: put(AT_G + w, s))
    late = lane_sums(rows_ref[...])
    early = early_ref[...]
    first = lax.axis_index("by") * rows
    tile = jnp.concatenate(
        [early[0:1, :LANES], early[0:1, LANES:] + late[0:1] + ids_ref[0:1, :]]
        + [inverse_ref[pl.ds(first + r, 1), :] for r in range(rows)],
        axis=0,
    )
    size = SENT + rows
    for peer in range(peers):
        send_ref[size * peer : size * peer + size, :] = tile


def close_kernel(total_points, rows, peers, *refs):
    basis_ref, smooth_ref, base_ref, wall_ref, coef_ref, mask_ref = refs[:6]
    xy_ref, z_ref, got_ref, precond_hbm, next_hbm, hessen_hbm = refs[6:12]
    precond_ref, next_ref, hessen_ref, sems = refs[12:]
    lane, row = lane_ids(peers, LANES), row_ids(peers, LANES)
    side = lax.axis_size("by")

    def got(r):
        return got_ref[pl.ds(r, peers, stride=SENT + rows), :]

    def along_x(values, step):
        return pltpu.roll(values, (step * side) % peers, 0)

    def along_y(values, step):
        edge = row % side == (0 if step > 0 else side - 1)
        wrapped = pltpu.roll(values, (step * (1 - side)) % peers, 0)
        return jnp.where(edge, wrapped, pltpu.roll(values, step % peers, 0))

    def turn(values, lanes):
        return pltpu.roll(values, (-lanes) % LANES, 1)

    sums = got(1)
    corner = sums + along_x(turn(sums, 2 * CGZ), 1)
    other = turn(sums, CGZ) + along_x(turn(sums, 3 * CGZ), 1)
    corner = corner + along_y(other, 1)
    number = lane.astype(F32)
    hits = [number == sums[:, AT_ID + v : AT_ID + v + 1] for v in range(CGZ)]
    coarse = jnp.zeros((peers, LANES), F32)
    for v in range(CGZ):
        coarse = coarse + jnp.where(hits[v], corner[:, AT_SUM + v : AT_SUM + v + 1], 0.0)
    coarse = fold(coarse)
    solved = jnp.zeros((peers, LANES), F32)
    for r in range(rows):
        part = jnp.where(lane == row * rows + r, coarse, 0.0)
        solved = solved + jnp.sum(part, axis=1, keepdims=True) * got(SENT + r)
    solved = fold(solved)
    near = jnp.zeros((peers, LANES), F32)
    for v in range(CGZ):
        value = jnp.sum(jnp.where(hits[v], solved, 0.0), axis=1, keepdims=True)
        near = jnp.where(lane % CGZ == v, value, near)
    right = along_x(near, -1)
    quarter = lane % VERTS // CGZ
    lower = jnp.where(quarter < 2, near, right)
    spread = jnp.where(quarter % 2 == 0, lower, along_y(lower, -1))
    me = lax.axis_index("bx") * side + lax.axis_index("by")
    own = fold(jnp.where(row == me, spread, 0.0))
    coef, active = columns(coef_ref), columns(mask_ref)
    along, bent = [], []
    for ab in range(4):
        plain = jnp.zeros((EZ, NODES), F32)
        stiff = jnp.zeros((EZ, NODES), F32)
        for level in range(CGZ):
            value = own[:, ab * CGZ + level : ab * CGZ + level + 1]
            plain = plain + value * z_ref[level * EZ : (level + 1) * EZ, :]
            stiff = stiff + value * z_ref[(CGZ + level) * EZ : (CGZ + level + 1) * EZ, :]
        along.append(plain)
        bent.append(stiff)
    copies, fields = [], []
    for x in range(EX):
        for y in range(EY):
            field = jnp.zeros((EZ, NODES), F32)
            for ab in range(4):
                at = (ab * EX + x) * EY + y
                field = field + along[ab] * xy_ref[at : at + 1, :]
            precond_ref[x, y] = smooth_ref[x, y] + active[x][y] * field
            n = len(copies)
            copies.append(
                pltpu.make_async_copy(precond_ref.at[x, y], precond_hbm.at[x, y], sems.at[n])
            )
            copies[-1].start()
            fields.append(field)
    group = lane // VERTS
    shifted = spread
    for far in range(1, VERTS // 2):
        shifted = jnp.where(group == far, turn(spread, far), shifted)
    weight = jnp.where(group == 0, 1.0, 2.0)
    square = got(0) * spread * shifted * weight
    scaled = sums * spread
    square = square + jnp.where(group == AT_G // VERTS, 2.0 * scaled, 0.0)
    distant = jnp.logical_and(lane >= AT_FAR, lane < AT_FAR + VERTS // 2)
    square = square + jnp.where(distant, 2.0 * scaled * turn(spread, VERTS // 2), 0.0)
    square = square + jnp.where(lane == AT_R + KV, sums, 0.0)
    square = jnp.sum(fold(square), axis=1, keepdims=True) / total_points
    linear, plain = fold(scaled), fold(sums)
    line = lane_ids(1, LANES)
    proj = []
    for v in range(KV):
        term = jnp.where(line // VERTS == v, linear, 0.0) + jnp.where(line == AT_R + v, plain, 0.0)
        proj.append(jnp.sum(term, axis=1, keepdims=True) / total_points)
    pair = jnp.zeros((1, LANES), F32)
    position = AT_GRAM
    for v in range(KV):
        for u in range(v, KV):
            factor = 1.0 if u == v else 2.0
            pair = jnp.where(line == position, factor * proj[v] * proj[u], pair)
            position += 1
    gram = jnp.sum(pair * plain, axis=1, keepdims=True) / total_points
    dot = functools.reduce(jnp.add, [p * p for p in proj])
    beta = jnp.sqrt(square - 2.0 * dot + gram + EPSILON)
    result = jnp.zeros((1, LANES), F32)
    for v, value in enumerate(proj + [beta]):
        result = jnp.where(line == v, value, result)
    hessen_ref[...] = result[:, : KV + 1]
    copies.append(pltpu.make_async_copy(hessen_ref, hessen_hbm, sems.at[2 * EX * EY]))
    copies[-1].start()
    inverse = 1.0 / beta
    for x in range(EX):
        for y in range(EY):
            image = jnp.zeros((EZ, NODES), F32)
            for ab in range(4):
                at = (ab * EX + x) * EY + y
                image = image + (
                    along[ab] * xy_ref[XY + at : XY + at + 1, :] + bent[ab] * xy_ref[at : at + 1, :]
                )
            residual = base_ref[x, y] + (active[x][y] * coef[x][y]) * image
            residual = residual + wall_ref[x, y] * fields[x * EY + y]
            for v in range(KV):
                residual = residual - proj[v] * basis_ref[v, x, y]
            next_ref[x, y] = residual * inverse
            n = EX * EY + x * EY + y
            copies.append(pltpu.make_async_copy(next_ref.at[x, y], next_hbm.at[x, y], sems.at[n]))
            copies[-1].start()
    for copy in copies:
        copy.wait()


def spec(kind=pltpu.VMEM):
    return pl.BlockSpec(memory_space=kind)


def call(kernel, outs, in_specs, args, out_specs=None, scratch=(), cost=1000000):
    return pl.pallas_call(
        kernel,
        out_shape=[jax.ShapeDtypeStruct(shape, dtype) for shape, dtype in outs],
        in_specs=in_specs,
        out_specs=out_specs or [spec() for _ in outs],
        scratch_shapes=scratch,
        compiler_params=pltpu.CompilerParams(vmem_limit_bytes=VMEM_BYTES),
        cost_estimate=pl.CostEstimate(flops=cost, bytes_accessed=cost, transcendentals=0),
    )(*args)


def exchange(sends):
    out = [None] * 4
    for place in range(4):
        axis = "bx" if place < 2 else "by"
        size = lax.axis_size(axis)
        assert size % 2 == 0
        pairs = [(i, (i + 1) % size) for i in range(place % 2, size, 2)]
        pairs = pairs + [(j, i) for i, j in pairs]
        out[place] = lax.ppermute(sends[place], axis, pairs)
    return out


def smooth_part(basis, coef, modes, eigen, mask, sends):
    halo = exchange(sends)
    tables = call(
        functools.partial(tables_kernel, 1.0 / math.sqrt(EX * EY * EZ * NODES)),
        [((NODES, NODES), BF16)]
        + [((LANES, LANES), BF16)] * 2
        + [((8, NODES), F32), ((2 * XY, NODES), F32), ((2 * CGZ * EZ, NODES), F32)]
        + [FIELD, FIELD, ((LANES, LANES), F32)],
        [spec()] * 5,
        (modes, eigen, basis, coef, mask),
    )
    smooth, *sends = call(
        smooth_kernel,
        [FIELD] + [((8, 256), F32)] * 4,
        [spec()] * 8,
        (tables[6], tables[7], mask, tables[0], *halo),
    )
    return halo, tables, smooth, exchange(sends)


FIELD = ((EX, EY, EZ, NODES), F32)
SENDS = [((16, 256), F32)] * 4


def one_exchange(basis, coef, modes, eigen, mask, vertex_ids, coarse_inverse):
    peers = lax.axis_size("bx") * lax.axis_size("by")
    rows = coarse_inverse.shape[1] // peers
    points = EX * EY * EZ * NODES
    *local, a, b, c, d = call(
        load_kernel,
        [(x.shape, x.dtype) for x in (basis, mask, coef, modes, eigen, coarse_inverse)]
        + [((8, LANES), F32)]
        + SENDS,
        [spec(pltpu.HBM)] * 7,
        tuple(pltpu.with_memory_space_constraint(x, pltpu.HBM) for x in (basis, mask, coef, modes, eigen, vertex_ids, coarse_inverse)),
        scratch=[pltpu.VMEM(vertex_ids.shape, vertex_ids.dtype), pltpu.SemaphoreType.DMA((8,))],
    )
    basis, mask, coef, modes, eigen, coarse_inverse, ids = local
    halo, tables, smooth, faces = smooth_part(basis, coef, modes, eigen, mask, (a, b, c, d))
    early, fields, wall, part = call(
        fields_kernel,
        [((8, 2 * LANES), F32), ((VERTS,) + FIELD[0], F32), FIELD, FIELD],
        [spec()] * 14,
        (basis, coef, mask, *halo, tables[4], tables[5], smooth, *tables[1:4], tables[8]),
        scratch=[pltpu.VMEM((2 * LANES, LANES), F32)],
    )
    base, row = call(
        functools.partial(base_kernel, rows, peers),
        [FIELD, (((SENT + rows) * peers, LANES), F32)],
        [spec()] * 11,
        (basis, part, mask, ids, coarse_inverse, *faces, early, fields),
        scratch=[pltpu.VMEM((LANES, LANES), F32)],
    )
    row = row.reshape(peers, SENT + rows, 1, LANES)
    got = lax.all_to_all(row, ("bx", "by"), 0, 0).reshape((SENT + rows) * peers, LANES)
    precond, next_vector, hessen = call(
        functools.partial(close_kernel, float(points * peers), rows, peers),
        [FIELD, FIELD, ((1, KV + 1), F32)],
        [spec()] * 9,
        (basis, smooth, base, wall, coef, mask, tables[4], tables[5], got),
        out_specs=[spec(pltpu.HBM)] * 3,
        scratch=[pltpu.VMEM(*FIELD)] * 2
        + [pltpu.VMEM((1, KV + 1), F32), pltpu.SemaphoreType.DMA((2 * EX * EY + 1,))],
    )
    return precond, next_vector, hessen.reshape(KV + 1)


def two_exchanges(basis, coef, modes, eigen, mask, vertex_ids, coarse_inverse):
    peers = lax.axis_size("bx") * lax.axis_size("by")
    count = coarse_inverse.shape[1]
    points = EX * EY * EZ * NODES
    row, *sends = call(
        functools.partial(start_kernel, 1.0 / math.sqrt(points), count),
        [((1, count), F32)] + SENDS,
        [spec()] * 2 + [spec(pltpu.SMEM)],
        (basis, mask, vertex_ids),
    )
    coarse = lax.psum(row, ("bx", "by"))
    solved = jnp.dot(coarse_inverse, coarse[0], precision=HIGHEST)
    solved = lax.all_gather(solved, "bx", axis=0, tiled=True)[None]
    halo, tables, smooth, faces = smooth_part(basis, coef, modes, eigen, mask, sends)
    precond, image, row = call(
        functools.partial(image_kernel, count),
        [FIELD, FIELD, ((1, LANES), F32)],
        [spec()] * 4 + [spec(pltpu.SMEM)] + [spec()] * 12,
        (basis, smooth, coef, mask, vertex_ids, solved, *tables[1:4], *faces, *halo),
    )
    row = lax.psum(row, ("bx", "by"))
    next_vector, hessen = call(
        functools.partial(finish_kernel, float(points * peers)),
        [FIELD, ((KV + 1,), F32)],
        [spec()] * 3,
        (basis, image, row),
        out_specs=[spec(), spec(pltpu.SMEM)],
    )
    return precond, next_vector, hessen


def body(basis, coef, modes, eigen, mask, vertex_ids, coarse_inverse):
    assert coef.shape == (EX, EY, EZ) and basis.shape[0] == KV
    peers = lax.axis_size("bx") * lax.axis_size("by")
    count = coarse_inverse.shape[1]
    small = count == LANES and count == 4 * peers
    steps = one_exchange if small else two_exchanges
    return tuple(steps(basis, coef, modes, eigen, mask, vertex_ids, coarse_inverse))


def solution(mesh):
    placed = (
        P(None, "bx", "by", None, None),
        P("bx", "by", None),
        P(),
        P(),
        P("bx", "by", None),
        P("bx", "by", None, None, None),
        P("bx", None),
    )
    return jax.shard_map(
        body,
        mesh=mesh,
        in_specs=placed,
        out_specs=(P("bx", "by", None, None), P("bx", "by", None, None), P()),
        check_vma=False,
    )
```

```python
import functools
import math

import jax
import jax.numpy as jnp
from jax import lax
from jax.experimental import pallas as pl
from jax.experimental.pallas import tpu as pltpu
from jax.sharding import PartitionSpec as P


PTS = 8
NODES = PTS**3
KV = 4
CGZ = 4
EX = 2
EY = 2
EZ = 16
LANES = 128
VMEM_BYTES = 12 << 20
HALF = 8
XY = 4 * EX * EY
AT_G, AT_FAR, AT_R, AT_SUM, AT_GRAM, AT_ID = 64, 80, 88, 96, 112, 122
SENT = 2
MIXED = 24
APART = 33
VERTS = 4 * CGZ

PENALTY = 2.0
SHIFT = 1.0
EPSILON = 1e-06
HIGHEST = lax.Precision.HIGHEST
F32 = jnp.float32
BF16 = jnp.bfloat16


def lane_ids(rows, lanes):
    return lax.broadcasted_iota(jnp.int32, (rows, lanes), 1)


def row_ids(rows, lanes):
    return lax.broadcasted_iota(jnp.int32, (rows, lanes), 0)


def roll_chunks(x, shift):
    shift = shift % LANES
    if shift == 0:
        return x
    pieces = [
        pltpu.roll(x[:, c : c + LANES], shift, 1) for c in range(0, x.shape[1], LANES)
    ]
    return pieces[0] if len(pieces) == 1 else jnp.concatenate(pieces, axis=1)


def column(row):
    wide = jnp.broadcast_to(row, (EZ, EZ))
    keep = row_ids(EZ, EZ) == lane_ids(EZ, EZ)
    return jnp.sum(jnp.where(keep, wide, jnp.zeros_like(wide)), axis=1, keepdims=True)


def columns(ref):
    return [[column(ref[x, y : y + 1, :].astype(F32)) for y in range(EY)] for x in range(EX)]


def blocks_of(parts):
    return [part[8 * b : 8 * b + 8] for part in parts for b in range(EZ // 8)]


def pack_x(parts, high):
    low_half = lane_ids(8, LANES) < 64
    offset = NODES - LANES if high else 0
    cut = [block[:, offset : offset + LANES] for block in blocks_of(parts)]
    out = []
    for m in range(2):
        even = pltpu.roll(cut[2 * m], 64, 1) if high else cut[2 * m]
        odd = cut[2 * m + 1] if high else pltpu.roll(cut[2 * m + 1], 64, 1)
        out.append(jnp.where(low_half, even, odd))
    return jnp.concatenate(out, axis=1)


def unpack_x(packed, high):
    low_half = lane_ids(8, LANES) < 64
    zero = jnp.zeros((8, LANES), F32)
    groups = []
    for g in range(2):
        rows = []
        for b in (2 * g, 2 * g + 1):
            chunk = packed[:, LANES * (b // 2) : LANES * (b // 2) + LANES]
            if (b % 2 == 0) == high:
                chunk = pltpu.roll(chunk, 64, 1)
            chunk = jnp.where(low_half, zero, chunk) if high else jnp.where(low_half, chunk, zero)
            rows.append(
                jnp.concatenate([zero] * 3 + [chunk] if high else [chunk] + [zero] * 3, axis=1)
            )
        groups.append(jnp.concatenate(rows, axis=0))
    return groups


def pack_y(parts, high):
    slot = lane_ids(8, NODES) // PTS % PTS
    from_slot = PTS - 1 if high else 0
    total = jnp.zeros((8, NODES), F32)
    for b, block in enumerate(blocks_of(parts)):
        total = jnp.where(slot == b, roll_chunks(block, PTS * (b - from_slot)), total)
    lower, upper = total[:, :256], roll_chunks(total[:, 256:], 32)
    return jnp.where(slot[:, :256] < 4, lower, upper)


def unpack_y(packed, high):
    slot = lane_ids(8, LANES) // PTS % PTS
    to_slot = PTS - 1 if high else 0
    zero = jnp.zeros((8, LANES), F32)
    groups = []
    for g in range(2):
        rows = []
        for b in (2 * g, 2 * g + 1):
            chunks = []
            for c in range(4):
                source = packed[:, LANES * (c % 2) : LANES * (c % 2) + LANES]
                moved = roll_chunks(source, PTS * (to_slot - b - 4 * (c // 2)))
                chunks.append(jnp.where(slot == to_slot, moved, zero))
            rows.append(jnp.concatenate(chunks, axis=1))
        groups.append(jnp.concatenate(rows, axis=0))
    return groups


def pack_all(groups):
    right = pack_x([groups[EX - 1][y] for y in range(EY)], True)
    left = pack_x([groups[0][y] for y in range(EY)], False)
    back = pack_y([groups[x][EY - 1] for x in range(EX)], True)
    front = pack_y([groups[x][0] for x in range(EX)], False)
    return [*pair_up(right, left, "bx"), *pair_up(back, front, "by")]


def pair_up(first, second, axis):
    place = jnp.full(first.shape, lax.rem(lax.axis_index(axis), 2), jnp.int32)
    even = place == 0
    return jnp.where(even, first, second), jnp.where(even, second, first)


def unpack_all(packed):
    right, left = pair_up(packed[0], packed[1], "bx")
    back, front = pair_up(packed[2], packed[3], "by")
    packed = (left, right, front, back)
    left = unpack_x(packed[0], False)
    right = unpack_x(packed[1], True)
    front = unpack_y(packed[2], False)
    back = unpack_y(packed[3], True)
    out = [[None] * EY for _ in range(EX)]
    for x in range(EX):
        for y in range(EY):
            terms = []
            if x == 0:
                terms.append(left[y])
            if x == EX - 1:
                terms.append(right[y])
            if y == 0:
                terms.append(front[x])
            if y == EY - 1:
                terms.append(back[x])
            out[x][y] = functools.reduce(jnp.add, terms)
    return out


def own_neighbors(groups):
    lane = lane_ids(EZ, NODES)
    row = row_ids(EZ, NODES)
    j, k = lane // PTS % PTS, lane % PTS
    low_z = jnp.logical_and(k == 0, row > 0)
    high_z = jnp.logical_and(k == PTS - 1, row < EZ - 1)
    zero = jnp.zeros((EZ, NODES), F32)
    pad = jnp.zeros((EZ, NODES - LANES), F32)
    low_half = lane_ids(EZ, LANES) < 64
    zero_chunk = jnp.zeros((EZ, LANES), F32)
    out = [[None] * EY for _ in range(EX)]
    for x in range(EX):
        for y in range(EY):
            here = groups[x][y]
            total = jnp.where(low_z, roll_chunks(pltpu.roll(here, 1, 0), 1 - PTS), zero)
            total = total + jnp.where(
                high_z, roll_chunks(pltpu.roll(here, EZ - 1, 0), PTS - 1), zero
            )
            if y > 0:
                moved = roll_chunks(groups[x][y - 1], PTS - PTS * PTS)
                total = total + jnp.where(j == 0, moved, zero)
            if y < EY - 1:
                moved = roll_chunks(groups[x][y + 1], PTS * PTS - PTS)
                total = total + jnp.where(j == PTS - 1, moved, zero)
            if x > 0:
                chunk = pltpu.roll(groups[x - 1][y][:, NODES - LANES :], 64, 1)
                chunk = jnp.where(low_half, chunk, zero_chunk)
                total = total + jnp.concatenate([chunk, pad], axis=1)
            if x < EX - 1:
                chunk = pltpu.roll(groups[x + 1][y][:, :LANES], 64, 1)
                chunk = jnp.where(low_half, zero_chunk, chunk)
                total = total + jnp.concatenate([pad, chunk], axis=1)
            out[x][y] = total
    return out


def load_groups(ref, *lead):
    return [[ref[(*lead, x, y)] for y in range(EY)] for x in range(EX)]


def stack(groups):
    return jnp.concatenate([groups[x][y] for x in range(EX) for y in range(EY)], axis=0)


def unstack(whole):
    return [
        [whole[(x * EY + y) * EZ : (x * EY + y + 1) * EZ] for y in range(EY)] for x in range(EX)
    ]


def hat(place, span, levels, level):
    place = place.astype(F32) / float(span) * float(levels - 1)
    return jnp.maximum(0.0, 1.0 - jnp.abs(place - float(level)))


def hat_z():
    lane, row = lane_ids(EZ, NODES), row_ids(EZ, NODES)
    place = row * (PTS - 1) + lane % PTS
    return [hat(place, EZ * (PTS - 1), CGZ, level) for level in range(CGZ)]


def hat_x(x, a, rows=1):
    place = x * (PTS - 1) + lane_ids(rows, NODES) // (PTS * PTS)
    return hat(place, EX * (PTS - 1), 2, a)


def hat_y(y, b, rows=1):
    place = y * (PTS - 1) + lane_ids(rows, NODES) // PTS % PTS
    return hat(place, EY * (PTS - 1), 2, b)


def face_count(rows):
    lane = lane_ids(rows, NODES)
    total = jnp.zeros((rows, NODES), F32)
    for part in (lane // (PTS * PTS), lane // PTS % PTS, lane % PTS):
        edge = jnp.logical_or(part == 0, part == PTS - 1)
        total = total + jnp.where(edge, 1.0, 0.0)
    return total


def all_sum(x):
    return jnp.sum(jnp.sum(x, axis=0, keepdims=True), axis=1, keepdims=True)


def coarse_row(current, ids_ref, count, scale):
    weight_z = hat_z()
    lane = lane_ids(1, count)
    out = jnp.zeros((1, count), F32)
    for level in range(CGZ):
        sums = [[None] * EY for _ in range(EX)]
        for x in range(EX):
            for y in range(EY):
                sums[x][y] = jnp.sum(current[x][y] * weight_z[level], axis=0, keepdims=True)
        for a in range(2):
            for b in range(2):
                total = jnp.zeros((1, NODES), F32)
                for x in range(EX):
                    for y in range(EY):
                        total = total + sums[x][y] * (hat_x(x, a) * hat_y(y, b))
                value = jnp.sum(total, axis=1, keepdims=True) * scale
                out = out + jnp.where(lane == ids_ref[0, 0, a, b, level], value, 0.0)
    return out


def send_faces(basis_ref, mask_ref, outs):
    current = load_groups(basis_ref, KV - 1)
    active = columns(mask_ref)
    wide = [[jnp.broadcast_to(active[x][y], (EZ, NODES)) for y in range(EY)] for x in range(EX)]
    for ref, face, part in zip(outs, pack_all(current), pack_all(wide)):
        ref[0:8, :] = face
        ref[8:16, :] = part
    return current


def start_kernel(scale, count, basis_ref, mask_ref, ids_ref, row_ref, *outs):
    current = send_faces(basis_ref, mask_ref, outs)
    row_ref[...] = coarse_row(current, ids_ref, count, scale)


def load_kernel(*refs):
    basis_hbm, mask_hbm, coef_hbm, modes_hbm, eigen_hbm, ids_hbm, inverse_hbm = refs[:7]
    basis_ref, mask_ref, coef_ref, modes_ref, eigen_ref, inverse_ref, ids_ref = refs[7:14]
    outs, ids_scratch, sems = refs[14:18], refs[18], refs[19]
    older = slice(0, KV - 1)
    copies = [
        pltpu.make_async_copy(source, target, sems.at[n])
        for n, (source, target) in enumerate(
            (
                (basis_hbm.at[KV - 1], basis_ref.at[KV - 1]),
                (mask_hbm, mask_ref),
                (basis_hbm.at[older], basis_ref.at[older]),
                (coef_hbm, coef_ref),
                (modes_hbm, modes_ref),
                (eigen_hbm, eigen_ref),
                (ids_hbm, ids_scratch),
                (inverse_hbm, inverse_ref),
            )
        )
    ]
    for copy in copies:
        copy.start()
    copies[0].wait()
    copies[1].wait()
    send_faces(basis_ref, mask_ref, outs)
    for copy in copies[2:]:
        copy.wait()
    lane = lane_ids(1, LANES)
    row = jnp.zeros((1, LANES), F32)
    short = ids_scratch[0, 0, 0, 0:1, :].astype(F32)
    for level in range(CGZ):
        row = jnp.where(lane == AT_ID + level, short[:, level : level + 1], row)
    ids_ref[...] = jnp.broadcast_to(row, (8, LANES))


def picker(stride):
    return lane_ids(PTS, NODES) // stride % PTS == row_ids(PTS, NODES)


def expand(matrix, stride):
    pick = picker(stride).astype(F32).astype(BF16)
    out, rest = None, matrix
    for _ in range(3):
        part = rest.astype(BF16)
        rest = rest - part.astype(F32)
        term = jnp.dot(part, pick, preferred_element_type=F32)
        out = term if out is None else out + term
    return out


def tables_kernel(scale, modes_ref, eigen_ref, basis_ref, coef_ref, mask_ref, *refs):
    sb_ref, lh_ref, ll_ref, lx_ref, xy_ref, z_ref, extended_ref, divisor_ref, sums_ref, rows_ref = refs
    strides = (PTS * PTS, PTS, 1)
    straight, stiff, unit = [], [], []
    for d in range(3):
        mode = modes_ref[d]
        scaled = mode * eigen_ref[d : d + 1, :]
        one = lax.dot_general(
            scaled, mode, (((1,), (1,)), ((), ())), precision=HIGHEST, preferred_element_type=F32
        )
        straight.append(expand(mode, strides[d]))
        stiff.append(expand(one, strides[d]))
        unit.append(picker(strides[d]).astype(F32))
    for i in range(PTS):
        for j in range(PTS):
            rows = slice((i * PTS + j) * PTS, (i * PTS + j + 1) * PTS)
            pair = straight[0][i : i + 1] * straight[1][j : j + 1]
            sb_ref[rows, :] = (pair * straight[2]).astype(BF16)
    lane = lane_ids(8, LANES)
    for half in range(2):
        for j in range(PTS):
            rows = slice((half * PTS + j) * PTS, (half * PTS + j + 1) * PTS)
            full = stiff[1][j : j + 1, :LANES] * unit[2][:, :LANES]
            full = full + unit[1][j : j + 1, :LANES] * stiff[2][:, :LANES]
            full = jnp.where(lane // 64 == half, full, 0.0)
            head = full.astype(BF16)
            lh_ref[rows, :] = head
            ll_ref[rows, :] = (full - head.astype(F32)).astype(BF16)
    low_half = lane_ids(1, NODES) % LANES < 64
    for c in range(NODES // LANES):
        even, odd = stiff[0][2 * c : 2 * c + 1], stiff[0][2 * c + 1 : 2 * c + 2]
        lx_ref[c : c + 1, :] = jnp.where(low_half, even, odd)
        lx_ref[c + 4 : c + 5, :] = jnp.where(low_half, odd, even)
    point, row = lane_ids(PTS, PTS), row_ids(PTS, PTS)
    pairs = (row < 2 * EX, row // 2 * (PTS - 1) + point, row % 2)
    short = jnp.maximum(
        0.0,
        1.0 - jnp.abs(pairs[1].astype(F32) / float(EX * (PTS - 1)) - pairs[2].astype(F32)),
    )
    short = jnp.where(pairs[0], short, 0.0)
    stiff_x = jnp.dot(short, stiff[0], precision=HIGHEST, preferred_element_type=F32)
    stiff_y = jnp.dot(short, stiff[1], precision=HIGHEST, preferred_element_type=F32)
    for a in range(2):
        for b in range(2):
            for x in range(EX):
                for y in range(EY):
                    at = ((a * 2 + b) * EX + x) * EY + y
                    plain_x, plain_y = hat_x(x, a), hat_y(y, b)
                    xy_ref[at : at + 1, :] = plain_x * plain_y
                    xy_ref[XY + at : XY + at + 1, :] = (
                        stiff_x[x * 2 + a : x * 2 + a + 1] * plain_y
                        + plain_x * stiff_y[y * 2 + b : y * 2 + b + 1]
                    )
    place = row_ids(EZ, PTS) * (PTS - 1) + lane_ids(EZ, PTS)
    for level, weight in enumerate(hat_z()):
        z_ref[level * EZ : (level + 1) * EZ, :] = weight
        tall = hat(place, EZ * (PTS - 1), CGZ, level)
        z_ref[(CGZ + level) * EZ : (CGZ + level + 1) * EZ, :] = jnp.dot(
            tall, stiff[2], precision=HIGHEST, preferred_element_type=F32
        )
    spectrum = functools.reduce(
        jnp.add, [expand(eigen_ref[d : d + 1, :], strides[d]) for d in range(3)]
    )
    current = load_groups(basis_ref, KV - 1)
    inside = own_neighbors(current)
    coef = columns(coef_ref)
    for x in range(EX):
        for y in range(EY):
            extended_ref[x, y] = current[x][y] + inside[x][y]
            divisor_ref[x, y] = coef[x][y] * spectrum + SHIFT
    rows_ref[...] = jnp.zeros_like(rows_ref)
    for level in range(CGZ):
        sums = [[None] * EY for _ in range(EX)]
        for x in range(EX):
            for y in range(EY):
                sums[x][y] = fold(current[x][y] * z_ref[level * EZ : (level + 1) * EZ, :])
        for ab in range(4):
            total = jnp.zeros((1, NODES), F32)
            for x in range(EX):
                for y in range(EY):
                    at = (ab * EX + x) * EY + y
                    total = total + sums[x][y] * xy_ref[at : at + 1, :]
            parts = [total[:, c : c + LANES] for c in range(0, NODES, LANES)]
            at = AT_SUM + ab * CGZ + level
            rows_ref[at : at + 1, :] = functools.reduce(jnp.add, parts) * scale
    sums_ref[...] = lane_sums(rows_ref[...])


def smooth_kernel(*refs):
    own_ref, divisor_ref, mask_ref, sb_ref = refs[:4]
    halo = [ref[0:8, :] for ref in refs[4:8]]
    smooth_ref, *send = refs[8:]
    own, outside = load_groups(own_ref), unpack_all(halo)
    active = columns(mask_ref)
    extended = [[own[x][y] + outside[x][y] for y in range(EY)] for x in range(EX)]
    modal = jnp.dot(stack(extended).astype(BF16), sb_ref[...], preferred_element_type=F32)
    modal = unstack(modal)
    modal = [[modal[x][y] / divisor_ref[x, y] for y in range(EY)] for x in range(EX)]
    smooth = lax.dot_general(
        stack(modal).astype(BF16),
        sb_ref[...],
        (((1,), (1,)), ((), ())),
        preferred_element_type=F32,
    )
    smooth = unstack(smooth)
    smooth = [[smooth[x][y] * active[x][y] for y in range(EY)] for x in range(EX)]
    for x in range(EX):
        for y in range(EY):
            smooth_ref[x, y] = smooth[x][y]
    for ref, face in zip(send, pack_all(smooth)):
        ref[...] = face


def stiff_apply(groups, lh_ref, ll_ref, lx_ref):
    whole = stack(groups)
    chunks = [whole[:, c : c + LANES] for c in range(0, NODES, LANES)]
    tall = jnp.concatenate(chunks, axis=0)
    head = tall.astype(BF16)
    tail = (tall - head.astype(F32)).astype(BF16)
    rows, size = tall.shape[0], whole.shape[0]
    both = jnp.dot(jnp.concatenate([head, tail], axis=0), lh_ref[...], preferred_element_type=F32)
    inner = both[:rows] + (both[rows:] + jnp.dot(head, ll_ref[...], preferred_element_type=F32))
    turned = [pltpu.roll(chunk, 64, 1) for chunk in chunks]
    out = []
    for c in range(len(chunks)):
        lanes = slice(c * LANES, (c + 1) * LANES)
        total = inner[c * size : (c + 1) * size]
        for d in range(len(chunks)):
            total = total + chunks[d] * lx_ref[d : d + 1, lanes]
            total = total + turned[d] * lx_ref[d + 4 : d + 5, lanes]
        out.append(total)
    return unstack(jnp.concatenate(out, axis=1))


def image_kernel(count, *refs):
    basis_ref, smooth_ref, coef_ref, mask_ref, ids_ref, got_ref, lh_ref, ll_ref, lx_ref = refs[:9]
    face_refs, mask_refs = refs[9:13], refs[13:17]
    precond_ref, image_ref, row_ref = refs[17:]
    coef, active = columns(coef_ref), columns(mask_ref)
    solved = got_ref[...]
    lane = lane_ids(1, count)
    weight_z = hat_z()
    field = [[jnp.zeros((EZ, NODES), F32) for _ in range(EY)] for _ in range(EX)]
    for a in range(2):
        for b in range(2):
            along = jnp.zeros((EZ, NODES), F32)
            for level in range(CGZ):
                hit = jnp.where(lane == ids_ref[0, 0, a, b, level], solved, 0.0)
                along = along + weight_z[level] * jnp.sum(hit, axis=1, keepdims=True)
            for x in range(EX):
                for y in range(EY):
                    field[x][y] = field[x][y] + along * (hat_x(x, a) * hat_y(y, b))
    smooth = load_groups(smooth_ref)
    precond = [
        [smooth[x][y] + active[x][y] * field[x][y] for y in range(EY)] for x in range(EX)
    ]
    stiff = stiff_apply(precond, lh_ref, ll_ref, lx_ref)
    inside = own_neighbors(precond)
    outside = unpack_all([ref[...] for ref in face_refs])
    open_faces = unpack_all([ref[8:16, :] for ref in mask_refs])
    counts = face_count(EZ)
    dots = [jnp.zeros((EZ, NODES), F32) for _ in range(KV + 1)]
    for x in range(EX):
        for y in range(EY):
            across = outside[x][y] + open_faces[x][y] * field[x][y]
            image = active[x][y] * (
                coef[x][y] * stiff[x][y]
                + PENALTY * (counts * precond[x][y] - (inside[x][y] + across))
            )
            precond_ref[x, y] = precond[x][y]
            image_ref[x, y] = image
            for v in range(KV):
                dots[v] = dots[v] + basis_ref[v, x, y] * image
            dots[KV] = dots[KV] + image * image
    values = [all_sum(d) for d in dots]
    basis = [load_groups(basis_ref, v) for v in range(KV)]
    for v in range(KV):
        for u in range(v, KV):
            total = jnp.zeros((EZ, NODES), F32)
            for x in range(EX):
                for y in range(EY):
                    total = total + basis[v][x][y] * basis[u][x][y]
            values.append(all_sum(total))
    row = jnp.zeros((1, LANES), F32)
    row_lane = lane_ids(1, LANES)
    for position, value in enumerate(values):
        row = jnp.where(row_lane == position, value, row)
    row_ref[...] = row


def finish_kernel(total_points, basis_ref, image_ref, got_ref, next_ref, hessen_ref):
    sums = got_ref[...] / total_points
    lane = lane_ids(1, LANES)

    def pick(position):
        return jnp.sum(jnp.where(lane == position, sums, 0.0), axis=1, keepdims=True)

    proj = [pick(v) for v in range(KV)]
    square = pick(KV)
    position = KV + 1
    quad = jnp.zeros((1, 1), F32)
    for v in range(KV):
        for u in range(v, KV):
            factor = 1.0 if u == v else 2.0
            quad = quad + factor * proj[v] * proj[u] * pick(position)
            position += 1
    dot = functools.reduce(jnp.add, [p * p for p in proj])
    beta = jnp.sqrt(square - 2.0 * dot + quad + EPSILON)
    for x in range(EX):
        for y in range(EY):
            residual = image_ref[x, y]
            for v in range(KV):
                residual = residual - proj[v] * basis_ref[v, x, y]
            next_ref[x, y] = residual / beta
    for v, value in enumerate(proj + [beta]):
        hessen_ref[v] = jnp.sum(value)


def levels_of(half):
    found = []
    for level in range(CGZ):
        for point in range(half * HALF * (PTS - 1), (half * HALF + HALF - 1) * (PTS - 1) + PTS):
            if abs(point * (CGZ - 1) / (EZ * (PTS - 1)) - level) < 1.0 + 1e-3:
                found.append(level)
                break
    return found


def lane_sums(x):
    return lax.dot_general(
        jnp.ones((8, LANES), F32),
        x,
        (((1,), (1,)), ((), ())),
        precision=HIGHEST,
        preferred_element_type=F32,
    )


def fold(acc):
    return jnp.sum(acc, axis=0, keepdims=True)


def fold_eight(accs):
    row = row_ids(8, LANES)
    step = 4
    while step:
        keep = row // step % 2 == 0
        half = len(accs) // 2
        merged = []
        for first, second in zip(accs[:half], accs[half:]):
            here = jnp.where(keep, first, pltpu.roll(second, step, 0))
            there = jnp.where(keep, pltpu.roll(first, 8 - step, 0), second)
            merged.append(here + there)
        accs, step = merged, step // 2
    return accs[0]


class RowSums:
    def __init__(self, ref, tiles_ref):
        self.ref, self.tiles_ref, self.rows = ref, tiles_ref, set()

    def put(self, row, acc):
        self.tiles_ref[row] = acc
        self.rows.add(row)

    def finish(self):
        empty = jnp.zeros((8, LANES), F32)
        for base in sorted({row // 8 * 8 for row in self.rows}):
            tiles = [self.tiles_ref[r] if r in self.rows else empty for r in range(base, base + 8)]
            self.ref[base : base + 8, :] = fold_eight(tiles)


def pieces_of(half):
    for x in range(EX):
        for y in range(EY):
            for c in range(NODES // LANES):
                yield x, y, slice(half * HALF, half * HALF + HALF), slice(c * LANES, (c + 1) * LANES)


def products(left, right, halves, out_row):
    accs = {}
    for half in halves:
        lefts, rights = left(half), right(half)
        for piece in pieces_of(half):
            own = {v: load(*piece) for v, load in lefts.items()}
            other = own if rights is None else {w: load(*piece) for w, load in rights.items()}
            for v, first in own.items():
                for w, second in other.items():
                    if rights is None and w < v:
                        continue
                    term = first * second
                    accs[v, w] = accs[v, w] + term if (v, w) in accs else term
    for (v, w), acc in accs.items():
        out_row(v, w, acc)


def fields_kernel(basis_ref, coef_ref, mask_ref, *refs):
    mask_refs, (xy_ref, z_ref) = refs[:4], refs[4:6]
    smooth_ref, lh_ref, ll_ref, lx_ref, sums_ref = refs[6:11]
    early_ref, field_ref, wall_ref, part_ref, mixed_ref = refs[11:]
    coef, active = columns(coef_ref), columns(mask_ref)
    wide = [[jnp.broadcast_to(active[x][y], (EZ, NODES)) for y in range(EY)] for x in range(EX)]
    inside, outside = own_neighbors(wide), unpack_all([ref[8:16, :] for ref in mask_refs])
    counts = face_count(EZ)
    halves = range(EZ // HALF)
    levels = [levels_of(half) for half in halves]


    def mix(vector, x, y, half, value):
        first = ((x * EY + y) * len(halves) + half) * (NODES // LANES)
        for c in range(NODES // LANES):
            at = pl.ds((first + c) * HALF * APART + vector, HALF, stride=APART)
            mixed_ref[at, :] = value[:, c * LANES : (c + 1) * LANES]

    smooth = load_groups(smooth_ref)
    stiff_part = stiff_apply(smooth, lh_ref, ll_ref, lx_ref)
    inside_part = own_neighbors(smooth)
    for x in range(EX):
        for y in range(EY):
            wall = active[x][y] * PENALTY * (counts - (inside[x][y] + outside[x][y]))
            wall_ref[x, y] = wall
            part_ref[x, y] = active[x][y] * (
                coef[x][y] * stiff_part[x][y]
                + PENALTY * (counts * smooth[x][y] - inside_part[x][y])
            )
            weight = active[x][y] * coef[x][y]
            for half in halves:
                rows = slice(half * HALF, half * HALF + HALF)
                for ab in range(4):
                    at = (ab * EX + x) * EY + y
                    plain = xy_ref[at : at + 1, :]
                    first = weight[rows] * xy_ref[XY + at : XY + at + 1, :] + wall[rows] * plain
                    second = weight[rows] * plain
                    for level in levels[half]:
                        tall = slice(level * EZ + half * HALF, level * EZ + half * HALF + HALF)
                        stiff = slice((CGZ + level) * EZ + half * HALF, (CGZ + level) * EZ + half * HALF + HALF)
                        value = z_ref[tall, :] * first + z_ref[stiff, :] * second
                        field_ref[ab * CGZ + level, x, y, rows, :] = value
                        mix(KV + ab * CGZ + level, x, y, half, value)
                    for level in set(range(CGZ)) - set(levels[half]):
                        mix(KV + ab * CGZ + level, x, y, half, jnp.zeros((HALF, NODES), F32))
                for v in range(KV):
                    mix(v, x, y, half, basis_ref[v, x, y, rows, :])
    total = jnp.zeros((2 * MIXED, 2 * MIXED), F32)
    group = 8 * APART
    for start in range(0, mixed_ref.shape[0], group):
        whole = jnp.concatenate(
            [mixed_ref[start + k * APART : start + k * APART + MIXED, :] for k in range(8)], axis=1
        )
        head = whole.astype(BF16).astype(F32)
        both = jnp.concatenate([head, whole - head], axis=0).astype(BF16)
        total = total + lax.dot_general(
            both, both, (((1,), (1,)), ((), ())), preferred_element_type=F32
        )
    gram = (total[:MIXED, :MIXED] + total[MIXED:, MIXED:]) + (
        total[:MIXED, MIXED:] + total[MIXED:, :MIXED]
    )
    used = jnp.logical_and(row_ids(MIXED, MIXED) < KV + VERTS, lane_ids(MIXED, MIXED) < KV + VERTS)
    gram = jnp.where(used, gram, 0.0)
    lane = lane_ids(1, 2 * LANES)
    inner = lane % VERTS
    second = lane - LANES
    none = jnp.full((1, 2 * LANES), -1, jnp.int32)
    of_row = jnp.where(lane < LANES, KV + inner, jnp.where(second < KV * VERTS, second // VERTS, none))
    of_lane = jnp.where(lane < LANES, KV + (inner + lane // VERTS) % VERTS, KV + inner)
    distant = jnp.logical_and(second >= AT_FAR, second < AT_FAR + VERTS // 2)
    of_row = jnp.where(distant, KV + inner, of_row)
    of_lane = jnp.where(distant, KV + inner + VERTS // 2, of_lane)
    position = AT_GRAM
    for v in range(KV):
        for u in range(v, KV):
            of_row = jnp.where(second == position, v, of_row)
            of_lane = jnp.where(second == position, u, of_lane)
            position += 1
    pick = (row_ids(MIXED, 2 * LANES) == of_lane).astype(F32)
    moved = jnp.dot(gram, pick, precision=HIGHEST, preferred_element_type=F32)
    line = fold(jnp.where(row_ids(MIXED, 2 * LANES) == of_row, moved, 0.0))
    line = line + jnp.concatenate([jnp.zeros((1, LANES), F32), sums_ref[0:1, :]], axis=1)
    early_ref[...] = jnp.broadcast_to(line, (8, 2 * LANES))


def base_kernel(rows, peers, *refs):
    basis_ref, part_ref, mask_ref, ids_ref, inverse_ref = refs[:5]
    face_refs, early_ref, field_ref = refs[5:9], refs[9], refs[10]
    base_ref, send_ref, rows_ref, tiles_ref = refs[11:]
    active = columns(mask_ref)
    outside = unpack_all([ref[...] for ref in face_refs])
    for x in range(EX):
        for y in range(EY):
            base_ref[x, y] = part_ref[x, y] - (PENALTY * active[x][y]) * outside[x][y]
    rows_ref[...] = jnp.zeros_like(rows_ref)
    halves = range(EZ // HALF)

    def base(half):
        return {KV: (lambda x, y, r, c: base_ref[x, y, r, c])}

    def vectors(half):
        found = {v: (lambda x, y, r, c, v=v: basis_ref[v, x, y, r, c]) for v in range(KV)}
        found.update(base(half))
        return found

    def fields(part):
        def at(half):
            return {
                v: (lambda x, y, r, c, v=v: field_ref[v, x, y, r, c])
                for v in range(part * 8, part * 8 + 8)
                if v % CGZ in levels_of(half)
            }

        return at

    sums = RowSums(rows_ref, tiles_ref)
    put = sums.put

    products(base, vectors, halves, lambda v, w, s: put(AT_R + w, s))
    for part in range(VERTS // 8):
        products(base, fields(part), halves, lambda v, w, s: put(AT_G + w, s))
    sums.finish()
    late = lane_sums(rows_ref[...])
    early = early_ref[...]
    first = lax.axis_index("by") * rows
    tile = jnp.concatenate(
        [early[0:1, :LANES], early[0:1, LANES:] + late[0:1] + ids_ref[0:1, :]]
        + [inverse_ref[pl.ds(first + r, 1), :] for r in range(rows)],
        axis=0,
    )
    size = SENT + rows
    for peer in range(peers):
        send_ref[size * peer : size * peer + size, :] = tile


def close_kernel(total_points, rows, peers, *refs):
    basis_ref, smooth_ref, base_ref, wall_ref, coef_ref, mask_ref = refs[:6]
    xy_ref, z_ref, got_ref, precond_hbm, next_hbm, hessen_hbm = refs[6:12]
    precond_ref, next_ref, hessen_ref, sems = refs[12:]
    lane, row = lane_ids(peers, LANES), row_ids(peers, LANES)
    side = lax.axis_size("by")

    def got(r):
        return got_ref[pl.ds(r, peers, stride=SENT + rows), :]

    def along_x(values, step):
        return pltpu.roll(values, (step * side) % peers, 0)

    def along_y(values, step):
        edge = row % side == (0 if step > 0 else side - 1)
        wrapped = pltpu.roll(values, (step * (1 - side)) % peers, 0)
        return jnp.where(edge, wrapped, pltpu.roll(values, step % peers, 0))

    def turn(values, lanes):
        return pltpu.roll(values, (-lanes) % LANES, 1)

    sums = got(1)
    corner = sums + along_x(turn(sums, 2 * CGZ), 1)
    other = turn(sums, CGZ) + along_x(turn(sums, 3 * CGZ), 1)
    corner = corner + along_y(other, 1)
    number = lane.astype(F32)
    hits = [number == sums[:, AT_ID + v : AT_ID + v + 1] for v in range(CGZ)]
    coarse = jnp.zeros((peers, LANES), F32)
    for v in range(CGZ):
        coarse = coarse + jnp.where(hits[v], corner[:, AT_SUM + v : AT_SUM + v + 1], 0.0)
    coarse = fold(coarse)
    solved = jnp.zeros((peers, LANES), F32)
    for r in range(rows):
        part = jnp.where(lane == row * rows + r, coarse, 0.0)
        solved = solved + jnp.sum(part, axis=1, keepdims=True) * got(SENT + r)
    solved = fold(solved)
    near = jnp.zeros((peers, LANES), F32)
    for v in range(CGZ):
        value = jnp.sum(jnp.where(hits[v], solved, 0.0), axis=1, keepdims=True)
        near = jnp.where(lane % CGZ == v, value, near)
    right = along_x(near, -1)
    quarter = lane % VERTS // CGZ
    lower = jnp.where(quarter < 2, near, right)
    spread = jnp.where(quarter % 2 == 0, lower, along_y(lower, -1))
    me = lax.axis_index("bx") * side + lax.axis_index("by")
    own = fold(jnp.where(row == me, spread, 0.0))
    coef, active = columns(coef_ref), columns(mask_ref)
    along, bent = [], []
    for ab in range(4):
        plain = jnp.zeros((EZ, NODES), F32)
        stiff = jnp.zeros((EZ, NODES), F32)
        for level in range(CGZ):
            value = own[:, ab * CGZ + level : ab * CGZ + level + 1]
            plain = plain + value * z_ref[level * EZ : (level + 1) * EZ, :]
            stiff = stiff + value * z_ref[(CGZ + level) * EZ : (CGZ + level + 1) * EZ, :]
        along.append(plain)
        bent.append(stiff)
    copies, fields = [], []
    for x in range(EX):
        for y in range(EY):
            field = jnp.zeros((EZ, NODES), F32)
            for ab in range(4):
                at = (ab * EX + x) * EY + y
                field = field + along[ab] * xy_ref[at : at + 1, :]
            precond_ref[x, y] = smooth_ref[x, y] + active[x][y] * field
            n = len(copies)
            copies.append(
                pltpu.make_async_copy(precond_ref.at[x, y], precond_hbm.at[x, y], sems.at[n])
            )
            copies[-1].start()
            fields.append(field)
    group = lane // VERTS
    shifted = spread
    for far in range(1, VERTS // 2):
        shifted = jnp.where(group == far, turn(spread, far), shifted)
    weight = jnp.where(group == 0, 1.0, 2.0)
    square = got(0) * spread * shifted * weight
    scaled = sums * spread
    square = square + jnp.where(group == AT_G // VERTS, 2.0 * scaled, 0.0)
    distant = jnp.logical_and(lane >= AT_FAR, lane < AT_FAR + VERTS // 2)
    square = square + jnp.where(distant, 2.0 * scaled * turn(spread, VERTS // 2), 0.0)
    square = square + jnp.where(lane == AT_R + KV, sums, 0.0)
    square = jnp.sum(fold(square), axis=1, keepdims=True) / total_points
    linear, plain = fold(scaled), fold(sums)
    line = lane_ids(1, LANES)
    proj = []
    for v in range(KV):
        term = jnp.where(line // VERTS == v, linear, 0.0) + jnp.where(line == AT_R + v, plain, 0.0)
        proj.append(jnp.sum(term, axis=1, keepdims=True) / total_points)
    pair = jnp.zeros((1, LANES), F32)
    position = AT_GRAM
    for v in range(KV):
        for u in range(v, KV):
            factor = 1.0 if u == v else 2.0
            pair = jnp.where(line == position, factor * proj[v] * proj[u], pair)
            position += 1
    gram = jnp.sum(pair * plain, axis=1, keepdims=True) / total_points
    dot = functools.reduce(jnp.add, [p * p for p in proj])
    beta = jnp.sqrt(square - 2.0 * dot + gram + EPSILON)
    result = jnp.zeros((1, LANES), F32)
    for v, value in enumerate(proj + [beta]):
        result = jnp.where(line == v, value, result)
    hessen_ref[...] = result[:, : KV + 1]
    copies.append(pltpu.make_async_copy(hessen_ref, hessen_hbm, sems.at[2 * EX * EY]))
    copies[-1].start()
    inverse = 1.0 / beta
    for x in range(EX):
        for y in range(EY):
            image = jnp.zeros((EZ, NODES), F32)
            for ab in range(4):
                at = (ab * EX + x) * EY + y
                image = image + (
                    along[ab] * xy_ref[XY + at : XY + at + 1, :] + bent[ab] * xy_ref[at : at + 1, :]
                )
            residual = base_ref[x, y] + (active[x][y] * coef[x][y]) * image
            residual = residual + wall_ref[x, y] * fields[x * EY + y]
            for v in range(KV):
                residual = residual - proj[v] * basis_ref[v, x, y]
            next_ref[x, y] = residual * inverse
            n = EX * EY + x * EY + y
            copies.append(pltpu.make_async_copy(next_ref.at[x, y], next_hbm.at[x, y], sems.at[n]))
            copies[-1].start()
    for copy in copies:
        copy.wait()


def spec(kind=pltpu.VMEM):
    return pl.BlockSpec(memory_space=kind)


def call(kernel, outs, in_specs, args, out_specs=None, scratch=(), cost=1000000):
    return pl.pallas_call(
        kernel,
        out_shape=[jax.ShapeDtypeStruct(shape, dtype) for shape, dtype in outs],
        in_specs=in_specs,
        out_specs=out_specs or [spec() for _ in outs],
        scratch_shapes=scratch,
        compiler_params=pltpu.CompilerParams(vmem_limit_bytes=VMEM_BYTES),
        cost_estimate=pl.CostEstimate(flops=cost, bytes_accessed=cost, transcendentals=0),
    )(*args)


def exchange(sends):
    out = [None] * 4
    for place in range(4):
        axis = "bx" if place < 2 else "by"
        size = lax.axis_size(axis)
        assert size % 2 == 0
        pairs = [(i, (i + 1) % size) for i in range(place % 2, size, 2)]
        pairs = pairs + [(j, i) for i, j in pairs]
        out[place] = lax.ppermute(sends[place], axis, pairs)
    return out


def smooth_part(basis, coef, modes, eigen, mask, sends):
    halo = exchange(sends)
    tables = call(
        functools.partial(tables_kernel, 1.0 / math.sqrt(EX * EY * EZ * NODES)),
        [((NODES, NODES), BF16)]
        + [((LANES, LANES), BF16)] * 2
        + [((8, NODES), F32), ((2 * XY, NODES), F32), ((2 * CGZ * EZ, NODES), F32)]
        + [FIELD, FIELD, ((8, LANES), F32)],
        [spec()] * 5,
        (modes, eigen, basis, coef, mask),
        scratch=[pltpu.VMEM((LANES, LANES), F32)],
    )
    smooth, *sends = call(
        smooth_kernel,
        [FIELD] + [((8, 256), F32)] * 4,
        [spec()] * 8,
        (tables[6], tables[7], mask, tables[0], *halo),
    )
    return halo, tables, smooth, exchange(sends)


FIELD = ((EX, EY, EZ, NODES), F32)
SENDS = [((16, 256), F32)] * 4


def one_exchange(basis, coef, modes, eigen, mask, vertex_ids, coarse_inverse):
    peers = lax.axis_size("bx") * lax.axis_size("by")
    rows = coarse_inverse.shape[1] // peers
    points = EX * EY * EZ * NODES
    *local, a, b, c, d = call(
        load_kernel,
        [(x.shape, x.dtype) for x in (basis, mask, coef, modes, eigen, coarse_inverse)]
        + [((8, LANES), F32)]
        + SENDS,
        [spec(pltpu.HBM)] * 7,
        tuple(pltpu.with_memory_space_constraint(x, pltpu.HBM) for x in (basis, mask, coef, modes, eigen, vertex_ids, coarse_inverse)),
        scratch=[pltpu.VMEM(vertex_ids.shape, vertex_ids.dtype), pltpu.SemaphoreType.DMA((8,))],
    )
    basis, mask, coef, modes, eigen, coarse_inverse, ids = local
    halo, tables, smooth, faces = smooth_part(basis, coef, modes, eigen, mask, (a, b, c, d))
    early, fields, wall, part = call(
        fields_kernel,
        [((8, 2 * LANES), F32), ((VERTS,) + FIELD[0], F32), FIELD, FIELD],
        [spec()] * 14,
        (basis, coef, mask, *halo, tables[4], tables[5], smooth, *tables[1:4], tables[8]),
        scratch=[pltpu.VMEM((EX * EY * EZ * NODES // LANES * APART, LANES), F32)],
    )
    base, row = call(
        functools.partial(base_kernel, rows, peers),
        [FIELD, (((SENT + rows) * peers, LANES), F32)],
        [spec()] * 11,
        (basis, part, mask, ids, coarse_inverse, *faces, early, fields),
        scratch=[pltpu.VMEM((LANES, LANES), F32), pltpu.VMEM((LANES, 8, LANES), F32)],
    )
    row = row.reshape(peers, SENT + rows, 1, LANES)
    got = lax.all_to_all(row, ("bx", "by"), 0, 0).reshape((SENT + rows) * peers, LANES)
    precond, next_vector, hessen = call(
        functools.partial(close_kernel, float(points * peers), rows, peers),
        [FIELD, FIELD, ((1, KV + 1), F32)],
        [spec()] * 9,
        (basis, smooth, base, wall, coef, mask, tables[4], tables[5], got),
        out_specs=[spec(pltpu.HBM)] * 3,
        scratch=[pltpu.VMEM(*FIELD)] * 2
        + [pltpu.VMEM((1, KV + 1), F32), pltpu.SemaphoreType.DMA((2 * EX * EY + 1,))],
    )
    return precond, next_vector, hessen.reshape(KV + 1)


def two_exchanges(basis, coef, modes, eigen, mask, vertex_ids, coarse_inverse):
    peers = lax.axis_size("bx") * lax.axis_size("by")
    count = coarse_inverse.shape[1]
    points = EX * EY * EZ * NODES
    row, *sends = call(
        functools.partial(start_kernel, 1.0 / math.sqrt(points), count),
        [((1, count), F32)] + SENDS,
        [spec()] * 2 + [spec(pltpu.SMEM)],
        (basis, mask, vertex_ids),
    )
    coarse = lax.psum(row, ("bx", "by"))
    solved = jnp.dot(coarse_inverse, coarse[0], precision=HIGHEST)
    solved = lax.all_gather(solved, "bx", axis=0, tiled=True)[None]
    halo, tables, smooth, faces = smooth_part(basis, coef, modes, eigen, mask, sends)
    precond, image, row = call(
        functools.partial(image_kernel, count),
        [FIELD, FIELD, ((1, LANES), F32)],
        [spec()] * 4 + [spec(pltpu.SMEM)] + [spec()] * 12,
        (basis, smooth, coef, mask, vertex_ids, solved, *tables[1:4], *faces, *halo),
    )
    row = lax.psum(row, ("bx", "by"))
    next_vector, hessen = call(
        functools.partial(finish_kernel, float(points * peers)),
        [FIELD, ((KV + 1,), F32)],
        [spec()] * 3,
        (basis, image, row),
        out_specs=[spec(), spec(pltpu.SMEM)],
    )
    return precond, next_vector, hessen


def body(basis, coef, modes, eigen, mask, vertex_ids, coarse_inverse):
    assert coef.shape == (EX, EY, EZ) and basis.shape[0] == KV
    peers = lax.axis_size("bx") * lax.axis_size("by")
    count = coarse_inverse.shape[1]
    small = count == LANES and count == 4 * peers
    steps = one_exchange if small else two_exchanges
    return tuple(steps(basis, coef, modes, eigen, mask, vertex_ids, coarse_inverse))


def solution(mesh):
    placed = (
        P(None, "bx", "by", None, None),
        P("bx", "by", None),
        P(),
        P(),
        P("bx", "by", None),
        P("bx", "by", None, None, None),
        P("bx", None),
    )
    return jax.shard_map(
        body,
        mesh=mesh,
        in_specs=placed,
        out_specs=(P("bx", "by", None, None), P("bx", "by", None, None), P()),
        check_vma=False,
    )
```
